32 devices in a mesh: dp: 4 (over y, x), mp: 8 (over z, core).
Axes of the slice: x: 2, y: 2, z: 4, core: 2. Of those that a mesh axis runs over, the one named last changes fastest.
Arguments:
- tokens: bfloat16 [4096, 1024], P('dp'), may hold values from -6 to 6
- states: bfloat16 [8, 128, 1024], P('dp'), may hold values from -6 to 6
- cotangent: bfloat16 [4096, 1024], P('dp'), may hold values from -6 to 6
- self_weight: bfloat16 [3, 1024, 1024], P(None, None, 'mp'), may hold values from -0.1875 to 0.1875
- self_output: bfloat16 [1024, 1024], P('mp'), may hold values from -1 to 1
- cross_query: bfloat16 [1024, 1024], P(None, 'mp'), may hold values from -0.1875 to 0.1875
- cross_pair: bfloat16 [2, 1024, 1024], P(None, None, 'mp'), may hold values from -0.1875 to 0.1875
- cross_output: bfloat16 [1024, 1024], P('mp'), may hold values from -0.5 to 0.5
- hidden_weight: bfloat16 [1024, 4096], P(None, 'mp'), may hold values from -0.1875 to 0.1875
- hidden_bias: bfloat16 [4096], P('mp'), may hold values from -3 to 3
- output_weight: bfloat16 [4096, 1024], P('mp'), may hold values from -0.09375 to 0.09375
- output_bias: bfloat16 [1024], replicated, may hold values from -3 to 3
- norm_gain: bfloat16 [3, 1024], replicated, may hold values from 0.5 to 1.5
- norm_shift: bfloat16 [3, 1024], replicated, may hold values from -2 to 2
- state_row: int32 [4], P('dp'), may hold values from 0 to 1
- state_segment: int32 [8, 128], P('dp'), may hold values from 0 to 3, never falling along the last dimension, each value on 1 to 64 neighbouring positions
- caption: int32 [4], P('dp'), may hold values from 0 to 3
Outputs:
- block_output: bfloat16 [4096, 1024], P(('dp', 'mp'))
- grad_tokens: float32 [4096, 1024], P(('dp', 'mp'))
- grad_states: float32 [8, 128, 1024], P('dp')
- grad_self_weight: float32 [3, 1024, 1024], P(None, None, 'mp')
- grad_self_output: float32 [1024, 1024], P('mp')
- grad_cross_query: float32 [1024, 1024], P(None, 'mp')
- grad_cross_pair: float32 [2, 1024, 1024], P(None, None, 'mp')
- grad_cross_output: float32 [1024, 1024], P('mp')
- grad_hidden_weight: float32 [1024, 4096], P(None, 'mp')
- grad_hidden_bias: float32 [4096], P('mp')
- grad_output_weight: float32 [4096, 1024], P('mp')
- grad_output_bias: float32 [1024], replicated
- grad_norm_gain: float32 [3, 1024], replicated
- grad_norm_shift: float32 [3, 1024], replicated
The draws below stay inside these ranges and needn't reach their ends.
Inputs may be any that keep to these rules, and one draw needn't show every extreme that they name: `state_segment`: in each encoder row the caption numbers never fall, and every caption 0 to 3 holds 1 to 64 states.
All inputs are finite; a program needn't handle non-finite values.
Results may differ from the reference program's by a relative error of at most 0.025.
Values may be sent and summed in bfloat16 or wider, within the bound.
No kernel may reach another device: no remote copies, remote signals or barrier semaphores. Data moves between devices by JAX's collectives and lax.ppermute only.
A program may use at most 128 MiB of HBM per device.

```python
import math
import jax
import jax.numpy as jnp
import numpy as np
from jax import lax

D = 1024
HEADS = 16
HDIM = 64
FF = 4096
IMG_LEN = 1024
ENC_LEN = 128
ENC_DEV = 2
SEGS = 4
IMG_DEV = 1
IMAGES = 4
TOKENS = 4096
ENC_ROWS = 8


def touch_ends(entries, rng, least, top_value):
    extent = entries.shape
    spot = [jax.random.randint(jax.random.fold_in(rng, axis), (), 0, extent[axis]) for axis in range(len(extent))]
    entries = entries.at[tuple(spot)].set(least)
    longest = extent.index(max(extent))
    spot[longest] = (spot[longest] + 1) % extent[longest]
    return entries.at[tuple(spot)].set(top_value)


def block_scale(rng, dims, pieces, low, largest):
    def one(position, blocks):
        draws = jax.random.uniform(jax.random.fold_in(jax.random.fold_in(rng, 6), position), (blocks,), jnp.float32, low / len(pieces), largest / len(pieces))
        return jnp.repeat(jnp.exp(draws), dims[position] // blocks).reshape((-1,) + (1,) * (len(dims) - position - 1))

    loudness = one(*pieces[0])
    for cut in pieces[1:]:
        loudness = loudness * one(*cut)
    return loudness


def split_up(number_of, total, most, slope):
    portions = [(1 << 20) // math.isqrt(standing ** slope) + 1 for standing in range(2, number_of + 1)]
    spare, given = total - most - (number_of - 1), [1] * (number_of - 1)
    while spare > 0:
        candidates = [i for i in range(number_of - 1) if given[i] < most]
        pool, remaining = sum([portions[i] for i in candidates]), spare
        for i in candidates:
            more = min(most - given[i], max(1, remaining * portions[i] // pool), spare)
            given[i] = given[i] + more
            spare = spare - more
    return np.array([most] + given)


def ragged_sizes(key, count, total, bound, lean):
    if count == 2:
        one = jax.random.randint(key, (), max(1, total - bound), min(bound, total - 1) + 1)
        return jnp.stack([one, total - one])
    lengths = jnp.asarray(split_up(count, total, bound, lean), jnp.int32)
    couples = (count - 1) // 2
    giver, taker = lengths[1:1 + 2 * couples:2], lengths[2:2 + 2 * couples:2]
    margin = jnp.minimum(giver - 1, bound - taker)
    moved = jax.random.randint(jax.random.fold_in(key, 1), (couples,), 0, 1 << 20) % (margin + 1)
    lengths = lengths.at[1:1 + 2 * couples:2].set(giver - moved).at[2:2 + 2 * couples:2].set(taker + moved)
    return lengths[jax.random.permutation(jax.random.fold_in(key, 2), count)]


def bell_draw(rng, dims, scale, reach, split=(), held_as=jnp.bfloat16):
    drawn = jax.random.normal(rng, dims, jnp.float32) * scale
    if len(split) > 0:
        drawn = block_scale(rng, dims, split, -0.22, 0.18) * drawn
    return jnp.clip(drawn, min=-reach, max=reach).astype(held_as)


def setup_inputs(seed: int = 0) -> dict:
    arg_keys = jax.random.split(jax.random.key(seed), 18)
    return {
        "tokens": bell_draw(arg_keys[0], (TOKENS, D), 1.0, 6.0, ((0, 4),)),
        "states": bell_draw(arg_keys[1], (ENC_ROWS, ENC_LEN, D), 1.0, 6.0, ((0, 4),)),
        "cotangent": bell_draw(arg_keys[2], (TOKENS, D), 1.0, 6.0, ((0, 4),)),
        "self_weight": bell_draw(arg_keys[3], (3, D, D), D ** -0.5, 0.1875, ((2, 8),)),
        "self_output": bell_draw(arg_keys[4], (D, D), (D // 32) ** -0.5, 1.0, ((0, 8),)),
        "cross_query": bell_draw(arg_keys[5], (D, D), D ** -0.5, 0.1875, ((1, 8),)),
        "cross_pair": bell_draw(arg_keys[6], (2, D, D), D ** -0.5, 0.1875, ((2, 8),)),
        "cross_output": bell_draw(arg_keys[7], (D, D), (D // 8) ** -0.5, 0.5, ((0, 8),)),
        "hidden_weight": bell_draw(arg_keys[8], (D, FF), D ** -0.5, 0.1875, ((1, 8),)),
        "hidden_bias": bell_draw(arg_keys[9], (FF,), 0.5, 3.0, ((0, 8),)),
        "output_weight": bell_draw(arg_keys[10], (FF, D), FF ** -0.5, 0.09375, ((0, 8),)),
        "output_bias": bell_draw(arg_keys[11], (D,), 0.5, 3.0),
        "norm_gain": jnp.clip(1.0 + 0.1 * jax.random.normal(arg_keys[12], (3, D), jnp.float32), 0.5, 1.5).astype(jnp.bfloat16),
        "norm_shift": bell_draw(arg_keys[13], (3, D), 0.3, 2.0),
        "state_row": touch_ends(jax.random.randint(arg_keys[14], (IMAGES,), 0, ENC_DEV), jax.random.fold_in(arg_keys[14], 1), 0, ENC_DEV - 1).astype(jnp.int32),
        "state_segment": jax.vmap(lambda own: jnp.searchsorted(jnp.cumsum(ragged_sizes(own, SEGS, ENC_LEN, ENC_LEN // 2, 0)), jnp.arange(ENC_LEN), side="right"))(jax.random.split(arg_keys[15], ENC_ROWS)).reshape((ENC_ROWS, ENC_LEN)).astype(jnp.int32),
        "caption": touch_ends(jax.random.randint(arg_keys[16], (IMAGES,), 0, SEGS), jax.random.fold_in(arg_keys[16], 1), 0, SEGS - 1).astype(jnp.int32),
    }


@jax.custom_vjp
def low(v):
    return lax.optimization_barrier(v.astype(jnp.bfloat16)).astype(jnp.float32)

@jax.custom_vjp
def low_back(v):
    return v

def low_keep(v):
    return (low(v), None)

def low_pass(kept, grad):
    return (grad,)

def back_keep(v):
    return (v, None)

def back_low(kept, grad):
    return (low(grad),)
low.defvjp(low_keep, low_pass)
low_back.defvjp(back_keep, back_low)
EPSILON = 1e-05
NEG_FILL = -1e+30
PRECISE = lax.Precision.HIGHEST

def layer_norm(resid, gain, shift):
    center = resid - lax.optimization_barrier(jnp.mean(resid, -1, keepdims=True))
    return center * lax.rsqrt(lax.optimization_barrier(jnp.mean(center * center, -1, keepdims=True)) + EPSILON) * gain + shift

def attention(query, keys, values, allowed):
    scores = low_back(jnp.einsum('qhd,khd->hqk', query, keys, precision=PRECISE)) * HDIM ** (-0.5)
    scores = jnp.where(allowed[None], scores, NEG_FILL)
    probs = low(jax.nn.softmax(scores, axis=-1))
    return jnp.einsum('hqk,khd->qhd', probs, values, precision=PRECISE)

def reference(tokens, states, cotangent, self_weight, self_output, cross_query, cross_pair, cross_output, hidden_weight, hidden_bias, output_weight, output_bias, norm_gain, norm_shift, state_row, state_segment, caption):
    rows_of_image = (lax.iota(jnp.int32, IMAGES) // IMG_DEV * ENC_DEV + state_row).astype(jnp.int32)
    labels = state_segment[rows_of_image]
    visible = labels == caption[:, None]
    causal = lax.iota(jnp.int32, IMG_LEN)[:, None] >= lax.iota(jnp.int32, IMG_LEN)[None, :]

    def self_image(trio):
        return attention(trio[0], trio[1], trio[2], causal)

    def cross_image(quad):
        seen = jnp.broadcast_to(quad[3][None, :], (IMG_LEN, ENC_LEN))
        return attention(quad[0], quad[1], quad[2], seen)

    def forward(resid_in, state_in, triple_weight, attn_weight, query_weight, pair_weight, cross_weight, hidden_matrix, hidden_shift, output_matrix, output_shift, gain_rows, shift_rows):
        normed_one = low(layer_norm(resid_in, gain_rows[0], shift_rows[0]))
        triple = low(low_back(jnp.einsum('td,cde->cte', normed_one, triple_weight, precision=PRECISE)))
        triple = triple.reshape(3, IMAGES, IMG_LEN, HEADS, HDIM)
        attended = lax.map(jax.checkpoint(self_image), (triple[0], triple[1], triple[2]))
        attended = low(low_back(attended.reshape(TOKENS, D)))
        first = resid_in + low_back(jnp.dot(attended, attn_weight, precision=PRECISE))
        normed_two = low(layer_norm(first, gain_rows[1], shift_rows[1]))
        queries = low(low_back(jnp.dot(normed_two, query_weight, precision=PRECISE)))
        queries = queries.reshape(IMAGES, IMG_LEN, HEADS, HDIM)
        pair = low(low_back(jnp.einsum('rsd,cde->crse', state_in, pair_weight, precision=PRECISE)))
        chosen = pair[:, rows_of_image].reshape(2, IMAGES, ENC_LEN, HEADS, HDIM)
        crossed = lax.map(jax.checkpoint(cross_image), (queries, chosen[0], chosen[1], visible))
        crossed = low(low_back(crossed.reshape(TOKENS, D)))
        second = first + low_back(jnp.dot(crossed, cross_weight, precision=PRECISE))
        normed_three = low(layer_norm(second, gain_rows[2], shift_rows[2]))
        hidden_in = low_back(jnp.dot(normed_three, hidden_matrix, precision=PRECISE) + hidden_shift)
        active = low(jax.nn.gelu(hidden_in))
        return second + low_back(jnp.dot(active, output_matrix, precision=PRECISE)) + output_shift
    floats = tuple((item.astype(jnp.float32) for item in (tokens, states, self_weight, self_output, cross_query, cross_pair, cross_output, hidden_weight, hidden_bias, output_weight, output_bias, norm_gain, norm_shift)))
    result, pullback = jax.vjp(forward, *floats)
    grads = pullback(cotangent.astype(jnp.float32))
    return (result.astype(jnp.bfloat16), grads[0], grads[1], grads[2], grads[3], grads[4], grads[5], grads[6], grads[7], grads[8], grads[9], grads[10], grads[11], grads[12])
```

```python
import functools
import math

import jax
import jax.numpy as jnp
from jax import lax
from jax.experimental import pallas as pl
from jax.experimental.pallas import tpu as pltpu
from jax.sharding import PartitionSpec as P

HDIM = 64
SEEN = 64
QB = 256
EPSILON = 1e-05
NEG_FILL = -1e30
SCALE = HDIM ** (-0.5)
F32 = jnp.float32
BF16 = jnp.bfloat16


def dot_nn(a, b):
    return lax.dot_general(a, b, (((1,), (0,)), ((), ())), preferred_element_type=F32)


def dot_nt(a, b):
    return lax.dot_general(a, b, (((1,), (1,)), ((), ())), preferred_element_type=F32)


def dot_tn(a, b):
    return lax.dot_general(a, b, (((0,), (0,)), ((), ())), preferred_element_type=F32)


def normalize(resid):
    center = resid - jnp.mean(resid, -1, keepdims=True)
    inverse = lax.rsqrt(jnp.mean(center * center, -1, keepdims=True) + EPSILON)
    return (center * inverse, inverse)


def norm_backward(standard, inverse, grad_normed, gain):
    scaled = grad_normed * gain
    return inverse * (
        scaled
        - jnp.mean(scaled, -1, keepdims=True)
        - standard * jnp.mean(scaled * standard, -1, keepdims=True)
    )


def at(index, size):
    return pl.ds(pl.multiple_of(index * size, size), size)


def staged(kernel, ins, outs, extra, *refs):
    count_in, count_out = len(ins), len(outs)
    idx, refs = refs[0], list(refs[1:])
    inner = refs[: count_in + count_out]
    own = refs[count_in + count_out : count_in + count_out + extra]
    rest = refs[count_in + count_out + extra :]
    sem_in, sem_out = rest[-2:]
    held = iter(rest[:-2])
    started, results = [], []
    for i, here in enumerate(ins):
        if here:
            local = next(held)
            started.append(pltpu.make_async_copy(inner[i], local, sem_in.at[len(started)]))
            inner[i] = local
    for i, here in enumerate(outs):
        if here:
            local = next(held)
            target = inner[count_in + i]
            results.append(pltpu.make_async_copy(local, target, sem_out.at[len(results)]))
            inner[count_in + i] = local
    for copy in started:
        copy.start()
    for copy in started:
        copy.wait()
    kernel(idx, *inner, *own)
    for copy in results:
        copy.start()
    for copy in results:
        copy.wait()


def call(
    kernel, outs, idx, *args, scratch=(), after=(), stage=False, tight=False, raw=(), cost=1, name=None, spill=8
):
    if after:
        idx = lax.optimization_barrier((idx, *after))[0]
    out_shape = [jax.ShapeDtypeStruct(s, t) for s, t in outs]
    big = lambda a: bool(stage) and a.size >= 1 << 15
    ins_far = [big(a) and i not in raw for i, a in enumerate(args)]
    outs_far = [big(a) for a in out_shape]
    vmem = pl.BlockSpec(memory_space=pltpu.VMEM)
    hbm = pl.BlockSpec(memory_space=pltpu.HBM)
    held = spill << 20
    for i, a in enumerate((*args, *out_shape)):
        if i not in raw:
            held += a.size * a.dtype.itemsize
    for a in scratch:
        if len(getattr(a, "shape", ())) > 1 and a.dtype in (F32, BF16):
            held += math.prod(a.shape) * jnp.dtype(a.dtype).itemsize
    scratch = list(scratch)
    if any(ins_far) or any(outs_far):
        kernel = functools.partial(staged, kernel, ins_far, outs_far, len(scratch))
        for a, far in zip((*args, *out_shape), ins_far + outs_far):
            if far:
                scratch.append(pltpu.VMEM(a.shape, a.dtype))
        scratch.append(pltpu.SemaphoreType.DMA((max(1, sum(ins_far)),)))
        scratch.append(pltpu.SemaphoreType.DMA((max(1, sum(outs_far)),)))
    return pl.pallas_call(
        kernel,
        out_shape=out_shape,
        in_specs=[pl.BlockSpec(memory_space=pltpu.SMEM)]
        + [hbm if far or i in raw else vmem for i, far in enumerate(ins_far)],
        out_specs=[hbm if far else vmem for far in outs_far],
        scratch_shapes=scratch,
        cost_estimate=pl.CostEstimate(flops=cost, bytes_accessed=1, transcendentals=0),
        compiler_params=pltpu.CompilerParams(
            vmem_limit_bytes=min(held, 60 << 20) if tight else 60 << 20
        ),
        name=name,
    )(idx, *args)


def head_select(parts, axis):
    if len(parts) == 1:
        return parts[0]
    head = lax.broadcasted_iota(jnp.int32, parts[0].shape, axis) // HDIM
    return jnp.where(head == 0, parts[0], parts[1])


def head_only(value, h, count):
    if count == 1:
        return value
    head = lax.broadcasted_iota(jnp.int32, value.shape, 1) // HDIM
    return jnp.where(head == h, value, jnp.zeros_like(value))


def self_kernel(
    chips, idx, tok, weight, gain, shift, states, pair, segment, normed, triple, probs, *rest
):
    att_out = rest[:chips]
    val_t, att, kv = rest[chips:]
    rows, width = tok.shape[0], weight.shape[2]
    heads = width // HDIM
    g = gain[0:1, :].astype(F32)
    s = shift[0:1, :].astype(F32)
    for i in range(rows // QB):
        here = slice(i * QB, (i + 1) * QB)
        standard, _ = normalize(tok[here, :].astype(F32))
        n = (standard * g + s).astype(BF16)
        normed[here, :] = n
        query = dot_nn(n, weight[0]).astype(BF16)
        triple[0, here, :] = query
        triple[1, here, :] = dot_nn(n, weight[1]).astype(BF16)
        value = dot_nn(n, weight[2])
        triple[2, here, :] = value.astype(BF16)
        val_t[:, here] = value.T.astype(BF16)
        seen = (i + 1) * QB
        outs = []
        for h in range(heads):
            scores = dot_nt(triple[1, 0:seen, :], head_only(query, h, heads)) * SCALE
            key_at = lax.broadcasted_iota(jnp.int32, scores.shape, 0)
            row_at = lax.broadcasted_iota(jnp.int32, scores.shape, 1) + i * QB
            scores = jnp.where(key_at <= row_at, scores, NEG_FILL)
            e = jnp.exp(scores - jnp.max(scores, 0, keepdims=True))
            p = (e * (1.0 / jnp.sum(e, 0, keepdims=True))).astype(BF16)
            probs[h, 0:seen, here] = p
            outs.append(dot_nn(val_t[:, 0:seen], p))
        att[here, :] = head_select(outs, 0).T.astype(BF16)
    own = (att_out[0].shape[0] - 2 * SEEN) // 2
    before = segment[pl.ds(idx[2], 1), :] < idx[3]
    begin = jnp.minimum(jnp.sum(before.astype(jnp.int32)), states.shape[1] - SEEN)
    for c in range(2):
        kv[...] = dot_nn(states[idx[2]], pair[c])
        for k in range(chips):
            where = slice(2 * own + c * SEEN, 2 * own + (c + 1) * SEEN)
            att_out[k][where, :] = kv[pl.ds(begin, SEEN), :].astype(BF16)
    for k in range(chips):
        for cc in range(2):
            att_out[k][cc * own : (cc + 1) * own, :] = att[at(idx[0] ^ (2 * k + cc), own), :]


def pair_tiles(block, heads):
    return jnp.concatenate([head_only(block, h, heads) for h in range(heads)], 0)


def half_reduce(op, value, heads, fill):
    if heads == 1:
        return op(value, -1, keepdims=True)
    half = lax.broadcasted_iota(jnp.int32, value.shape, 1) // SEEN
    first = op(jnp.where(half == 0, value, fill), -1, keepdims=True)
    other = op(jnp.where(half == 1, value, fill), -1, keepdims=True)
    return jnp.where(half == 0, first, other)


def fetch_weights(chips, dps, idx, weights, wf, sem):
    width = wf.shape[1] // (2 * chips)
    cut = wf.shape[2] // dps
    span = (chips - 1) * width
    half = chips * width
    lists = []
    for m in range(3):
        copies = []
        for cc in range(2):
            source = weights[cc * (dps + 1)]
            where = wf.at[m, cc * half : cc * half + width, :]
            copies.append((source.at[m * width : (m + 1) * width, :], where))
            for q in range(dps):
                source = weights[cc * (dps + 1) + 1 + q]
                cols = at(idx[1] ^ q, cut)
                where = wf.at[m, cc * half + width : (cc + 1) * half, cols]
                copies.append((source.at[m * span : (m + 1) * span, :], where))
        lists.append(
            [pltpu.make_async_copy(s, d, sem.at[m, i]) for i, (s, d) in enumerate(copies)]
        )
    return lists


def own_rows(idx, source, rows, sem):
    copy = pltpu.make_async_copy(source.at[at(idx[0], rows.shape[0]), :], rows, sem)
    copy.start()
    return copy


def cross_kernel(chips, dps, idx, tokens, gain, shift, seen, *rest):
    take = iter(rest)
    pull = lambda n: [next(take) for _ in range(n)]
    weights = pull(2 * dps + 2)
    att_in = [pull(chips), pull(chips)]
    first_o, pack_o, q_o, cp_o, second_o, n3_o = pull(6)
    wf, sem, tok, tok_sem = pull(4)
    fetch = own_rows(idx, tokens, tok, tok_sem)
    own, dim = tok.shape
    width = wf.shape[1] // (2 * chips)
    heads = width // HDIM
    half = chips * width
    copies = fetch_weights(chips, dps, idx, weights, wf, sem)
    for each in copies:
        for copy in each:
            copy.start()
    for k in range(chips):
        pack_o[0, :, k * width : (k + 1) * width] = att_in[0][k][0:own, :]
        pack_o[0, :, half + k * width : half + (k + 1) * width] = att_in[1][k][own : 2 * own, :]
    fetch.wait()
    for copy in copies[0]:
        copy.wait()
    resid = tok[...].astype(F32) + dot_nn(pack_o[0], wf[0])
    first_o[...] = resid
    n2 = (normalize(resid)[0] * gain[1:2, :].astype(F32) + shift[1:2, :].astype(F32)).astype(BF16)
    pack_o[1, :, :] = n2
    for copy in copies[1]:
        copy.wait()
    q_o[...] = dot_nt(n2, wf[1]).astype(BF16)
    allowed = seen[...] > 0
    for cc in range(2):
        for k in range(chips):
            b = cc * chips + k
            lanes = slice(b * width, (b + 1) * width)
            keys = pair_tiles(att_in[cc][k][2 * own : 2 * own + SEEN, :], heads)
            values = pair_tiles(att_in[cc][k][2 * own + SEEN :, :], heads)
            scores = dot_nt(q_o[:, lanes], keys) * SCALE
            scores = jnp.where(allowed, scores, NEG_FILL)
            e = jnp.exp(scores - half_reduce(jnp.max, scores, heads, NEG_FILL))
            p = (e * (1.0 / half_reduce(jnp.sum, e, heads, 0.0))).astype(BF16)
            cp_o[b] = p
            pack_o[2, :, lanes] = dot_nn(p, values).astype(BF16)
    for copy in copies[2]:
        copy.wait()
    resid = resid + dot_nn(pack_o[2], wf[2])
    second_o[...] = resid
    n3 = normalize(resid)[0] * gain[2:3, :].astype(F32) + shift[2:3, :].astype(F32)
    n3_o[...] = n3.astype(BF16)


def active_kernel(chips, idx, cot, weight, *outs):
    rows = outs[0].shape[0]
    for k in range(chips):
        outs[k][...] = dot_nt(cot[at((idx[0] // 2) ^ k, rows), :], weight[...])


def hidden_kernel(idx, same, other, weight, bias, grad_active, n3_o, act_o, ghi_o, bs_o, bo_o, back):
    own = same.shape[0]
    core = lax.rem(idx[0], 2)
    n3_o[at(core, own), :] = same[...]
    n3_o[at(1 - core, own), :] = other[...]
    v = dot_nn(n3_o[...], weight[...]) + bias[...].astype(F32)
    root = 0.7978845608028654
    square = v * v
    t = jnp.tanh(root * v * (1.0 + 0.044715 * square))
    act_o[...] = (0.5 * v * (1.0 + t)).astype(BF16)
    slope = 0.5 * (1.0 + t) + 0.5 * v * (1.0 - t * t) * (root * (1.0 + 0.134145 * square))
    ghi = (grad_active[...] * slope).astype(BF16)
    ghi_o[...] = ghi
    back[...] = dot_nt(ghi, weight[...])
    bs_o[...] = back[at(core, own), :].astype(BF16)
    bo_o[...] = back[at(1 - core, own), :].astype(BF16)


def mlp_out_kernel(chips, idx, weight, *rest):
    acts = rest[:chips]
    outs = rest[chips : 3 * chips]
    part = rest[3 * chips]
    own = outs[0].shape[0]
    core = lax.rem(idx[0], 2)
    for k in range(chips):
        part[...] = dot_nn(acts[k][...], weight[...])
        outs[2 * k][...] = part[at(core, own), :].astype(BF16)
        outs[2 * k + 1][...] = part[at(1 - core, own), :].astype(BF16)


def mlp_grad_kernel(chips, idx, cot, *rest):
    acts = rest[:chips]
    ghis = rest[chips : 2 * chips]
    n3s = rest[2 * chips : 3 * chips]
    out, bias_o, act, ghi, n3 = rest[3 * chips :]
    step = acts[0].shape[0]
    hid = acts[0].shape[1]
    dps, _, cut = out.shape
    total = jnp.zeros((1, hid), F32)
    for k in range(chips):
        rows = at((idx[0] // 2) ^ k, step)
        act[rows, :] = acts[k][...]
        ghi[rows, :] = ghis[k][...]
        n3[rows, :] = n3s[k][...]
        total += jnp.sum(ghis[k][...].astype(F32), 0, keepdims=True)
    bias_o[...] = total
    for q in range(dps):
        cols = slice(q * cut, (q + 1) * cut)
        out[q, 0:hid, :] = dot_tn(act[...], cot[:, cols]).astype(BF16)
        out[q, hid : 2 * hid, :] = dot_tn(ghi[...], n3[:, cols]).astype(BF16)


def cross_back_kernel(chips, dps, idx, cotangent, gain, second, first, cp, q, *rest):
    take = iter(rest)
    pull = lambda n: [next(take) for _ in range(n)]
    weights = pull(2 * dps + 2)
    parts = pull(chips)
    kv = [pull(chips), pull(chips)]
    pack_o, gf_o, stat_o, same_o, other_o = pull(5)
    gt_o = pull(chips)
    gc, wf, sem, cot, cot_sem = pull(5)
    fetch = own_rows(idx, cotangent, cot, cot_sem)
    copies = fetch_weights(chips, dps, idx, weights, wf, sem)
    for each in reversed(copies):
        for copy in each:
            copy.start()
    dkv_o = (same_o, other_o)
    own = cot.shape[0]
    width = kv[0][0].shape[1]
    heads = width // HDIM
    grad_normed = parts[0][...].astype(F32)
    for k in range(1, chips):
        grad_normed += parts[k][...].astype(F32)
    fetch.wait()
    c = cot[...].astype(F32)
    standard, inverse = normalize(second[...])
    grad = c + norm_backward(standard, inverse, grad_normed, gain[2:3, :].astype(F32))
    stat_o[0:1, :] = jnp.sum(grad_normed * standard, 0, keepdims=True)
    stat_o[1:2, :] = jnp.sum(grad_normed, 0, keepdims=True)
    stat_o[4:5, :] = jnp.sum(c, 0, keepdims=True)
    g2 = grad.astype(BF16)
    pack_o[2, :, :] = g2
    for copy in copies[2]:
        copy.wait()
    gc[...] = dot_nt(g2, wf[2]).astype(BF16)
    for cc in range(2):
        for k in range(chips):
            b = cc * chips + k
            lanes = slice(b * width, (b + 1) * width)
            keys = pair_tiles(kv[cc][k][2 * own : 2 * own + SEEN, :], heads)
            values = pair_tiles(kv[cc][k][2 * own + SEEN :, :], heads)
            gcb = gc[:, lanes]
            dp = dot_nt(gcb, values)
            low = cp[b]
            p = low.astype(F32)
            inner = half_reduce(jnp.sum, dp * p, heads, 0.0)
            ds = (p * (dp - inner) * SCALE).astype(BF16)
            pack_o[1, :, lanes] = dot_nn(ds, keys).astype(BF16)
            dk = dot_tn(ds, q[:, lanes])
            dv = dot_tn(low, gcb)
            for i, d in enumerate((dk, dv)):
                fold = head_select([d[h * SEEN : (h + 1) * SEEN, :] for h in range(heads)], 1)
                dkv_o[cc][k, i, :, :] = fold.astype(BF16)
    for copy in copies[1]:
        copy.wait()
    grad_normed = dot_nn(pack_o[1], wf[1])
    standard, inverse = normalize(first[...])
    grad = grad + norm_backward(standard, inverse, grad_normed, gain[1:2, :].astype(F32))
    stat_o[2:3, :] = jnp.sum(grad_normed * standard, 0, keepdims=True)
    stat_o[3:4, :] = jnp.sum(grad_normed, 0, keepdims=True)
    gf_o[...] = grad
    g1 = grad.astype(BF16)
    pack_o[0, :, :] = g1
    for copy in copies[0]:
        copy.wait()
    gatt = dot_nt(g1, wf[0]).astype(BF16)
    for cc in range(2):
        for k in range(chips):
            b = cc * chips + k
            gt_o[k][cc, :, :] = gatt[:, b * width : (b + 1) * width]


def row_grad_kernel(chips, idx, fwd, fwd2, bwd, bwd2, out, left, right):
    dps, height, cut = out.shape
    width = height // (3 * chips)
    own = fwd.shape[1]
    half = chips * width
    for m, (l, r) in enumerate((((fwd, fwd2), (bwd, bwd2)), ((bwd, bwd2), (fwd, fwd2)), ((fwd, fwd2), (bwd, bwd2)))):
        left[0:own, :] = l[0][m, :, 0:half]
        left[own : 2 * own, :] = l[1][m, :, half : 2 * half]
        right[0:own, :] = r[0][m]
        right[own : 2 * own, :] = r[1][m]
        for q in range(dps):
            part = dot_tn(left[...], right[:, q * cut : (q + 1) * cut]).astype(BF16)
            for k in range(chips):
                row = (3 * k + m) * width
                out[q, row : row + width, :] = part[k * width : (k + 1) * width, :]


def pack_kernel(idx, *refs):
    parts, out = refs[:-1], refs[-1]
    width = parts[0].shape[0] // 3
    for m in range(3):
        for k, part in enumerate(parts):
            row = (m * len(parts) + k) * width
            out[row : row + width, :] = part[m * width : (m + 1) * width, :]


def self_back_kernel(chips, idx, triple, probs, weight, *rest):
    take = iter(rest)
    pull = lambda n: [next(take) for _ in range(n)]
    grads = [pull(chips), pull(chips)]
    (gt_o,) = pull(1)
    bs_o, bo_o = pull(chips), pull(chips)
    gout, key_t, wcat, dk, dv, back = pull(6)
    rows, width = triple.shape[1], triple.shape[2]
    heads = width // HDIM
    own = bs_o[0].shape[0]
    for k in range(chips):
        gout[at(idx[0] ^ (2 * k), own), :] = grads[0][k][0]
        gout[at(idx[0] ^ (2 * k + 1), own), :] = grads[1][k][1]
    for c in range(3):
        wcat[:, c * width : (c + 1) * width] = weight[c]
    count = rows // QB
    for i in range(count):
        here = slice(i * QB, (i + 1) * QB)
        key_t[:, here] = triple[1, here, :].astype(F32).T.astype(BF16)
    for i in reversed(range(count)):
        here = slice(i * QB, (i + 1) * QB)
        seen = (i + 1) * QB
        dq = []
        for h in range(heads):
            go = head_only(gout[here, :], h, heads)
            query = head_only(triple[0, here, :], h, heads)
            dp = dot_nt(triple[2, 0:seen, :], go)
            low = probs[h, 0:seen, here]
            p = low.astype(F32)
            inner = jnp.sum(dp * p, 0, keepdims=True)
            ds = (p * (dp - inner) * SCALE).astype(BF16)
            new_k = dot_nn(ds, query)
            new_v = dot_nn(low, go)
            if i == count - 1 and h == 0:
                dk[0:seen, :] = new_k
                dv[0:seen, :] = new_v
            else:
                dk[0:seen, :] += new_k
                dv[0:seen, :] += new_v
            dq.append(dot_nn(key_t[:, 0:seen], ds))
        gt_o[here, 0:width] = head_select(dq, 0).T.astype(BF16)
        gt_o[here, width : 2 * width] = dk[here, :].astype(BF16)
        gt_o[here, 2 * width : 3 * width] = dv[here, :].astype(BF16)
        back[here, :] = dot_nt(gt_o[here, :], wcat[...]).astype(BF16)
    for k in range(chips):
        bs_o[k][...] = back[at(idx[0] ^ (2 * k), own), :]
        bo_o[k][...] = back[at(idx[0] ^ (2 * k + 1), own), :]


def self_grad_kernel(chips, dps, idx, tok, normed, gt, states, gp, *rest):
    same, other = rest[:chips], rest[chips : 2 * chips]
    out, stat_o = rest[2 * chips :]
    cut = out.shape[2]
    width = gp.shape[2]
    for q in range(dps):
        cols = slice(q * cut, (q + 1) * cut)
        out[q, 0 : 3 * width, :] = dot_tn(gt[...], normed[:, cols]).astype(BF16)
        for c in range(2):
            out[q, (3 + c) * width : (4 + c) * width, :] = dot_tn(
                gp[c], states[:, cols]
            ).astype(BF16)
    own = same[0].shape[0]
    gain = jnp.zeros((1, tok.shape[1]), F32)
    shift = gain
    for k in range(chips):
        for cc, part in enumerate((same[k], other[k])):
            g = part[...].astype(F32)
            standard, _ = normalize(tok[at(idx[0] ^ (2 * k + cc), own), :].astype(F32))
            gain += jnp.sum(g * standard, 0, keepdims=True)
            shift += jnp.sum(g, 0, keepdims=True)
    stat_o[0:1, :] = gain
    stat_o[1:2, :] = shift


def token_kernel(idx, tokens, gain, grad, *rest):
    parts, (out, tok, sem) = rest[:-3], rest[-3:]
    own_rows(idx, tokens, tok, sem).wait()
    grad_normed = parts[0][...].astype(F32)
    for part in parts[1:]:
        grad_normed += part[...].astype(F32)
    standard, inverse = normalize(tok[...].astype(F32))
    out[...] = grad[...] + norm_backward(standard, inverse, grad_normed, gain[0:1, :].astype(F32))


def place_kernel(plan, idx, *refs):
    parts, outs = refs[: -len(plan)], refs[-len(plan) :]
    if len(parts) == 1:
        source = parts[0]
        count, _, cut = source.shape
        take = lambda q, rows: source[q, rows, :]
        where_of = lambda q: slice(q * cut, (q + 1) * cut)
    else:
        count, cut = len(parts), parts[0].shape[1]
        take = lambda q, rows: parts[q][rows, :]
        where_of = lambda q: at(idx[1] ^ q, cut)
    row = 0
    for out, (height, lead, flip) in zip(outs, plan):
        for q in range(count):
            where = where_of(q)
            piece = take(q, slice(row, row + height)).astype(F32)
            if not flip:
                out[:, where] = piece
            elif lead is None:
                out[where, :] = piece.T
            else:
                step = height // lead
                for c in range(lead):
                    out[c, where, :] = piece[c * step : (c + 1) * step, :].T
        row += height


def flip_bits(axis, bits, size):
    return functools.partial(
        lax.ppermute, axis_name=axis, perm=[(i, i ^ bits) for i in range(size)]
    )


def total(*parts):
    out = parts[0].astype(F32)
    for part in parts[1:]:
        out = out + part.astype(F32)
    return out


def body(
    tokens,
    states,
    cotangent,
    self_weight,
    self_output,
    cross_query,
    cross_pair,
    cross_output,
    hidden_weight,
    hidden_bias,
    output_weight,
    output_bias,
    norm_gain,
    norm_shift,
    state_row,
    state_segment,
    caption,
):
    rows, dim = tokens.shape
    width = cross_query.shape[1]
    heads = width // HDIM
    hid = hidden_bias.shape[0]
    cores = lax.axis_size("mp")
    chips = cores // 2
    dps = lax.axis_size("dp")
    own = rows // cores
    cut = dim // dps
    me = lax.axis_index("mp")
    dpi = lax.axis_index("dp")
    idx = jnp.stack([me, dpi, state_row[0], caption[0]]).astype(jnp.int32)
    to_z = [flip_bits("mp", 2 * k, cores) for k in range(chips)]
    to_core = flip_bits("mp", 1, cores)
    to_dp = [flip_bits("dp", q, dps) for q in range(dps)]
    far = range(1, chips)
    peers = range(1, dps)

    def share_dp(piece):
        return lax.all_to_all(jnp.broadcast_to(piece[None], (dps,) + piece.shape), "dp", 0, 0)

    def swap_dp(pieces):
        return lax.all_to_all(pieces, "dp", 0, 0)

    def sum_dp(pieces):
        return jnp.sum(pieces.astype(F32), 0).astype(BF16)

    labels = lax.dynamic_index_in_dim(state_segment, state_row[0], 0, False)
    begin = jnp.minimum(jnp.sum((labels < caption[0]).astype(jnp.int32)), labels.shape[0] - SEEN)
    labels = lax.dynamic_slice_in_dim(labels, begin, SEEN, 0)
    seen = jnp.tile((labels == caption[0]).astype(jnp.int32)[None, :], (1, heads))
    near = lax.dynamic_slice(states, (state_row[0], begin, 0), (1, SEEN, dim))[0]

    mine = jnp.concatenate([self_output, cross_query.T, cross_output], 0)
    piece = lax.dynamic_slice_in_dim(mine, dpi * cut, cut, 1)
    got = [to_z[k](piece) for k in far]

    outs = call(
        functools.partial(self_kernel, chips),
        [
            ((rows, dim), BF16),
            ((3, rows, width), BF16),
            ((heads, rows, rows), BF16),
        ]
        + [((2 * own + 2 * SEEN, width), BF16)] * chips,
        idx,
        tokens,
        self_weight,
        norm_gain,
        norm_shift,
        states,
        cross_pair,
        state_segment,
        scratch=[
            pltpu.VMEM((width, rows), BF16),
            pltpu.VMEM((rows, width), BF16),
            pltpu.VMEM((states.shape[1], width), F32),
        ],
        after=(piece,),
        stage=True,
        name="self_fwd",
    )
    normed_one, triple, probs = outs[:3]
    att = outs[3:]
    got = lax.optimization_barrier((*got, att[0]))[:-1]
    (cat,) = call(pack_kernel, [((3 * width * (chips - 1), cut), BF16)], idx, *got, tight=True, name="pack")
    att = [att[0]] + [to_z[k](att[k]) for k in far]
    att2 = [to_core(x) for x in att]

    grad_active = call(
        functools.partial(active_kernel, chips),
        [((2 * own, hid), F32)] * chips,
        idx,
        cotangent,
        output_weight,
        after=att[:1],
        stage=True,
        name="grad_active",
    )

    cats = [cat] + [to_dp[q](cat) for q in peers]
    cats, grad_active, seen = lax.optimization_barrier((cats, grad_active, seen))
    weights = [mine, *cats, to_core(mine), *[to_core(x) for x in cats]]

    sq = cores * width
    first, fwd, q, cp, second, n3 = call(
        functools.partial(cross_kernel, chips, dps),
        [
            ((own, dim), F32),
            ((3, own, dim), BF16),
            ((own, sq), BF16),
            ((cores, own, heads * SEEN), BF16),
            ((own, dim), F32),
            ((own, dim), BF16),
        ],
        idx,
        tokens,
        norm_gain,
        norm_shift,
        seen,
        *weights,
        *att,
        *att2,
        scratch=[
            pltpu.VMEM((3, sq, dim), BF16),
            pltpu.SemaphoreType.DMA((3, 2 * dps + 2)),
            pltpu.VMEM((own, dim), BF16),
            pltpu.SemaphoreType.DMA,
        ],
        raw=(0, *range(4, 4 + len(weights))),
        stage=True,
        name="cross_fwd",
    )

    n3s = [n3] + [to_z[k](n3) for k in far]
    fwd2 = to_core(fwd)
    bias_row = hidden_bias[None, :]
    acts, ghis, chunks, sent = [], [], [], []
    for k in range(chips):
        arrived = n3s[k]
        if k:
            arrived = lax.optimization_barrier((arrived, acts[min(k, 2) - 1]))[0]
        chunk, act, ghi, bs, bo = call(
            hidden_kernel,
            [
                ((2 * own, dim), BF16),
                ((2 * own, hid), BF16),
                ((2 * own, hid), BF16),
                ((own, dim), BF16),
                ((own, dim), BF16),
            ],
            idx,
            arrived,
            to_core(arrived),
            hidden_weight,
            bias_row,
            grad_active[k],
            scratch=[pltpu.VMEM((2 * own, dim), F32)],
            after=acts[-1:],
            tight=True,
            name="hidden",
        )
        acts.append(act)
        ghis.append(ghi)
        chunks.append(chunk)
        sent.append(total(bs, to_core(bo)).astype(BF16))
    backs = sent[:1] + [to_z[k](sent[k]) for k in far]
    mlp_grad, bias_part = call(
        functools.partial(mlp_grad_kernel, chips),
        [((dps, 2 * hid, cut), BF16), ((1, hid), F32)],
        idx,
        cotangent,
        *acts,
        *ghis,
        *chunks,
        scratch=[
            pltpu.VMEM((rows, hid), BF16),
            pltpu.VMEM((rows, hid), BF16),
            pltpu.VMEM((rows, dim), BF16),
        ],
        after=sent,
        stage=True,
        name="mlp_grad",
    )
    mlp_grad, backs[1] = lax.optimization_barrier((mlp_grad, backs[1]))
    mlp_swap = swap_dp(mlp_grad)
    outs = call(
        functools.partial(mlp_out_kernel, chips),
        [((own, dim), BF16)] * (2 * chips),
        idx,
        output_weight,
        *acts,
        scratch=[pltpu.VMEM((2 * own, dim), F32)],
        after=(mlp_grad,),
        stage=True,
        name="mlp_out",
    )
    *backs, mlp_part = lax.optimization_barrier((*backs, outs))

    outs = call(
        functools.partial(cross_back_kernel, chips, dps),
        [
            ((3, own, dim), BF16),
            ((own, dim), F32),
            ((8, dim), F32),
            ((chips, 2, SEEN, width), BF16),
            ((chips, 2, SEEN, width), BF16),
        ]
        + [((2, own, width), BF16)] * chips,
        idx,
        cotangent,
        norm_gain,
        second,
        first,
        cp,
        q,
        *weights,
        *backs,
        *att,
        *att2,
        scratch=[
            pltpu.VMEM((own, sq), BF16),
            pltpu.VMEM((3, sq, dim), BF16),
            pltpu.SemaphoreType.DMA((3, 2 * dps + 2)),
            pltpu.VMEM((own, dim), BF16),
            pltpu.SemaphoreType.DMA,
        ],
        raw=(0, *range(6, 6 + len(weights))),
        cost=10**12,
        stage=True,
        name="cross_bwd",
    )
    bwd, gf, stat_a, dkv, dkv_other = outs[:5]
    gatt = outs[5:]
    gatt = [gatt[0]] + [to_z[k](gatt[k]) for k in far]

    (row_grad,) = call(
        functools.partial(row_grad_kernel, chips),
        [((dps, chips * 3 * width, cut), BF16)],
        idx,
        fwd,
        fwd2,
        bwd,
        to_core(bwd),
        scratch=[pltpu.VMEM((2 * own, chips * width), BF16), pltpu.VMEM((2 * own, dim), BF16)],
        stage=True,
        name="row_grad",
    )
    gatt, row_grad, mlp_swap, mlp_part = lax.optimization_barrier(
        (gatt, row_grad, mlp_swap, mlp_part)
    )
    gatt2 = [to_core(x) for x in gatt]
    row_swap = swap_dp(row_grad)

    outs = call(
        functools.partial(self_back_kernel, chips),
        [((rows, 3 * width), BF16)] + [((own, dim), BF16)] * (2 * chips),
        idx,
        triple,
        probs,
        self_weight,
        *gatt,
        *gatt2,
        scratch=[
            pltpu.VMEM((rows, width), BF16),
            pltpu.VMEM((width, rows), BF16),
            pltpu.VMEM((dim, 3 * width), BF16),
            pltpu.VMEM((rows, width), F32),
            pltpu.VMEM((rows, width), F32),
            pltpu.VMEM((rows, dim), BF16),
        ],
        stage=True,
        name="self_bwd",
    )
    gt, bs, bo = outs[0], outs[1 : 1 + chips], outs[1 + chips :]
    sent = [total(bs[k], to_core(bo[k])).astype(BF16) for k in range(chips)]
    mlp_swap = lax.optimization_barrier((mlp_swap, sent[0]))[0]
    mlp_piece = sum_dp(mlp_swap)
    mlp_all = [mlp_piece] + [to_dp[q](mlp_piece) for q in peers]
    parts = sent[:1] + [to_z[k](sent[k]) for k in far]

    dkv = total(dkv, to_core(dkv_other)).astype(BF16)
    gp = total(dkv[0], *[to_z[k](dkv[k]) for k in far]).astype(BF16)

    self_part, stat_b = call(
        functools.partial(self_grad_kernel, chips, dps),
        [((dps, 5 * width, cut), BF16), ((8, dim), F32)],
        idx,
        tokens,
        normed_one,
        gt,
        near,
        gp,
        *bs,
        *bo,
        after=sent,
        stage=True,
        name="self_grad",
    )
    parts, self_part, row_swap, stat_b = lax.optimization_barrier(
        (parts, self_part, row_swap, stat_b)
    )
    (grad_tokens,) = call(
        token_kernel,
        [((own, dim), F32)],
        idx,
        tokens,
        norm_gain,
        gf,
        *parts,
        scratch=[pltpu.VMEM((own, dim), BF16), pltpu.SemaphoreType.DMA],
        raw=(0,),
        stage=True,
        name="tokens",
    )
    self_swap = swap_dp(self_part)
    mlp_part = lax.optimization_barrier((mlp_part, parts[0]))[0]
    mlp_sent = [
        total(mlp_part[2 * k], to_core(mlp_part[2 * k + 1])).astype(BF16) for k in range(chips)
    ]
    mlp_parts = mlp_sent[:1] + [to_z[k](mlp_sent[k]) for k in far]
    state_part = jnp.einsum("cse,cde->sd", gp, cross_pair, preferred_element_type=F32)
    state_part = state_part.astype(BF16)
    state_part = total(state_part, to_core(state_part)).astype(BF16)
    state_grad = total(state_part, *[to_z[k](state_part) for k in far])
    grad_states = lax.dynamic_update_slice(
        jnp.zeros(states.shape, F32), state_grad[None], (state_row[0], begin, 0)
    )
    block_output = (second + total(*mlp_parts) + output_bias.astype(F32)).astype(BF16)

    row_piece = sum_dp(row_swap).reshape(chips, 3 * width, cut)
    row_piece = total(row_piece[0], *[to_z[k](row_piece[k]) for k in far]).astype(BF16)
    self_piece = sum_dp(self_swap)
    slots = lax.dynamic_update_slice(jnp.zeros((cores, hid), F32), bias_part, (me, 0))
    stats = jnp.concatenate([stat_b[:2], stat_a[:5], slots.reshape(-1, dim)], 0)
    for axis, size in (("mp", cores), ("dp", dps)):
        bits = 1
        while bits < size:
            stats = stats + flip_bits(axis, bits, size)(stats)
            bits *= 2

    def place(pieces, plan, shapes, name):
        return call(
            functools.partial(place_kernel, plan),
            [(s, F32) for s in shapes],
            idx,
            *pieces,
            stage=True,
            name=name,
        )

    grad_output_weight, grad_hidden_weight = place(
        mlp_all, ((hid, None, False), (hid, None, True)), ((hid, dim), (dim, hid)), "place_mlp"
    )
    piece = jnp.concatenate([row_piece, self_piece], 0)
    piece, stats = lax.optimization_barrier((piece, stats))
    (
        grad_self_output,
        grad_cross_query,
        grad_cross_output,
        grad_self_weight,
        grad_cross_pair,
    ) = place(
        [share_dp(piece)],
        (
            (width, None, False),
            (width, None, True),
            (width, None, False),
            (3 * width, 3, True),
            (2 * width, 2, True),
        ),
        (
            (width, dim),
            (dim, width),
            (width, dim),
            (3, dim, width),
            (2, dim, width),
        ),
        "place",
    )
    grad_norm_gain = jnp.stack([stats[0], stats[4], stats[2]])
    grad_norm_shift = jnp.stack([stats[1], stats[5], stats[3]])
    grad_output_bias = stats[6]
    grad_hidden_bias = lax.dynamic_index_in_dim(stats[7:].reshape(cores, hid), me, 0, False)
    return (
        block_output,
        grad_tokens,
        grad_states,
        grad_self_weight,
        grad_self_output,
        grad_cross_query,
        grad_cross_pair,
        grad_cross_output,
        grad_hidden_weight,
        grad_hidden_bias,
        grad_output_weight,
        grad_output_bias,
        grad_norm_gain,
        grad_norm_shift,
    )


def solution(mesh):
    placed = (
        P("dp", None),
        P("dp", None, None),
        P("dp", None),
        P(None, None, "mp"),
        P("mp", None),
        P(None, "mp"),
        P(None, None, "mp"),
        P("mp", None),
        P(None, "mp"),
        P("mp"),
        P("mp", None),
        P(),
        P(),
        P(),
        P("dp"),
        P("dp", None),
        P("dp"),
    )
    return jax.shard_map(
        body,
        mesh=mesh,
        in_specs=placed,
        out_specs=(
            P(("dp", "mp"), None),
            P(("dp", "mp"), None),
            P("dp", None, None),
            P(None, None, "mp"),
            P("mp", None),
            P(None, "mp"),
            P(None, None, "mp"),
            P("mp", None),
            P(None, "mp"),
            P("mp"),
            P("mp", None),
            P(),
            P(),
            P(),
        ),
        check_vma=False,
    )
```

```python
import functools
import math

import jax
import jax.numpy as jnp
from jax import lax
from jax.experimental import pallas as pl
from jax.experimental.pallas import tpu as pltpu
from jax.sharding import PartitionSpec as P

HDIM = 64
SEEN = 64
QB = 256
EPSILON = 1e-05
NEG_FILL = -1e30
SCALE = HDIM ** (-0.5)
F32 = jnp.float32
BF16 = jnp.bfloat16


def dot_nn(a, b):
    return lax.dot_general(a, b, (((1,), (0,)), ((), ())), preferred_element_type=F32)


def dot_nt(a, b):
    return lax.dot_general(a, b, (((1,), (1,)), ((), ())), preferred_element_type=F32)


def dot_tn(a, b):
    return lax.dot_general(a, b, (((0,), (0,)), ((), ())), preferred_element_type=F32)


def normalize(resid):
    center = resid - jnp.mean(resid, -1, keepdims=True)
    inverse = lax.rsqrt(jnp.mean(center * center, -1, keepdims=True) + EPSILON)
    return (center * inverse, inverse)


def norm_backward(standard, inverse, grad_normed, gain):
    scaled = grad_normed * gain
    return inverse * (
        scaled
        - jnp.mean(scaled, -1, keepdims=True)
        - standard * jnp.mean(scaled * standard, -1, keepdims=True)
    )


def at(index, size):
    return pl.ds(pl.multiple_of(index * size, size), size)


def staged(kernel, ins, outs, extra, *refs):
    count_in, count_out = len(ins), len(outs)
    idx, refs = refs[0], list(refs[1:])
    inner = refs[: count_in + count_out]
    own = refs[count_in + count_out : count_in + count_out + extra]
    rest = refs[count_in + count_out + extra :]
    sem_in, sem_out = rest[-2:]
    held = iter(rest[:-2])
    started, results = [], []
    for i, here in enumerate(ins):
        if here:
            local = next(held)
            started.append(pltpu.make_async_copy(inner[i], local, sem_in.at[len(started)]))
            inner[i] = local
    for i, here in enumerate(outs):
        if here:
            local = next(held)
            target = inner[count_in + i]
            results.append(pltpu.make_async_copy(local, target, sem_out.at[len(results)]))
            inner[count_in + i] = local
    for copy in started:
        copy.start()
    for copy in started:
        copy.wait()
    kernel(idx, *inner, *own)
    for copy in results:
        copy.start()
    for copy in results:
        copy.wait()


def call(
    kernel, outs, idx, *args, scratch=(), after=(), stage=False, tight=False, raw=(), cost=1, name=None, spill=8
):
    if after:
        idx = lax.optimization_barrier((idx, *after))[0]
    out_shape = [jax.ShapeDtypeStruct(s, t) for s, t in outs]
    big = lambda a: bool(stage) and a.size >= 1 << 15
    ins_far = [big(a) and i not in raw for i, a in enumerate(args)]
    outs_far = [big(a) for a in out_shape]
    vmem = pl.BlockSpec(memory_space=pltpu.VMEM)
    hbm = pl.BlockSpec(memory_space=pltpu.HBM)
    held = spill << 20
    for i, a in enumerate((*args, *out_shape)):
        if i not in raw:
            held += a.size * a.dtype.itemsize
    for a in scratch:
        if len(getattr(a, "shape", ())) > 1 and a.dtype in (F32, BF16):
            held += math.prod(a.shape) * jnp.dtype(a.dtype).itemsize
    scratch = list(scratch)
    if any(ins_far) or any(outs_far):
        kernel = functools.partial(staged, kernel, ins_far, outs_far, len(scratch))
        for a, far in zip((*args, *out_shape), ins_far + outs_far):
            if far:
                scratch.append(pltpu.VMEM(a.shape, a.dtype))
        scratch.append(pltpu.SemaphoreType.DMA((max(1, sum(ins_far)),)))
        scratch.append(pltpu.SemaphoreType.DMA((max(1, sum(outs_far)),)))
    return pl.pallas_call(
        kernel,
        out_shape=out_shape,
        in_specs=[pl.BlockSpec(memory_space=pltpu.SMEM)]
        + [hbm if far or i in raw else vmem for i, far in enumerate(ins_far)],
        out_specs=[hbm if far else vmem for far in outs_far],
        scratch_shapes=scratch,
        cost_estimate=pl.CostEstimate(flops=cost, bytes_accessed=1, transcendentals=0),
        compiler_params=pltpu.CompilerParams(
            vmem_limit_bytes=min(held, 60 << 20) if tight else 60 << 20
        ),
        name=name,
    )(idx, *args)


def head_select(parts, axis):
    if len(parts) == 1:
        return parts[0]
    head = lax.broadcasted_iota(jnp.int32, parts[0].shape, axis) // HDIM
    return jnp.where(head == 0, parts[0], parts[1])


def head_only(value, h, count):
    if count == 1:
        return value
    head = lax.broadcasted_iota(jnp.int32, value.shape, 1) // HDIM
    return jnp.where(head == h, value, jnp.zeros_like(value))


def self_kernel(
    chips, idx, tok, weight, gain, shift, states, pair, segment, normed, triple, probs, *rest
):
    att_out = rest[:chips]
    val_t, att, kv = rest[chips:]
    rows, width = tok.shape[0], weight.shape[2]
    heads = width // HDIM
    g = gain[0:1, :].astype(F32)
    s = shift[0:1, :].astype(F32)
    for i in range(rows // QB):
        here = slice(i * QB, (i + 1) * QB)
        standard, _ = normalize(tok[here, :].astype(F32))
        n = (standard * g + s).astype(BF16)
        normed[here, :] = n
        query = dot_nn(n, weight[0]).astype(BF16)
        triple[0, here, :] = query
        triple[1, here, :] = dot_nn(n, weight[1]).astype(BF16)
        value = dot_nn(n, weight[2])
        triple[2, here, :] = value.astype(BF16)
        val_t[:, here] = value.T.astype(BF16)
        seen = (i + 1) * QB
        outs = []
        for h in range(heads):
            scores = dot_nt(triple[1, 0:seen, :], head_only(query, h, heads)) * SCALE
            key_at = lax.broadcasted_iota(jnp.int32, scores.shape, 0)
            row_at = lax.broadcasted_iota(jnp.int32, scores.shape, 1) + i * QB
            scores = jnp.where(key_at <= row_at, scores, NEG_FILL)
            e = jnp.exp(scores - jnp.max(scores, 0, keepdims=True))
            p = (e * (1.0 / jnp.sum(e, 0, keepdims=True))).astype(BF16)
            probs[h, 0:seen, here] = p
            outs.append(dot_nn(val_t[:, 0:seen], p))
        att[here, :] = head_select(outs, 0).T.astype(BF16)
    own = (att_out[0].shape[0] - 2 * SEEN) // 2
    before = segment[pl.ds(idx[2], 1), :] < idx[3]
    begin = jnp.minimum(jnp.sum(before.astype(jnp.int32)), states.shape[1] - SEEN)
    for c in range(2):
        kv[...] = dot_nn(states[idx[2]], pair[c])
        for k in range(chips):
            where = slice(2 * own + c * SEEN, 2 * own + (c + 1) * SEEN)
            att_out[k][where, :] = kv[pl.ds(begin, SEEN), :].astype(BF16)
    for k in range(chips):
        for cc in range(2):
            att_out[k][cc * own : (cc + 1) * own, :] = att[at(idx[0] ^ (2 * k + cc), own), :]


def pair_tiles(block, heads):
    return jnp.concatenate([head_only(block, h, heads) for h in range(heads)], 0)


def half_reduce(op, value, heads, fill):
    if heads == 1:
        return op(value, -1, keepdims=True)
    half = lax.broadcasted_iota(jnp.int32, value.shape, 1) // SEEN
    first = op(jnp.where(half == 0, value, fill), -1, keepdims=True)
    other = op(jnp.where(half == 1, value, fill), -1, keepdims=True)
    return jnp.where(half == 0, first, other)


def fetch_weights(chips, dps, idx, weights, wf, sem):
    width = wf.shape[1] // (2 * chips)
    cut = wf.shape[2] // dps
    span = (chips - 1) * width
    half = chips * width
    lists = []
    for m in range(3):
        copies = []
        for cc in range(2):
            source = weights[cc * (dps + 1)]
            where = wf.at[m, cc * half : cc * half + width, :]
            copies.append((source.at[m * width : (m + 1) * width, :], where))
            for q in range(dps):
                source = weights[cc * (dps + 1) + 1 + q]
                cols = at(idx[1] ^ q, cut)
                where = wf.at[m, cc * half + width : (cc + 1) * half, cols]
                copies.append((source.at[m * span : (m + 1) * span, :], where))
        lists.append(
            [pltpu.make_async_copy(s, d, sem.at[m, i]) for i, (s, d) in enumerate(copies)]
        )
    return lists


def own_rows(idx, source, rows, sem):
    copy = pltpu.make_async_copy(source.at[at(idx[0], rows.shape[0]), :], rows, sem)
    copy.start()
    return copy


def cross_kernel(chips, dps, idx, tokens, gain, shift, seen, *rest):
    take = iter(rest)
    pull = lambda n: [next(take) for _ in range(n)]
    weights = pull(2 * dps + 2)
    att_in = [pull(chips), pull(chips)]
    first_o, pack_o, q_o, cp_o, second_o, n3_o = pull(6)
    wf, sem, tok, tok_sem = pull(4)
    fetch = own_rows(idx, tokens, tok, tok_sem)
    own, dim = tok.shape
    width = wf.shape[1] // (2 * chips)
    heads = width // HDIM
    half = chips * width
    copies = fetch_weights(chips, dps, idx, weights, wf, sem)
    for each in copies:
        for copy in each:
            copy.start()
    for k in range(chips):
        pack_o[0, :, k * width : (k + 1) * width] = att_in[0][k][0:own, :]
        pack_o[0, :, half + k * width : half + (k + 1) * width] = att_in[1][k][own : 2 * own, :]
    fetch.wait()
    for copy in copies[0]:
        copy.wait()
    resid = tok[...].astype(F32) + dot_nn(pack_o[0], wf[0])
    first_o[...] = resid
    n2 = (normalize(resid)[0] * gain[1:2, :].astype(F32) + shift[1:2, :].astype(F32)).astype(BF16)
    pack_o[1, :, :] = n2
    for copy in copies[1]:
        copy.wait()
    q_o[...] = dot_nt(n2, wf[1]).astype(BF16)
    allowed = seen[...] > 0
    for cc in range(2):
        for k in range(chips):
            b = cc * chips + k
            lanes = slice(b * width, (b + 1) * width)
            keys = pair_tiles(att_in[cc][k][2 * own : 2 * own + SEEN, :], heads)
            values = pair_tiles(att_in[cc][k][2 * own + SEEN :, :], heads)
            scores = dot_nt(q_o[:, lanes], keys) * SCALE
            scores = jnp.where(allowed, scores, NEG_FILL)
            e = jnp.exp(scores - half_reduce(jnp.max, scores, heads, NEG_FILL))
            p = (e * (1.0 / half_reduce(jnp.sum, e, heads, 0.0))).astype(BF16)
            cp_o[b] = p
            pack_o[2, :, lanes] = dot_nn(p, values).astype(BF16)
    for copy in copies[2]:
        copy.wait()
    resid = resid + dot_nn(pack_o[2], wf[2])
    second_o[...] = resid
    n3 = normalize(resid)[0] * gain[2:3, :].astype(F32) + shift[2:3, :].astype(F32)
    n3_o[...] = n3.astype(BF16)


def active_kernel(chips, idx, cot, weight, *outs):
    rows = outs[0].shape[0]
    for k in range(chips):
        outs[k][...] = dot_nt(cot[at((idx[0] // 2) ^ k, rows), :], weight[...])


def hidden_kernel(idx, same, other, weight, bias, grad_active, n3_o, act_o, ghi_o, bs_o, bo_o, back):
    own = same.shape[0]
    core = lax.rem(idx[0], 2)
    n3_o[at(core, own), :] = same[...]
    n3_o[at(1 - core, own), :] = other[...]
    v = dot_nn(n3_o[...], weight[...]) + bias[...].astype(F32)
    root = 0.7978845608028654
    square = v * v
    t = jnp.tanh(root * v * (1.0 + 0.044715 * square))
    act_o[...] = (0.5 * v * (1.0 + t)).astype(BF16)
    slope = 0.5 * (1.0 + t) + 0.5 * v * (1.0 - t * t) * (root * (1.0 + 0.134145 * square))
    ghi = (grad_active[...] * slope).astype(BF16)
    ghi_o[...] = ghi
    back[...] = dot_nt(ghi, weight[...])
    bs_o[...] = back[at(core, own), :].astype(BF16)
    bo_o[...] = back[at(1 - core, own), :].astype(BF16)


def mlp_out_kernel(chips, idx, weight, *rest):
    acts = rest[:chips]
    outs = rest[chips : 3 * chips]
    part = rest[3 * chips]
    own = outs[0].shape[0]
    core = lax.rem(idx[0], 2)
    for k in range(chips):
        part[...] = dot_nn(acts[k][...], weight[...])
        outs[2 * k][...] = part[at(core, own), :].astype(BF16)
        outs[2 * k + 1][...] = part[at(1 - core, own), :].astype(BF16)


def mlp_grad_kernel(chips, idx, cot, *rest):
    acts = rest[:chips]
    ghis = rest[chips : 2 * chips]
    n3s = rest[2 * chips : 3 * chips]
    out, bias_o, act, ghi, n3 = rest[3 * chips :]
    step = acts[0].shape[0]
    hid = acts[0].shape[1]
    dps, _, cut = out.shape
    total = jnp.zeros((1, hid), F32)
    for k in range(chips):
        rows = at((idx[0] // 2) ^ k, step)
        act[rows, :] = acts[k][...]
        ghi[rows, :] = ghis[k][...]
        n3[rows, :] = n3s[k][...]
        total += jnp.sum(ghis[k][...].astype(F32), 0, keepdims=True)
    bias_o[...] = total
    for q in range(dps):
        cols = slice(q * cut, (q + 1) * cut)
        out[q, 0:hid, :] = dot_tn(act[...], cot[:, cols]).astype(BF16)
        out[q, hid : 2 * hid, :] = dot_tn(ghi[...], n3[:, cols]).astype(BF16)


def cross_back_kernel(chips, dps, count, idx, cotangent, gain, second, first, cp, q, *rest):
    take = iter(rest)
    pull = lambda n: [next(take) for _ in range(n)]
    weights = pull(2 * dps + 2)
    parts = pull(count)
    kv = [pull(chips), pull(chips)]
    pack_o, gf_o, stat_o, same_o, other_o = pull(5)
    gt_o = pull(chips)
    gc, wf, sem, cot, cot_sem = pull(5)
    fetch = own_rows(idx, cotangent, cot, cot_sem)
    copies = fetch_weights(chips, dps, idx, weights, wf, sem)
    for each in reversed(copies):
        for copy in each:
            copy.start()
    dkv_o = (same_o, other_o)
    own = cot.shape[0]
    width = kv[0][0].shape[1]
    heads = width // HDIM
    grad_normed = parts[0][...].astype(F32)
    for part in parts[1:]:
        grad_normed += part[...].astype(F32)
    fetch.wait()
    c = cot[...].astype(F32)
    standard, inverse = normalize(second[...])
    grad = c + norm_backward(standard, inverse, grad_normed, gain[2:3, :].astype(F32))
    stat_o[0:1, :] = jnp.sum(grad_normed * standard, 0, keepdims=True)
    stat_o[1:2, :] = jnp.sum(grad_normed, 0, keepdims=True)
    stat_o[4:5, :] = jnp.sum(c, 0, keepdims=True)
    g2 = grad.astype(BF16)
    pack_o[2, :, :] = g2
    for copy in copies[2]:
        copy.wait()
    gc[...] = dot_nt(g2, wf[2]).astype(BF16)
    for cc in range(2):
        for k in range(chips):
            b = cc * chips + k
            lanes = slice(b * width, (b + 1) * width)
            keys = pair_tiles(kv[cc][k][2 * own : 2 * own + SEEN, :], heads)
            values = pair_tiles(kv[cc][k][2 * own + SEEN :, :], heads)
            gcb = gc[:, lanes]
            dp = dot_nt(gcb, values)
            low = cp[b]
            p = low.astype(F32)
            inner = half_reduce(jnp.sum, dp * p, heads, 0.0)
            ds = (p * (dp - inner) * SCALE).astype(BF16)
            pack_o[1, :, lanes] = dot_nn(ds, keys).astype(BF16)
            dk = dot_tn(ds, q[:, lanes])
            dv = dot_tn(low, gcb)
            for i, d in enumerate((dk, dv)):
                fold = head_select([d[h * SEEN : (h + 1) * SEEN, :] for h in range(heads)], 1)
                dkv_o[cc][k, i, :, :] = fold.astype(BF16)
    for copy in copies[1]:
        copy.wait()
    grad_normed = dot_nn(pack_o[1], wf[1])
    standard, inverse = normalize(first[...])
    grad = grad + norm_backward(standard, inverse, grad_normed, gain[1:2, :].astype(F32))
    stat_o[2:3, :] = jnp.sum(grad_normed * standard, 0, keepdims=True)
    stat_o[3:4, :] = jnp.sum(grad_normed, 0, keepdims=True)
    gf_o[...] = grad
    g1 = grad.astype(BF16)
    pack_o[0, :, :] = g1
    for copy in copies[0]:
        copy.wait()
    gatt = dot_nt(g1, wf[0]).astype(BF16)
    for cc in range(2):
        for k in range(chips):
            b = cc * chips + k
            gt_o[k][cc, :, :] = gatt[:, b * width : (b + 1) * width]


def row_grad_kernel(chips, idx, fwd, fwd2, bwd, bwd2, out, left, right):
    dps, height, cut = out.shape
    width = height // (3 * chips)
    own = fwd.shape[1]
    half = chips * width
    for m, (l, r) in enumerate((((fwd, fwd2), (bwd, bwd2)), ((bwd, bwd2), (fwd, fwd2)), ((fwd, fwd2), (bwd, bwd2)))):
        left[0:own, :] = l[0][m, :, 0:half]
        left[own : 2 * own, :] = l[1][m, :, half : 2 * half]
        right[0:own, :] = r[0][m]
        right[own : 2 * own, :] = r[1][m]
        for q in range(dps):
            part = dot_tn(left[...], right[:, q * cut : (q + 1) * cut]).astype(BF16)
            for k in range(chips):
                row = (3 * k + m) * width
                out[q, row : row + width, :] = part[k * width : (k + 1) * width, :]


def pack_kernel(idx, *refs):
    parts, out = refs[:-1], refs[-1]
    width = parts[0].shape[0] // 3
    for m in range(3):
        for k, part in enumerate(parts):
            row = (m * len(parts) + k) * width
            out[row : row + width, :] = part[m * width : (m + 1) * width, :]


def self_back_kernel(chips, idx, triple, probs, weight, *rest):
    take = iter(rest)
    pull = lambda n: [next(take) for _ in range(n)]
    grads = [pull(chips), pull(chips)]
    (gt_o,) = pull(1)
    bs_o, bo_o = pull(chips), pull(chips)
    gout, key_t, wcat, dk, dv, back = pull(6)
    rows, width = triple.shape[1], triple.shape[2]
    heads = width // HDIM
    own = bs_o[0].shape[0]
    for k in range(chips):
        gout[at(idx[0] ^ (2 * k), own), :] = grads[0][k][0]
        gout[at(idx[0] ^ (2 * k + 1), own), :] = grads[1][k][1]
    for c in range(3):
        wcat[:, c * width : (c + 1) * width] = weight[c]
    count = rows // QB
    for i in range(count):
        here = slice(i * QB, (i + 1) * QB)
        key_t[:, here] = triple[1, here, :].astype(F32).T.astype(BF16)
    for i in reversed(range(count)):
        here = slice(i * QB, (i + 1) * QB)
        seen = (i + 1) * QB
        dq = []
        for h in range(heads):
            go = head_only(gout[here, :], h, heads)
            query = head_only(triple[0, here, :], h, heads)
            dp = dot_nt(triple[2, 0:seen, :], go)
            low = probs[h, 0:seen, here]
            p = low.astype(F32)
            inner = jnp.sum(dp * p, 0, keepdims=True)
            ds = (p * (dp - inner) * SCALE).astype(BF16)
            new_k = dot_nn(ds, query)
            new_v = dot_nn(low, go)
            if i == count - 1 and h == 0:
                dk[0:seen, :] = new_k
                dv[0:seen, :] = new_v
            else:
                dk[0:seen, :] += new_k
                dv[0:seen, :] += new_v
            dq.append(dot_nn(key_t[:, 0:seen], ds))
        gt_o[here, 0:width] = head_select(dq, 0).T.astype(BF16)
        gt_o[here, width : 2 * width] = dk[here, :].astype(BF16)
        gt_o[here, 2 * width : 3 * width] = dv[here, :].astype(BF16)
        back[here, :] = dot_nt(gt_o[here, :], wcat[...]).astype(BF16)
    for k in range(chips):
        bs_o[k][...] = back[at(idx[0] ^ (2 * k), own), :]
        bo_o[k][...] = back[at(idx[0] ^ (2 * k + 1), own), :]


def self_grad_kernel(chips, dps, idx, tok, normed, gt, states, gp, *rest):
    same, other = rest[:chips], rest[chips : 2 * chips]
    out, stat_o = rest[2 * chips :]
    cut = out.shape[2]
    width = gp.shape[2]
    for q in range(dps):
        cols = slice(q * cut, (q + 1) * cut)
        out[q, 0 : 3 * width, :] = dot_tn(gt[...], normed[:, cols]).astype(BF16)
        for c in range(2):
            out[q, (3 + c) * width : (4 + c) * width, :] = dot_tn(
                gp[c], states[:, cols]
            ).astype(BF16)
    own = same[0].shape[0]
    gain = jnp.zeros((1, tok.shape[1]), F32)
    shift = gain
    for k in range(chips):
        for cc, part in enumerate((same[k], other[k])):
            g = part[...].astype(F32)
            standard, _ = normalize(tok[at(idx[0] ^ (2 * k + cc), own), :].astype(F32))
            gain += jnp.sum(g * standard, 0, keepdims=True)
            shift += jnp.sum(g, 0, keepdims=True)
    stat_o[0:1, :] = gain
    stat_o[1:2, :] = shift


def add_kernel(idx, *refs):
    count = len(refs) // 3
    for k in range(count):
        total = refs[k][...].astype(F32) + refs[count + k][...].astype(F32)
        refs[2 * count + k][...] = total.astype(BF16)


def token_kernel(idx, tokens, gain, grad, *rest):
    parts, (out, tok, sem) = rest[:-3], rest[-3:]
    own_rows(idx, tokens, tok, sem).wait()
    grad_normed = parts[0][...].astype(F32)
    for part in parts[1:]:
        grad_normed += part[...].astype(F32)
    standard, inverse = normalize(tok[...].astype(F32))
    out[...] = grad[...] + norm_backward(standard, inverse, grad_normed, gain[0:1, :].astype(F32))


def place_kernel(plan, idx, *refs):
    parts, outs = refs[: -len(plan)], refs[-len(plan) :]
    if len(parts) == 1:
        source = parts[0]
        count, _, cut = source.shape
        take = lambda q, rows: source[q, rows, :]
        where_of = lambda q: slice(q * cut, (q + 1) * cut)
    else:
        count, cut = len(parts), parts[0].shape[1]
        take = lambda q, rows: parts[q][rows, :]
        where_of = lambda q: at(idx[1] ^ q, cut)
    row = 0
    for out, (height, lead, flip) in zip(outs, plan):
        for q in range(count):
            where = where_of(q)
            piece = take(q, slice(row, row + height)).astype(F32)
            if not flip:
                out[:, where] = piece
            elif lead is None:
                out[where, :] = piece.T
            else:
                step = height // lead
                for c in range(lead):
                    out[c, where, :] = piece[c * step : (c + 1) * step, :].T
        row += height


def flip_bits(axis, bits, size):
    return functools.partial(
        lax.ppermute, axis_name=axis, perm=[(i, i ^ bits) for i in range(size)]
    )


def total(*parts):
    out = parts[0].astype(F32)
    for part in parts[1:]:
        out = out + part.astype(F32)
    return out


def body(
    tokens,
    states,
    cotangent,
    self_weight,
    self_output,
    cross_query,
    cross_pair,
    cross_output,
    hidden_weight,
    hidden_bias,
    output_weight,
    output_bias,
    norm_gain,
    norm_shift,
    state_row,
    state_segment,
    caption,
):
    rows, dim = tokens.shape
    width = cross_query.shape[1]
    heads = width // HDIM
    hid = hidden_bias.shape[0]
    cores = lax.axis_size("mp")
    chips = cores // 2
    dps = lax.axis_size("dp")
    own = rows // cores
    cut = dim // dps
    me = lax.axis_index("mp")
    dpi = lax.axis_index("dp")
    idx = jnp.stack([me, dpi, state_row[0], caption[0]]).astype(jnp.int32)
    to_z = [flip_bits("mp", 2 * k, cores) for k in range(chips)]
    to_core = flip_bits("mp", 1, cores)
    to_dp = [flip_bits("dp", q, dps) for q in range(dps)]
    far = range(1, chips)
    peers = range(1, dps)

    def share_dp(piece):
        return lax.all_to_all(jnp.broadcast_to(piece[None], (dps,) + piece.shape), "dp", 0, 0)

    def add_all(left, right, name):
        return list(
            call(
            add_kernel,
            [((own, dim), BF16)] * chips,
            idx,
            *left,
            *right,
            stage=True,
            name=name,
        ))

    def swap_dp(pieces):
        return lax.all_to_all(pieces, "dp", 0, 0)

    def sum_dp(pieces):
        return jnp.sum(pieces.astype(F32), 0).astype(BF16)

    labels = lax.dynamic_index_in_dim(state_segment, state_row[0], 0, False)
    begin = jnp.minimum(jnp.sum((labels < caption[0]).astype(jnp.int32)), labels.shape[0] - SEEN)
    labels = lax.dynamic_slice_in_dim(labels, begin, SEEN, 0)
    seen = jnp.tile((labels == caption[0]).astype(jnp.int32)[None, :], (1, heads))
    near = lax.dynamic_slice(states, (state_row[0], begin, 0), (1, SEEN, dim))[0]

    mine = jnp.concatenate([self_output, cross_query.T, cross_output], 0)
    piece = lax.dynamic_slice_in_dim(mine, dpi * cut, cut, 1)
    got = [to_z[k](piece) for k in far]

    outs = call(
        functools.partial(self_kernel, chips),
        [
            ((rows, dim), BF16),
            ((3, rows, width), BF16),
            ((heads, rows, rows), BF16),
        ]
        + [((2 * own + 2 * SEEN, width), BF16)] * chips,
        idx,
        tokens,
        self_weight,
        norm_gain,
        norm_shift,
        states,
        cross_pair,
        state_segment,
        scratch=[
            pltpu.VMEM((width, rows), BF16),
            pltpu.VMEM((rows, width), BF16),
            pltpu.VMEM((states.shape[1], width), F32),
        ],
        after=(piece,),
        stage=True,
        name="self_fwd",
    )
    normed_one, triple, probs = outs[:3]
    att = outs[3:]
    got = lax.optimization_barrier((*got, att[0]))[:-1]
    (cat,) = call(pack_kernel, [((3 * width * (chips - 1), cut), BF16)], idx, *got, tight=True, name="pack")
    att = [att[0]] + [to_z[k](att[k]) for k in far]
    att2 = [to_core(x) for x in att]

    grad_active = call(
        functools.partial(active_kernel, chips),
        [((2 * own, hid), F32)] * chips,
        idx,
        cotangent,
        output_weight,
        after=att[:1],
        stage=True,
        name="grad_active",
    )

    cats = [cat] + [to_dp[q](cat) for q in peers]
    cats, grad_active, seen = lax.optimization_barrier((cats, grad_active, seen))
    weights = [mine, *cats, to_core(mine), *[to_core(x) for x in cats]]

    sq = cores * width
    first, fwd, q, cp, second, n3 = call(
        functools.partial(cross_kernel, chips, dps),
        [
            ((own, dim), F32),
            ((3, own, dim), BF16),
            ((own, sq), BF16),
            ((cores, own, heads * SEEN), BF16),
            ((own, dim), F32),
            ((own, dim), BF16),
        ],
        idx,
        tokens,
        norm_gain,
        norm_shift,
        seen,
        *weights,
        *att,
        *att2,
        scratch=[
            pltpu.VMEM((3, sq, dim), BF16),
            pltpu.SemaphoreType.DMA((3, 2 * dps + 2)),
            pltpu.VMEM((own, dim), BF16),
            pltpu.SemaphoreType.DMA,
        ],
        raw=(0, *range(4, 4 + len(weights))),
        stage=True,
        name="cross_fwd",
    )

    relay = chips == 4
    order = (0, 1, 3, 2) if relay else range(chips)
    n3s = [n3] + [None if relay and k == 2 else to_z[k](n3) for k in far]
    fwd2 = to_core(fwd)
    bias_row = hidden_bias[None, :]
    acts, ghis, chunks, sent = [None] * chips, [None] * chips, [None] * chips, [None] * chips
    done = ()
    for k in order:
        arrived = n3s[k]
        chunk, act, ghi, bs, bo = call(
            hidden_kernel,
            [
                ((2 * own, dim), BF16),
                ((2 * own, hid), BF16),
                ((2 * own, hid), BF16),
                ((own, dim), BF16),
                ((own, dim), BF16),
            ],
            idx,
            arrived,
            to_core(arrived),
            hidden_weight,
            bias_row,
            grad_active[k],
            scratch=[pltpu.VMEM((2 * own, dim), F32)],
            after=done,
            tight=True,
            name="hidden",
        )
        done = (act,)
        acts[k], ghis[k], chunks[k] = act, ghi, chunk
        sent[k] = total(bs, to_core(bo)).astype(BF16)
        if k == 0:
            *n3s, _ = lax.optimization_barrier((*n3s, act))
            if relay:
                n3s[2] = to_z[1](n3s[3])
    backs = sent[:1] + [to_z[k](sent[k]) for k in range(1, 2 if relay else chips)]
    if relay:
        sent[2] = total(sent[2], to_z[1](sent[3])).astype(BF16)
        backs.append(to_z[2](sent[2]))
    mlp_grad, bias_part = call(
        functools.partial(mlp_grad_kernel, chips),
        [((dps, 2 * hid, cut), BF16), ((1, hid), F32)],
        idx,
        cotangent,
        *acts,
        *ghis,
        *chunks,
        scratch=[
            pltpu.VMEM((rows, hid), BF16),
            pltpu.VMEM((rows, hid), BF16),
            pltpu.VMEM((rows, dim), BF16),
        ],
        after=sent,
        stage=True,
        name="mlp_grad",
    )
    mlp_grad, backs[1] = lax.optimization_barrier((mlp_grad, backs[1]))
    mlp_swap = swap_dp(mlp_grad)
    outs = call(
        functools.partial(mlp_out_kernel, chips),
        [((own, dim), BF16)] * (2 * chips),
        idx,
        output_weight,
        *acts,
        scratch=[pltpu.VMEM((2 * own, dim), F32)],
        after=(mlp_grad,),
        stage=True,
        name="mlp_out",
    )
    *backs, mlp_part = lax.optimization_barrier((*backs, outs))

    outs = call(
        functools.partial(cross_back_kernel, chips, dps, len(backs)),
        [
            ((3, own, dim), BF16),
            ((own, dim), F32),
            ((8, dim), F32),
            ((chips, 2, SEEN, width), BF16),
            ((chips, 2, SEEN, width), BF16),
        ]
        + [((2, own, width), BF16)] * chips,
        idx,
        cotangent,
        norm_gain,
        second,
        first,
        cp,
        q,
        *weights,
        *backs,
        *att,
        *att2,
        scratch=[
            pltpu.VMEM((own, sq), BF16),
            pltpu.VMEM((3, sq, dim), BF16),
            pltpu.SemaphoreType.DMA((3, 2 * dps + 2)),
            pltpu.VMEM((own, dim), BF16),
            pltpu.SemaphoreType.DMA,
        ],
        raw=(0, *range(6, 6 + len(weights))),
        cost=10**12,
        stage=True,
        name="cross_bwd",
    )
    bwd, gf, stat_a, dkv, dkv_other = outs[:5]
    gatt = outs[5:]
    gatt = [gatt[0]] + [to_z[k](gatt[k]) for k in far]

    (row_grad,) = call(
        functools.partial(row_grad_kernel, chips),
        [((dps, chips * 3 * width, cut), BF16)],
        idx,
        fwd,
        fwd2,
        bwd,
        to_core(bwd),
        scratch=[pltpu.VMEM((2 * own, chips * width), BF16), pltpu.VMEM((2 * own, dim), BF16)],
        stage=True,
        name="row_grad",
    )
    gatt, row_grad, mlp_swap, mlp_part = lax.optimization_barrier(
        (gatt, row_grad, mlp_swap, mlp_part)
    )
    gatt2 = [to_core(x) for x in gatt]
    row_swap = swap_dp(row_grad)

    outs = call(
        functools.partial(self_back_kernel, chips),
        [((rows, 3 * width), BF16)] + [((own, dim), BF16)] * (2 * chips),
        idx,
        triple,
        probs,
        self_weight,
        *gatt,
        *gatt2,
        scratch=[
            pltpu.VMEM((rows, width), BF16),
            pltpu.VMEM((width, rows), BF16),
            pltpu.VMEM((dim, 3 * width), BF16),
            pltpu.VMEM((rows, width), F32),
            pltpu.VMEM((rows, width), F32),
            pltpu.VMEM((rows, dim), BF16),
        ],
        stage=True,
        name="self_bwd",
    )
    gt, bs, bo = outs[0], outs[1 : 1 + chips], outs[1 + chips :]
    bos = [to_core(x) for x in bo]

    dkv = total(dkv, to_core(dkv_other)).astype(BF16)
    gp = total(dkv[0], *[to_z[k](dkv[k]) for k in far]).astype(BF16)

    self_part, stat_b = call(
        functools.partial(self_grad_kernel, chips, dps),
        [((dps, 5 * width, cut), BF16), ((8, dim), F32)],
        idx,
        tokens,
        normed_one,
        gt,
        near,
        gp,
        *bs,
        *bo,
        stage=True,
        name="self_grad",
    )
    *bos, self_part = lax.optimization_barrier((*bos, self_part))
    sent = add_all(bs, bos, "self_add")
    parts = sent[:1] + [to_z[k](sent[k]) for k in far]
    row_swap, self_part, mlp_swap, _ = lax.optimization_barrier(
        (row_swap, self_part, mlp_swap, sent[0])
    )
    self_swap = swap_dp(self_part)
    mlp_piece = sum_dp(mlp_swap)
    early = [to_dp[q](mlp_piece) for q in (1, 2)]
    parts, self_swap, early, stat_b = lax.optimization_barrier((parts, self_swap, early, stat_b))
    mlp_all = [mlp_piece, *early] + [to_dp[q](mlp_piece) for q in range(3, dps)]
    (grad_tokens,) = call(
        token_kernel,
        [((own, dim), F32)],
        idx,
        tokens,
        norm_gain,
        gf,
        *parts,
        scratch=[pltpu.VMEM((own, dim), BF16), pltpu.SemaphoreType.DMA],
        raw=(0,),
        stage=True,
        name="tokens",
    )
    state_part = jnp.einsum("cse,cde->sd", gp, cross_pair, preferred_element_type=F32)
    state_part = state_part.astype(BF16)
    state_part = total(state_part, to_core(state_part)).astype(BF16)
    state_grad = total(state_part, *[to_z[k](state_part) for k in far])
    grad_states = lax.dynamic_update_slice(
        jnp.zeros(states.shape, F32), state_grad[None], (state_row[0], begin, 0)
    )
    row_piece = sum_dp(row_swap).reshape(chips, 3 * width, cut)
    row_piece = total(row_piece[0], *[to_z[k](row_piece[k]) for k in far]).astype(BF16)
    self_piece = sum_dp(self_swap)
    slots = lax.dynamic_update_slice(jnp.zeros((cores, hid), F32), bias_part, (me, 0))
    stats = jnp.concatenate([stat_b[:2], stat_a[:5], slots.reshape(-1, dim)], 0)
    def all_sum(value, axis, size):
        bits = 1
        while bits < size:
            value = value + flip_bits(axis, bits, size)(value)
            bits *= 2
        return value

    stats = all_sum(stats, "dp", dps)

    def place(pieces, plan, shapes, name):
        return call(
            functools.partial(place_kernel, plan),
            [(s, F32) for s in shapes],
            idx,
            *pieces,
            stage=True,
            name=name,
        )

    piece = jnp.concatenate([row_piece, self_piece], 0)
    piece, grad_tokens, stats = lax.optimization_barrier((piece, grad_tokens, stats))
    swapped = share_dp(piece)
    mlp_part = lax.optimization_barrier((mlp_part, grad_tokens))[0]
    mlp_sent = add_all(mlp_part[::2], [to_core(x) for x in mlp_part[1::2]], "out_add")
    mlp_parts = mlp_sent[:1] + [to_z[k](mlp_sent[k]) for k in far]
    block_output = (second + total(*mlp_parts) + output_bias.astype(F32)).astype(BF16)

    grad_output_weight, grad_hidden_weight = place(
        mlp_all, ((hid, None, False), (hid, None, True)), ((hid, dim), (dim, hid)), "place_mlp"
    )
    swapped, block_output, grad_output_weight = lax.optimization_barrier(
        (swapped, block_output, grad_output_weight)
    )
    (
        grad_self_output,
        grad_cross_query,
        grad_cross_output,
        grad_self_weight,
        grad_cross_pair,
    ) = place(
        [swapped],
        (
            (width, None, False),
            (width, None, True),
            (width, None, False),
            (3 * width, 3, True),
            (2 * width, 2, True),
        ),
        (
            (width, dim),
            (dim, width),
            (width, dim),
            (3, dim, width),
            (2, dim, width),
        ),
        "place",
    )
    stats = all_sum(stats, "mp", cores)
    grad_norm_gain = jnp.stack([stats[0], stats[4], stats[2]])
    grad_norm_shift = jnp.stack([stats[1], stats[5], stats[3]])
    grad_output_bias = stats[6]
    grad_hidden_bias = lax.dynamic_index_in_dim(stats[7:].reshape(cores, hid), me, 0, False)
    return (
        block_output,
        grad_tokens,
        grad_states,
        grad_self_weight,
        grad_self_output,
        grad_cross_query,
        grad_cross_pair,
        grad_cross_output,
        grad_hidden_weight,
        grad_hidden_bias,
        grad_output_weight,
        grad_output_bias,
        grad_norm_gain,
        grad_norm_shift,
    )


def solution(mesh):
    placed = (
        P("dp", None),
        P("dp", None, None),
        P("dp", None),
        P(None, None, "mp"),
        P("mp", None),
        P(None, "mp"),
        P(None, None, "mp"),
        P("mp", None),
        P(None, "mp"),
        P("mp"),
        P("mp", None),
        P(),
        P(),
        P(),
        P("dp"),
        P("dp", None),
        P("dp"),
    )
    return jax.shard_map(
        body,
        mesh=mesh,
        in_specs=placed,
        out_specs=(
            P(("dp", "mp"), None),
            P(("dp", "mp"), None),
            P("dp", None, None),
            P(None, None, "mp"),
            P("mp", None),
            P(None, "mp"),
            P(None, None, "mp"),
            P("mp", None),
            P(None, "mp"),
            P("mp"),
            P("mp", None),
            P(),
            P(),
            P(),
        ),
        check_vma=False,
    )
```

```python
import functools
import math

import jax
import jax.numpy as jnp
from jax import lax
from jax.experimental import pallas as pl
from jax.experimental.pallas import tpu as pltpu
from jax.sharding import PartitionSpec as P

HDIM = 64
SEEN = 64
QB = 256
PAD = 16
EPSILON = 1e-05
NEG_FILL = -1e30
SCALE = HDIM ** (-0.5)
F32 = jnp.float32
BF16 = jnp.bfloat16


def dot_nn(a, b):
    return lax.dot_general(a, b, (((1,), (0,)), ((), ())), preferred_element_type=F32)


def dot_nt(a, b):
    return lax.dot_general(a, b, (((1,), (1,)), ((), ())), preferred_element_type=F32)


def dot_tn(a, b):
    return lax.dot_general(a, b, (((0,), (0,)), ((), ())), preferred_element_type=F32)


def normalize(resid):
    center = resid - jnp.mean(resid, -1, keepdims=True)
    inverse = lax.rsqrt(jnp.mean(center * center, -1, keepdims=True) + EPSILON)
    return (center * inverse, inverse)


def norm_backward(standard, inverse, grad_normed, gain):
    scaled = grad_normed * gain
    return inverse * (
        scaled
        - jnp.mean(scaled, -1, keepdims=True)
        - standard * jnp.mean(scaled * standard, -1, keepdims=True)
    )


def at(index, size):
    return pl.ds(pl.multiple_of(index * size, size), size)


def staged(kernel, ins, outs, extra, *refs):
    count_in, count_out = len(ins), len(outs)
    idx, refs = refs[0], list(refs[1:])
    inner = refs[: count_in + count_out]
    own = refs[count_in + count_out : count_in + count_out + extra]
    rest = refs[count_in + count_out + extra :]
    sem_in, sem_out = rest[-2:]
    held = iter(rest[:-2])
    started, results = [], []
    for i, here in enumerate(ins):
        if here:
            local = next(held)
            started.append(pltpu.make_async_copy(inner[i], local, sem_in.at[len(started)]))
            inner[i] = local
    for i, here in enumerate(outs):
        if here:
            local = next(held)
            target = inner[count_in + i]
            results.append(pltpu.make_async_copy(local, target, sem_out.at[len(results)]))
            inner[count_in + i] = local
    for copy in started:
        copy.start()
    for copy in started:
        copy.wait()
    kernel(idx, *inner, *own)
    for copy in results:
        copy.start()
    for copy in results:
        copy.wait()


def call(
    kernel, outs, idx, *args, scratch=(), after=(), stage=False, tight=False, raw=(), cost=1, name=None, spill=8
):
    if after:
        idx = lax.optimization_barrier((idx, *after))[0]
    out_shape = [jax.ShapeDtypeStruct(s, t) for s, t in outs]
    big = lambda a: bool(stage) and a.size >= 1 << 15
    ins_far = [big(a) and i not in raw for i, a in enumerate(args)]
    outs_far = [big(a) for a in out_shape]
    vmem = pl.BlockSpec(memory_space=pltpu.VMEM)
    hbm = pl.BlockSpec(memory_space=pltpu.HBM)
    held = spill << 20
    for i, a in enumerate((*args, *out_shape)):
        if i not in raw:
            held += a.size * a.dtype.itemsize
    for a in scratch:
        if len(getattr(a, "shape", ())) > 1 and a.dtype in (F32, BF16):
            held += math.prod(a.shape) * jnp.dtype(a.dtype).itemsize
    scratch = list(scratch)
    if any(ins_far) or any(outs_far):
        kernel = functools.partial(staged, kernel, ins_far, outs_far, len(scratch))
        for a, far in zip((*args, *out_shape), ins_far + outs_far):
            if far:
                scratch.append(pltpu.VMEM(a.shape, a.dtype))
        scratch.append(pltpu.SemaphoreType.DMA((max(1, sum(ins_far)),)))
        scratch.append(pltpu.SemaphoreType.DMA((max(1, sum(outs_far)),)))
    return pl.pallas_call(
        kernel,
        out_shape=out_shape,
        in_specs=[pl.BlockSpec(memory_space=pltpu.SMEM)]
        + [hbm if far or i in raw else vmem for i, far in enumerate(ins_far)],
        out_specs=[hbm if far else vmem for far in outs_far],
        scratch_shapes=scratch,
        cost_estimate=pl.CostEstimate(flops=cost, bytes_accessed=1, transcendentals=0),
        compiler_params=pltpu.CompilerParams(
            vmem_limit_bytes=min(held, 60 << 20) if tight else 60 << 20
        ),
        name=name,
    )(idx, *args)


def head_select(parts, axis):
    if len(parts) == 1:
        return parts[0]
    head = lax.broadcasted_iota(jnp.int32, parts[0].shape, axis) // HDIM
    return jnp.where(head == 0, parts[0], parts[1])


def head_only(value, h, count):
    if count == 1:
        return value
    head = lax.broadcasted_iota(jnp.int32, value.shape, 1) // HDIM
    return jnp.where(head == h, value, jnp.zeros_like(value))


def self_kernel(
    chips, idx, tok, weight, gain, shift, states, pair, segment, normed, triple, probs, *rest
):
    att_out = rest[:chips]
    val_t, att, kv = rest[chips:]
    rows, width = tok.shape[0], weight.shape[2]
    heads = width // HDIM
    g = gain[0:1, :].astype(F32)
    s = shift[0:1, :].astype(F32)
    for i in range(rows // QB):
        here = slice(i * QB, (i + 1) * QB)
        standard, _ = normalize(tok[here, :].astype(F32))
        n = (standard * g + s).astype(BF16)
        normed[here, :] = n
        query = dot_nn(n, weight[0]).astype(BF16)
        triple[0, here, :] = query
        triple[1, here, :] = dot_nn(n, weight[1]).astype(BF16)
        value = dot_nn(n, weight[2])
        triple[2, here, :] = value.astype(BF16)
        val_t[:, here] = value.T.astype(BF16)
        seen = (i + 1) * QB
        outs = []
        for h in range(heads):
            scores = dot_nt(triple[1, 0:seen, :], head_only(query, h, heads)) * SCALE
            key_at = lax.broadcasted_iota(jnp.int32, scores.shape, 0)
            row_at = lax.broadcasted_iota(jnp.int32, scores.shape, 1) + i * QB
            scores = jnp.where(key_at <= row_at, scores, NEG_FILL)
            e = jnp.exp(scores - jnp.max(scores, 0, keepdims=True))
            p = (e * (1.0 / jnp.sum(e, 0, keepdims=True))).astype(BF16)
            probs[h, 0:seen, here] = p
            outs.append(dot_nn(val_t[:, 0:seen], p))
        att[here, :] = head_select(outs, 0).T.astype(BF16)
    own = (att_out[0].shape[0] - 2 * SEEN) // 2
    before = segment[pl.ds(idx[2], 1), :] < idx[3]
    begin = jnp.minimum(jnp.sum(before.astype(jnp.int32)), states.shape[1] - SEEN)
    for c in range(2):
        kv[...] = dot_nn(states[idx[2]], pair[c])
        for k in range(chips):
            where = slice(2 * own + c * SEEN, 2 * own + (c + 1) * SEEN)
            att_out[k][where, :] = kv[pl.ds(begin, SEEN), :].astype(BF16)
    for k in range(chips):
        for cc in range(2):
            att_out[k][cc * own : (cc + 1) * own, :] = att[at(idx[0] ^ (2 * k + cc), own), :]


def pair_tiles(block, heads):
    return jnp.concatenate([head_only(block, h, heads) for h in range(heads)], 0)


def half_reduce(op, value, heads, fill):
    if heads == 1:
        return op(value, -1, keepdims=True)
    half = lax.broadcasted_iota(jnp.int32, value.shape, 1) // SEEN
    first = op(jnp.where(half == 0, value, fill), -1, keepdims=True)
    other = op(jnp.where(half == 1, value, fill), -1, keepdims=True)
    return jnp.where(half == 0, first, other)


def fetch_weights(chips, dps, idx, weights, wf, sem):
    width = wf.shape[1] // (2 * chips)
    cut = wf.shape[2] // dps
    span = (chips - 1) * width
    half = chips * width
    lists = []
    for m in range(3):
        copies = []
        for cc in range(2):
            source = weights[cc * (dps + 1)]
            where = wf.at[m, cc * half : cc * half + width, :]
            copies.append((source.at[m * width : (m + 1) * width, :], where))
            for q in range(dps):
                source = weights[cc * (dps + 1) + 1 + q]
                cols = at(idx[1] ^ q, cut)
                where = wf.at[m, cc * half + width : (cc + 1) * half, cols]
                copies.append((source.at[m * span : (m + 1) * span, :], where))
        lists.append(
            [pltpu.make_async_copy(s, d, sem.at[m, i]) for i, (s, d) in enumerate(copies)]
        )
    return lists


def own_rows(idx, source, rows, sem):
    copy = pltpu.make_async_copy(source.at[at(idx[0], rows.shape[0]), :], rows, sem)
    copy.start()
    return copy


def cross_kernel(chips, dps, idx, tokens, gain, shift, seen, *rest):
    take = iter(rest)
    pull = lambda n: [next(take) for _ in range(n)]
    weights = pull(2 * dps + 2)
    att_in = [pull(chips), pull(chips)]
    first_o, pack_o, q_o, cp_o, second_o, n3_o = pull(6)
    wf, sem, tok, tok_sem = pull(4)
    fetch = own_rows(idx, tokens, tok, tok_sem)
    own, dim = tok.shape
    width = wf.shape[1] // (2 * chips)
    heads = width // HDIM
    half = chips * width
    copies = fetch_weights(chips, dps, idx, weights, wf, sem)
    for each in copies:
        for copy in each:
            copy.start()
    for k in range(chips):
        pack_o[0, :, k * width : (k + 1) * width] = att_in[0][k][0:own, :]
        pack_o[0, :, half + k * width : half + (k + 1) * width] = att_in[1][k][own : 2 * own, :]
    fetch.wait()
    for copy in copies[0]:
        copy.wait()
    resid = tok[...].astype(F32) + dot_nn(pack_o[0], wf[0])
    first_o[...] = resid
    n2 = (normalize(resid)[0] * gain[1:2, :].astype(F32) + shift[1:2, :].astype(F32)).astype(BF16)
    pack_o[1, :, :] = n2
    for copy in copies[1]:
        copy.wait()
    q_o[...] = dot_nt(n2, wf[1]).astype(BF16)
    allowed = seen[...] > 0
    for cc in range(2):
        for k in range(chips):
            b = cc * chips + k
            lanes = slice(b * width, (b + 1) * width)
            keys = pair_tiles(att_in[cc][k][2 * own : 2 * own + SEEN, :], heads)
            values = pair_tiles(att_in[cc][k][2 * own + SEEN :, :], heads)
            scores = dot_nt(q_o[:, lanes], keys) * SCALE
            scores = jnp.where(allowed, scores, NEG_FILL)
            e = jnp.exp(scores - half_reduce(jnp.max, scores, heads, NEG_FILL))
            p = (e * (1.0 / half_reduce(jnp.sum, e, heads, 0.0))).astype(BF16)
            cp_o[b] = p
            pack_o[2, :, lanes] = dot_nn(p, values).astype(BF16)
    for copy in copies[2]:
        copy.wait()
    resid = resid + dot_nn(pack_o[2], wf[2])
    second_o[...] = resid
    n3 = normalize(resid)[0] * gain[2:3, :].astype(F32) + shift[2:3, :].astype(F32)
    n3_o[...] = n3.astype(BF16)


def active_kernel(chips, idx, cot, weight, *outs):
    rows = outs[0].shape[0]
    for k in range(chips):
        outs[k][...] = dot_nt(cot[at((idx[0] // 2) ^ k, rows), :], weight[...])


def hidden_kernel(idx, same, other, weight, bias, grad_active, n3_o, act_o, ghi_o, bs_o, bo_o, back):
    own = same.shape[0]
    core = lax.rem(idx[0], 2)
    n3_o[at(core, own), :] = same[...]
    n3_o[at(1 - core, own), :] = other[...]
    v = dot_nn(n3_o[...], weight[...]) + bias[...].astype(F32)
    root = 0.7978845608028654
    square = v * v
    t = jnp.tanh(root * v * (1.0 + 0.044715 * square))
    act_o[...] = (0.5 * v * (1.0 + t)).astype(BF16)
    slope = 0.5 * (1.0 + t) + 0.5 * v * (1.0 - t * t) * (root * (1.0 + 0.134145 * square))
    ghi = (grad_active[...] * slope).astype(BF16)
    ghi_o[...] = ghi
    back[...] = dot_nt(ghi, weight[...])
    bs_o[...] = back[at(core, own), :].astype(BF16)
    dim = back.shape[1]
    bo_o[:, 0:dim] = back[at(1 - core, own), :].astype(BF16)
    bo_o[:, dim:] = act_o[at(1 - core, own), :]


def mlp_out_kernel(chips, idx, weight, weight2, *rest):
    acts, others, outs = rest[:chips], rest[chips : 2 * chips], rest[2 * chips :]
    hid = weight.shape[0]
    own = outs[0].shape[0]
    core = lax.rem(idx[0], 2)
    for k in range(chips):
        part = dot_nn(acts[k][at(core, own), :], weight[...])
        part += dot_nn(others[k][:, -hid:], weight2[...])
        outs[k][...] = part.astype(BF16)


def mlp_grad_kernel(chips, idx, cot, *rest):
    acts = rest[:chips]
    ghis = rest[chips : 2 * chips]
    n3s = rest[2 * chips : 3 * chips]
    out, act, ghi, n3 = rest[3 * chips :]
    step = acts[0].shape[0]
    hid = acts[0].shape[1]
    dps, _, cut = out.shape
    total = jnp.zeros((1, hid), F32)
    for k in range(chips):
        rows = at((idx[0] // 2) ^ k, step)
        act[rows, :] = acts[k][...]
        ghi[rows, :] = ghis[k][...]
        n3[rows, :] = n3s[k][...]
        total += jnp.sum(ghis[k][...].astype(F32), 0, keepdims=True)
    row = lax.broadcasted_iota(jnp.int32, (PAD, cut), 0)
    bias = jnp.zeros((PAD, cut), F32)
    for j in range(hid // cut):
        bias = jnp.where(row == j, total[:, j * cut : (j + 1) * cut], bias)
    for q in range(dps):
        cols = slice(q * cut, (q + 1) * cut)
        out[q, 0:hid, :] = dot_tn(act[...], cot[:, cols]).astype(BF16)
        out[q, hid : 2 * hid, :] = dot_tn(ghi[...], n3[:, cols]).astype(BF16)
        out[q, 2 * hid : 2 * hid + PAD, :] = bias.astype(BF16)


def cross_back_kernel(chips, dps, count, idx, cotangent, gain, second, first, cp, q, *rest):
    take = iter(rest)
    pull = lambda n: [next(take) for _ in range(n)]
    weights = pull(2 * dps + 2)
    parts = pull(count)
    kv = [pull(chips), pull(chips)]
    pack_o, gf_o, stat_o, same_o, other_o = pull(5)
    gt_o = pull(chips)
    gc, wf, sem, cot, cot_sem = pull(5)
    fetch = own_rows(idx, cotangent, cot, cot_sem)
    copies = fetch_weights(chips, dps, idx, weights, wf, sem)
    for each in reversed(copies):
        for copy in each:
            copy.start()
    dkv_o = (same_o, other_o)
    own = cot.shape[0]
    width = kv[0][0].shape[1]
    heads = width // HDIM
    grad_normed = parts[0][...].astype(F32)
    for part in parts[1:]:
        grad_normed += part[...].astype(F32)
    fetch.wait()
    c = cot[...].astype(F32)
    standard, inverse = normalize(second[...])
    grad = c + norm_backward(standard, inverse, grad_normed, gain[2:3, :].astype(F32))
    stat_o[0:1, :] = jnp.sum(grad_normed * standard, 0, keepdims=True)
    stat_o[1:2, :] = jnp.sum(grad_normed, 0, keepdims=True)
    stat_o[4:5, :] = jnp.sum(c, 0, keepdims=True)
    g2 = grad.astype(BF16)
    pack_o[2, :, :] = g2
    for copy in copies[2]:
        copy.wait()
    gc[...] = dot_nt(g2, wf[2]).astype(BF16)
    for cc in range(2):
        for k in range(chips):
            b = cc * chips + k
            lanes = slice(b * width, (b + 1) * width)
            keys = pair_tiles(kv[cc][k][2 * own : 2 * own + SEEN, :], heads)
            values = pair_tiles(kv[cc][k][2 * own + SEEN :, :], heads)
            gcb = gc[:, lanes]
            dp = dot_nt(gcb, values)
            low = cp[b]
            p = low.astype(F32)
            inner = half_reduce(jnp.sum, dp * p, heads, 0.0)
            ds = (p * (dp - inner) * SCALE).astype(BF16)
            pack_o[1, :, lanes] = dot_nn(ds, keys).astype(BF16)
            dk = dot_tn(ds, q[:, lanes])
            dv = dot_tn(low, gcb)
            for i, d in enumerate((dk, dv)):
                fold = head_select([d[h * SEEN : (h + 1) * SEEN, :] for h in range(heads)], 1)
                dkv_o[cc][k, i, :, :] = fold.astype(BF16)
    for copy in copies[1]:
        copy.wait()
    grad_normed = dot_nn(pack_o[1], wf[1])
    standard, inverse = normalize(first[...])
    grad = grad + norm_backward(standard, inverse, grad_normed, gain[1:2, :].astype(F32))
    stat_o[2:3, :] = jnp.sum(grad_normed * standard, 0, keepdims=True)
    stat_o[3:4, :] = jnp.sum(grad_normed, 0, keepdims=True)
    gf_o[...] = grad
    g1 = grad.astype(BF16)
    pack_o[0, :, :] = g1
    for copy in copies[0]:
        copy.wait()
    gatt = dot_nt(g1, wf[0]).astype(BF16)
    for cc in range(2):
        for k in range(chips):
            b = cc * chips + k
            gt_o[k][cc, :, :] = gatt[:, b * width : (b + 1) * width]


def row_grad_kernel(chips, idx, fwd, fwd2, bwd, bwd2, out, left, right):
    dps, height, cut = out.shape
    width = height // (3 * chips)
    own = fwd.shape[1]
    half = chips * width
    for m, (l, r) in enumerate((((fwd, fwd2), (bwd, bwd2)), ((bwd, bwd2), (fwd, fwd2)), ((fwd, fwd2), (bwd, bwd2)))):
        left[0:own, :] = l[0][m, :, 0:half]
        left[own : 2 * own, :] = l[1][m, :, half : 2 * half]
        right[0:own, :] = r[0][m]
        right[own : 2 * own, :] = r[1][m]
        for q in range(dps):
            part = dot_tn(left[...], right[:, q * cut : (q + 1) * cut]).astype(BF16)
            for k in range(chips):
                row = (3 * k + m) * width
                out[q, row : row + width, :] = part[k * width : (k + 1) * width, :]


def pack_kernel(idx, *refs):
    parts, out = refs[:-1], refs[-1]
    width = parts[0].shape[0] // 3
    for m in range(3):
        for k, part in enumerate(parts):
            row = (m * len(parts) + k) * width
            out[row : row + width, :] = part[m * width : (m + 1) * width, :]


def self_back_kernel(chips, idx, triple, probs, weight, *rest):
    take = iter(rest)
    pull = lambda n: [next(take) for _ in range(n)]
    grads = [pull(chips), pull(chips)]
    (gt_o,) = pull(1)
    bs_o, bo_o = pull(chips), pull(chips)
    gout, key_t, wcat, dk, dv, back = pull(6)
    rows, width = triple.shape[1], triple.shape[2]
    heads = width // HDIM
    own = bs_o[0].shape[0]
    for k in range(chips):
        gout[at(idx[0] ^ (2 * k), own), :] = grads[0][k][0]
        gout[at(idx[0] ^ (2 * k + 1), own), :] = grads[1][k][1]
    for c in range(3):
        wcat[:, c * width : (c + 1) * width] = weight[c]
    count = rows // QB
    for i in range(count):
        here = slice(i * QB, (i + 1) * QB)
        key_t[:, here] = triple[1, here, :].astype(F32).T.astype(BF16)
    for i in reversed(range(count)):
        here = slice(i * QB, (i + 1) * QB)
        seen = (i + 1) * QB
        dq = []
        for h in range(heads):
            go = head_only(gout[here, :], h, heads)
            query = head_only(triple[0, here, :], h, heads)
            dp = dot_nt(triple[2, 0:seen, :], go)
            low = probs[h, 0:seen, here]
            p = low.astype(F32)
            inner = jnp.sum(dp * p, 0, keepdims=True)
            ds = (p * (dp - inner) * SCALE).astype(BF16)
            new_k = dot_nn(ds, query)
            new_v = dot_nn(low, go)
            if i == count - 1 and h == 0:
                dk[0:seen, :] = new_k
                dv[0:seen, :] = new_v
            else:
                dk[0:seen, :] += new_k
                dv[0:seen, :] += new_v
            dq.append(dot_nn(key_t[:, 0:seen], ds))
        gt_o[here, 0:width] = head_select(dq, 0).T.astype(BF16)
        gt_o[here, width : 2 * width] = dk[here, :].astype(BF16)
        gt_o[here, 2 * width : 3 * width] = dv[here, :].astype(BF16)
        back[here, :] = dot_nt(gt_o[here, :], wcat[...]).astype(BF16)
    for k in range(chips):
        bs_o[k][...] = back[at(idx[0] ^ (2 * k), own), :]
        bo_o[k][...] = back[at(idx[0] ^ (2 * k + 1), own), :]


def self_grad_kernel(chips, dps, idx, tok, normed, gt, states, gp, stat, *rest):
    same, other, out = rest[:chips], rest[chips : 2 * chips], rest[2 * chips]
    cut = out.shape[2]
    width = gp.shape[2]
    for q in range(dps):
        cols = slice(q * cut, (q + 1) * cut)
        out[q, 0 : 3 * width, :] = dot_tn(gt[...], normed[:, cols]).astype(BF16)
        for c in range(2):
            out[q, (3 + c) * width : (4 + c) * width, :] = dot_tn(
                gp[c], states[:, cols]
            ).astype(BF16)
    own = same[0].shape[0]
    gain = jnp.zeros((1, tok.shape[1]), F32)
    shift = gain
    for k in range(chips):
        for cc, part in enumerate((same[k], other[k])):
            g = part[...].astype(F32)
            standard, _ = normalize(tok[at(idx[0] ^ (2 * k + cc), own), :].astype(F32))
            gain += jnp.sum(g * standard, 0, keepdims=True)
            shift += jnp.sum(g, 0, keepdims=True)
    row = lax.broadcasted_iota(jnp.int32, (PAD, tok.shape[1]), 0)
    both = jnp.where(row == 0, gain, jnp.where(row == 1, shift, 0.0))
    for i in range(5):
        both = jnp.where(row == i + 2, stat[i : i + 1, :], both)
    both = both.astype(BF16)
    for q in range(dps):
        for c in range(dps):
            here = slice(5 * width + c * PAD, 5 * width + (c + 1) * PAD)
            out[q, here, :] = both[:, c * cut : (c + 1) * cut]


def add_kernel(idx, *refs):
    count = len(refs) // 3
    for k in range(count):
        total = refs[k][...].astype(F32) + refs[count + k][...].astype(F32)
        refs[2 * count + k][...] = total.astype(BF16)


def token_kernel(idx, tokens, gain, grad, *rest):
    parts, (out, tok, sem) = rest[:-3], rest[-3:]
    own_rows(idx, tokens, tok, sem).wait()
    grad_normed = parts[0][...].astype(F32)
    for part in parts[1:]:
        grad_normed += part[...].astype(F32)
    standard, inverse = normalize(tok[...].astype(F32))
    out[...] = grad[...] + norm_backward(standard, inverse, grad_normed, gain[0:1, :].astype(F32))


def place_kernel(plan, idx, *refs):
    parts, outs = refs[: -len(plan)], refs[-len(plan) :]
    if len(parts) == 1:
        source = parts[0]
        count, _, cut = source.shape
        take = lambda q, rows: source[q, rows, :]
        where_of = lambda q: slice(q * cut, (q + 1) * cut)
    else:
        count, cut = len(parts), parts[0].shape[1]
        take = lambda q, rows: parts[q][rows, :]
        where_of = lambda q: at(idx[1] ^ q, cut)
    row = 0
    for out, (height, lead, flip) in zip(outs, plan):
        for q in range(count):
            where = where_of(q)
            piece = take(q, slice(row, row + height)).astype(F32)
            if not flip:
                out[:, where] = piece
            elif lead is None:
                out[where, :] = piece.T
            else:
                step = height // lead
                for c in range(lead):
                    out[c, where, :] = piece[c * step : (c + 1) * step, :].T
        row += height


def flip_bits(axis, bits, size):
    return functools.partial(
        lax.ppermute, axis_name=axis, perm=[(i, i ^ bits) for i in range(size)]
    )


def total(*parts):
    out = parts[0].astype(F32)
    for part in parts[1:]:
        out = out + part.astype(F32)
    return out


def body(
    tokens,
    states,
    cotangent,
    self_weight,
    self_output,
    cross_query,
    cross_pair,
    cross_output,
    hidden_weight,
    hidden_bias,
    output_weight,
    output_bias,
    norm_gain,
    norm_shift,
    state_row,
    state_segment,
    caption,
):
    rows, dim = tokens.shape
    width = cross_query.shape[1]
    heads = width // HDIM
    hid = hidden_bias.shape[0]
    cores = lax.axis_size("mp")
    chips = cores // 2
    dps = lax.axis_size("dp")
    own = rows // cores
    cut = dim // dps
    me = lax.axis_index("mp")
    dpi = lax.axis_index("dp")
    idx = jnp.stack([me, dpi, state_row[0], caption[0]]).astype(jnp.int32)
    to_z = [flip_bits("mp", 2 * k, cores) for k in range(chips)]
    to_core = flip_bits("mp", 1, cores)
    to_dp = [flip_bits("dp", q, dps) for q in range(dps)]
    far = range(1, chips)
    peers = range(1, dps)

    def share_dp(piece):
        return lax.all_to_all(jnp.broadcast_to(piece[None], (dps,) + piece.shape), "dp", 0, 0)

    def add_all(left, right, name):
        return list(
            call(
            add_kernel,
            [((own, dim), BF16)] * chips,
            idx,
            *left,
            *right,
            stage=True,
            name=name,
        ))

    def swap_dp(pieces):
        return lax.all_to_all(pieces, "dp", 0, 0)

    def sum_dp(pieces):
        return jnp.sum(pieces.astype(F32), 0).astype(BF16)

    labels = lax.dynamic_index_in_dim(state_segment, state_row[0], 0, False)
    begin = jnp.minimum(jnp.sum((labels < caption[0]).astype(jnp.int32)), labels.shape[0] - SEEN)
    labels = lax.dynamic_slice_in_dim(labels, begin, SEEN, 0)
    seen = jnp.tile((labels == caption[0]).astype(jnp.int32)[None, :], (1, heads))
    near = lax.dynamic_slice(states, (state_row[0], begin, 0), (1, SEEN, dim))[0]

    mine = jnp.concatenate([self_output, cross_query.T, cross_output], 0)
    piece = lax.dynamic_slice_in_dim(mine, dpi * cut, cut, 1)
    got = [to_z[k](piece) for k in far]
    output_weight2 = to_core(output_weight)

    outs = call(
        functools.partial(self_kernel, chips),
        [
            ((rows, dim), BF16),
            ((3, rows, width), BF16),
            ((heads, rows, rows), BF16),
        ]
        + [((2 * own + 2 * SEEN, width), BF16)] * chips,
        idx,
        tokens,
        self_weight,
        norm_gain,
        norm_shift,
        states,
        cross_pair,
        state_segment,
        scratch=[
            pltpu.VMEM((width, rows), BF16),
            pltpu.VMEM((rows, width), BF16),
            pltpu.VMEM((states.shape[1], width), F32),
        ],
        after=(piece,),
        stage=True,
        name="self_fwd",
    )
    normed_one, triple, probs = outs[:3]
    att = outs[3:]
    *got, output_weight2, _ = lax.optimization_barrier((*got, output_weight2, att[0]))
    (cat,) = call(pack_kernel, [((3 * width * (chips - 1), cut), BF16)], idx, *got, tight=True, name="pack")
    att = [att[0]] + [to_z[k](att[k]) for k in far]
    att2 = [to_core(x) for x in att]

    grad_active = call(
        functools.partial(active_kernel, chips),
        [((2 * own, hid), F32)] * chips,
        idx,
        cotangent,
        output_weight,
        after=att[:1],
        stage=True,
        name="grad_active",
    )

    cats = [cat] + [to_dp[q](cat) for q in peers]
    cats, grad_active, seen = lax.optimization_barrier((cats, grad_active, seen))
    weights = [mine, *cats, to_core(mine), *[to_core(x) for x in cats]]

    sq = cores * width
    first, fwd, q, cp, second, n3 = call(
        functools.partial(cross_kernel, chips, dps),
        [
            ((own, dim), F32),
            ((3, own, dim), BF16),
            ((own, sq), BF16),
            ((cores, own, heads * SEEN), BF16),
            ((own, dim), F32),
            ((own, dim), BF16),
        ],
        idx,
        tokens,
        norm_gain,
        norm_shift,
        seen,
        *weights,
        *att,
        *att2,
        scratch=[
            pltpu.VMEM((3, sq, dim), BF16),
            pltpu.SemaphoreType.DMA((3, 2 * dps + 2)),
            pltpu.VMEM((own, dim), BF16),
            pltpu.SemaphoreType.DMA,
        ],
        raw=(0, *range(4, 4 + len(weights))),
        stage=True,
        name="cross_fwd",
    )

    relay = chips == 4
    order = (0, 1, 3, 2) if relay else range(chips)
    n3s = [n3] + [None if relay and k == 2 else to_z[k](n3) for k in far]
    fwd2 = to_core(fwd)
    bias_row = hidden_bias[None, :]
    acts, ghis, chunks, sent, others = ([None] * chips for _ in range(5))
    done = ()
    for k in order:
        arrived = n3s[k]
        chunk, act, ghi, bs, bo = call(
            hidden_kernel,
            [
                ((2 * own, dim), BF16),
                ((2 * own, hid), BF16),
                ((2 * own, hid), BF16),
                ((own, dim), BF16),
                ((own, dim + hid), BF16),
            ],
            idx,
            arrived,
            to_core(arrived),
            hidden_weight,
            bias_row,
            grad_active[k],
            scratch=[pltpu.VMEM((2 * own, dim), F32)],
            after=done,
            tight=True,
            name="hidden",
        )
        done = (act,)
        acts[k], ghis[k], chunks[k] = act, ghi, chunk
        others[k] = to_core(bo)
        sent[k] = total(bs, others[k][:, :dim]).astype(BF16)
        if k == 0:
            *n3s, _ = lax.optimization_barrier((*n3s, act))
            if relay:
                n3s[2] = to_z[1](n3s[3])
    backs = sent[:1] + [to_z[k](sent[k]) for k in range(1, 2 if relay else chips)]
    if relay:
        sent[2] = total(sent[2], to_z[1](sent[3])).astype(BF16)
        backs.append(to_z[2](sent[2]))
    (mlp_grad,) = call(
        functools.partial(mlp_grad_kernel, chips),
        [((dps, 2 * hid + PAD, cut), BF16)],
        idx,
        cotangent,
        *acts,
        *ghis,
        *chunks,
        scratch=[
            pltpu.VMEM((rows, hid), BF16),
            pltpu.VMEM((rows, hid), BF16),
            pltpu.VMEM((rows, dim), BF16),
        ],
        after=sent,
        stage=True,
        name="mlp_grad",
    )
    mlp_grad, backs[1] = lax.optimization_barrier((mlp_grad, backs[1]))
    mlp_swap = swap_dp(mlp_grad)
    mlp_part = call(
        functools.partial(mlp_out_kernel, chips),
        [((own, dim), BF16)] * chips,
        idx,
        output_weight,
        output_weight2,
        *acts,
        *others,
        after=(mlp_grad,),
        stage=True,
        name="mlp_out",
    )
    *backs, mlp_part = lax.optimization_barrier((*backs, list(mlp_part)))
    mlp_parts = mlp_part[:1] + [to_z[k](mlp_part[k]) for k in far[:2]]

    outs = call(
        functools.partial(cross_back_kernel, chips, dps, len(backs)),
        [
            ((3, own, dim), BF16),
            ((own, dim), F32),
            ((8, dim), F32),
            ((chips, 2, SEEN, width), BF16),
            ((chips, 2, SEEN, width), BF16),
        ]
        + [((2, own, width), BF16)] * chips,
        idx,
        cotangent,
        norm_gain,
        second,
        first,
        cp,
        q,
        *weights,
        *backs,
        *att,
        *att2,
        scratch=[
            pltpu.VMEM((own, sq), BF16),
            pltpu.VMEM((3, sq, dim), BF16),
            pltpu.SemaphoreType.DMA((3, 2 * dps + 2)),
            pltpu.VMEM((own, dim), BF16),
            pltpu.SemaphoreType.DMA,
        ],
        raw=(0, *range(6, 6 + len(weights))),
        cost=10**12,
        stage=True,
        name="cross_bwd",
    )
    outs, mlp_parts, mlp_swap = lax.optimization_barrier((outs, mlp_parts, mlp_swap))
    mlp_piece = sum_dp(mlp_swap[:, : 2 * hid])
    mlp_all = [mlp_piece] + [to_dp[q](mlp_piece) for q in (1, 2)]
    bwd, gf, stat_a, dkv, dkv_other = outs[:5]
    gatt = outs[5:]
    gatt = [gatt[0]] + [to_z[k](gatt[k]) for k in far]

    (row_grad,) = call(
        functools.partial(row_grad_kernel, chips),
        [((dps, chips * 3 * width, cut), BF16)],
        idx,
        fwd,
        fwd2,
        bwd,
        to_core(bwd),
        scratch=[pltpu.VMEM((2 * own, chips * width), BF16), pltpu.VMEM((2 * own, dim), BF16)],
        stage=True,
        name="row_grad",
    )
    gatt, row_grad, mlp_all, mlp_part = lax.optimization_barrier(
        (gatt, row_grad, mlp_all, mlp_part)
    )
    mlp_all += [to_dp[q](mlp_all[0]) for q in range(3, dps)]
    gatt2 = [to_core(x) for x in gatt]
    row_swap = swap_dp(row_grad)
    mlp_parts += [to_z[k](mlp_part[k]) for k in far[2:]]

    outs = call(
        functools.partial(self_back_kernel, chips),
        [((rows, 3 * width), BF16)] + [((own, dim), BF16)] * (2 * chips),
        idx,
        triple,
        probs,
        self_weight,
        *gatt,
        *gatt2,
        scratch=[
            pltpu.VMEM((rows, width), BF16),
            pltpu.VMEM((width, rows), BF16),
            pltpu.VMEM((dim, 3 * width), BF16),
            pltpu.VMEM((rows, width), F32),
            pltpu.VMEM((rows, width), F32),
            pltpu.VMEM((rows, dim), BF16),
        ],
        cost=10**12,
        stage=True,
        name="self_bwd",
    )
    outs, mlp_parts = lax.optimization_barrier((outs, mlp_parts))
    gt, bs, bo = outs[0], outs[1 : 1 + chips], outs[1 + chips :]
    bos = [to_core(x) for x in bo]

    dkv = total(dkv, to_core(dkv_other)).astype(BF16)
    gp = total(dkv[0], *[to_z[k](dkv[k]) for k in far]).astype(BF16)

    *bos, gp = lax.optimization_barrier((*bos, gp))
    sent = add_all(bs, bos, "self_add")
    parts = sent[:1] + [to_z[k](sent[k]) for k in far]

    (self_part,) = call(
        functools.partial(self_grad_kernel, chips, dps),
        [((dps, 5 * width + dps * PAD, cut), BF16)],
        idx,
        tokens,
        normed_one,
        gt,
        near,
        gp,
        stat_a,
        *bs,
        *bo,
        after=sent[:1],
        stage=True,
        name="self_grad",
    )
    self_part, row_swap, mlp_all, parts[1:3] = lax.optimization_barrier(
        (self_part, row_swap, mlp_all, parts[1:3])
    )
    self_swap = swap_dp(self_part)
    row_piece = sum_dp(row_swap).reshape(chips, 3 * width, cut)
    row_parts = [row_piece[0]] + [to_z[k](row_piece[k]) for k in far]
    row_parts, self_swap = lax.optimization_barrier((row_parts, self_swap))
    row_piece = total(*row_parts).astype(BF16)
    self_sum = sum_dp(self_swap)
    piece = jnp.concatenate([row_piece, self_sum[: 5 * width]], 0)
    swapped = share_dp(piece)
    (grad_tokens,) = call(
        token_kernel,
        [((own, dim), F32)],
        idx,
        tokens,
        norm_gain,
        gf,
        *parts,
        scratch=[pltpu.VMEM((own, dim), BF16), pltpu.SemaphoreType.DMA],
        raw=(0,),
        stage=True,
        name="tokens",
    )
    state_part = jnp.einsum("cse,cde->sd", gp, cross_pair, preferred_element_type=F32)
    held = self_sum[5 * width :].reshape(dps, PAD, cut)
    held = jnp.concatenate([held[c] for c in range(dps)], 1)
    state_part = jnp.concatenate([state_part.astype(BF16), held], 0)
    state_part = total(state_part, to_core(state_part)).astype(BF16)
    state_sum = total(state_part, *[to_z[k](state_part) for k in far])
    grad_states = lax.dynamic_update_slice(
        jnp.zeros(states.shape, F32), state_sum[None, :SEEN], (state_row[0], begin, 0)
    )
    stats = state_sum[SEEN:]

    def place(pieces, plan, shapes, name):
        return call(
            functools.partial(place_kernel, plan),
            [(s, F32) for s in shapes],
            idx,
            *pieces,
            stage=True,
            name=name,
        )

    block_output = (second + total(*mlp_parts) + output_bias.astype(F32)).astype(BF16)
    grad_output_weight, grad_hidden_weight = place(
        mlp_all, ((hid, None, False), (hid, None, True)), ((hid, dim), (dim, hid)), "place_mlp"
    )
    swapped, block_output, grad_output_weight, grad_tokens, state_sum = lax.optimization_barrier(
        (swapped, block_output, grad_output_weight, grad_tokens, state_sum)
    )
    (
        grad_self_output,
        grad_cross_query,
        grad_cross_output,
        grad_self_weight,
        grad_cross_pair,
    ) = place(
        [swapped],
        (
            (width, None, False),
            (width, None, True),
            (width, None, False),
            (3 * width, 3, True),
            (2 * width, 2, True),
        ),
        (
            (width, dim),
            (dim, width),
            (width, dim),
            (3, dim, width),
            (2, dim, width),
        ),
        "place",
    )
    grad_norm_gain = jnp.stack([stats[0], stats[4], stats[2]])
    grad_norm_shift = jnp.stack([stats[1], stats[5], stats[3]])
    grad_output_bias = stats[6]
    grad_hidden_bias = jnp.sum(mlp_swap[:, 2 * hid : 2 * hid + hid // cut].astype(F32), 0).reshape(hid)
    return (
        block_output,
        grad_tokens,
        grad_states,
        grad_self_weight,
        grad_self_output,
        grad_cross_query,
        grad_cross_pair,
        grad_cross_output,
        grad_hidden_weight,
        grad_hidden_bias,
        grad_output_weight,
        grad_output_bias,
        grad_norm_gain,
        grad_norm_shift,
    )


def solution(mesh):
    placed = (
        P("dp", None),
        P("dp", None, None),
        P("dp", None),
        P(None, None, "mp"),
        P("mp", None),
        P(None, "mp"),
        P(None, None, "mp"),
        P("mp", None),
        P(None, "mp"),
        P("mp"),
        P("mp", None),
        P(),
        P(),
        P(),
        P("dp"),
        P("dp", None),
        P("dp"),
    )
    return jax.shard_map(
        body,
        mesh=mesh,
        in_specs=placed,
        out_specs=(
            P(("dp", "mp"), None),
            P(("dp", "mp"), None),
            P("dp", None, None),
            P(None, None, "mp"),
            P("mp", None),
            P(None, "mp"),
            P(None, None, "mp"),
            P("mp", None),
            P(None, "mp"),
            P("mp"),
            P("mp", None),
            P(),
            P(),
            P(),
        ),
        check_vma=False,
    )
```

```python
import functools
import math

import jax
import jax.numpy as jnp
from jax import lax
from jax.experimental import pallas as pl
from jax.experimental.pallas import tpu as pltpu
from jax.sharding import PartitionSpec as P

HDIM = 64
SEEN = 64
QB = 256
PAD = 16
EPSILON = 1e-05
NEG_FILL = -1e30
SCALE = HDIM ** (-0.5)
F32 = jnp.float32
BF16 = jnp.bfloat16


def dot_nn(a, b):
    return lax.dot_general(a, b, (((1,), (0,)), ((), ())), preferred_element_type=F32)


def dot_nt(a, b):
    return lax.dot_general(a, b, (((1,), (1,)), ((), ())), preferred_element_type=F32)


def dot_tn(a, b):
    return lax.dot_general(a, b, (((0,), (0,)), ((), ())), preferred_element_type=F32)


def normalize(resid):
    center = resid - jnp.mean(resid, -1, keepdims=True)
    inverse = lax.rsqrt(jnp.mean(center * center, -1, keepdims=True) + EPSILON)
    return (center * inverse, inverse)


def norm_backward(standard, inverse, grad_normed, gain):
    scaled = grad_normed * gain
    return inverse * (
        scaled
        - jnp.mean(scaled, -1, keepdims=True)
        - standard * jnp.mean(scaled * standard, -1, keepdims=True)
    )


def at(index, size):
    return pl.ds(pl.multiple_of(index * size, size), size)


def staged(kernel, ins, outs, extra, *refs):
    count_in, count_out = len(ins), len(outs)
    idx, refs = refs[0], list(refs[1:])
    inner = refs[: count_in + count_out]
    own = refs[count_in + count_out : count_in + count_out + extra]
    rest = refs[count_in + count_out + extra :]
    sem_in, sem_out = rest[-2:]
    held = iter(rest[:-2])
    started, results = [], []
    for i, here in enumerate(ins):
        if here:
            local = next(held)
            started.append(pltpu.make_async_copy(inner[i], local, sem_in.at[len(started)]))
            inner[i] = local
    for i, here in enumerate(outs):
        if here:
            local = next(held)
            target = inner[count_in + i]
            results.append(pltpu.make_async_copy(local, target, sem_out.at[len(results)]))
            inner[count_in + i] = local
    for copy in started:
        copy.start()
    for copy in started:
        copy.wait()
    kernel(idx, *inner, *own)
    for copy in results:
        copy.start()
    for copy in results:
        copy.wait()


def call(
    kernel, outs, idx, *args, scratch=(), after=(), stage=False, tight=False, raw=(), cost=1, name=None, spill=8
):
    if after:
        idx = lax.optimization_barrier((idx, *after))[0]
    out_shape = [jax.ShapeDtypeStruct(s, t) for s, t in outs]
    big = lambda a: bool(stage) and a.size >= 1 << 15
    ins_far = [big(a) and i not in raw for i, a in enumerate(args)]
    outs_far = [big(a) for a in out_shape]
    vmem = pl.BlockSpec(memory_space=pltpu.VMEM)
    hbm = pl.BlockSpec(memory_space=pltpu.HBM)
    held = spill << 20
    for i, a in enumerate((*args, *out_shape)):
        if i not in raw:
            held += a.size * a.dtype.itemsize
    for a in scratch:
        if len(getattr(a, "shape", ())) > 1 and a.dtype in (F32, BF16):
            held += math.prod(a.shape) * jnp.dtype(a.dtype).itemsize
    scratch = list(scratch)
    if any(ins_far) or any(outs_far):
        kernel = functools.partial(staged, kernel, ins_far, outs_far, len(scratch))
        for a, far in zip((*args, *out_shape), ins_far + outs_far):
            if far:
                scratch.append(pltpu.VMEM(a.shape, a.dtype))
        scratch.append(pltpu.SemaphoreType.DMA((max(1, sum(ins_far)),)))
        scratch.append(pltpu.SemaphoreType.DMA((max(1, sum(outs_far)),)))
    return pl.pallas_call(
        kernel,
        out_shape=out_shape,
        in_specs=[pl.BlockSpec(memory_space=pltpu.SMEM)]
        + [hbm if far or i in raw else vmem for i, far in enumerate(ins_far)],
        out_specs=[hbm if far else vmem for far in outs_far],
        scratch_shapes=scratch,
        cost_estimate=pl.CostEstimate(flops=cost, bytes_accessed=1, transcendentals=0),
        compiler_params=pltpu.CompilerParams(
            vmem_limit_bytes=min(held, 60 << 20) if tight else 60 << 20
        ),
        name=name,
    )(idx, *args)


def head_select(parts, axis):
    if len(parts) == 1:
        return parts[0]
    head = lax.broadcasted_iota(jnp.int32, parts[0].shape, axis) // HDIM
    return jnp.where(head == 0, parts[0], parts[1])


def head_only(value, h, count):
    if count == 1:
        return value
    head = lax.broadcasted_iota(jnp.int32, value.shape, 1) // HDIM
    return jnp.where(head == h, value, jnp.zeros_like(value))


def self_kernel(
    chips, idx, tok, weight, gain, shift, states, pair, segment, normed, triple, probs, *rest
):
    att_out = rest[:chips]
    val_t, att, kv = rest[chips:]
    rows, width = tok.shape[0], weight.shape[2]
    heads = width // HDIM
    g = gain[0:1, :].astype(F32)
    s = shift[0:1, :].astype(F32)

    def project(i, carry):
        here = at(i, QB)
        standard, _ = normalize(tok[here, :].astype(F32))
        n = (standard * g + s).astype(BF16)
        normed[here, :] = n
        triple[0, here, :] = dot_nn(n, weight[0]).astype(BF16)
        triple[1, here, :] = dot_nn(n, weight[1]).astype(BF16)
        value = dot_nn(n, weight[2])
        triple[2, here, :] = value.astype(BF16)
        val_t[:, here] = value.T.astype(BF16)
        return carry

    lax.fori_loop(0, rows // QB, project, 0)
    for i in range(rows // QB):
        here = slice(i * QB, (i + 1) * QB)
        query = triple[0, here, :]
        seen = (i + 1) * QB
        outs = []
        for h in range(heads):
            scores = dot_nt(triple[1, 0:seen, :], head_only(query, h, heads)) * SCALE
            key_at = lax.broadcasted_iota(jnp.int32, scores.shape, 0)
            row_at = lax.broadcasted_iota(jnp.int32, scores.shape, 1) + i * QB
            scores = jnp.where(key_at <= row_at, scores, NEG_FILL)
            e = jnp.exp(scores - jnp.max(scores, 0, keepdims=True))
            p = (e * (1.0 / jnp.sum(e, 0, keepdims=True))).astype(BF16)
            probs[h, 0:seen, here] = p
            outs.append(dot_nn(val_t[:, 0:seen], p))
        att[here, :] = head_select(outs, 0).T.astype(BF16)
    own = (att_out[0].shape[0] - 2 * SEEN) // 2
    before = segment[pl.ds(idx[2], 1), :] < idx[3]
    begin = jnp.minimum(jnp.sum(before.astype(jnp.int32)), states.shape[1] - SEEN)
    for c in range(2):
        kv[...] = dot_nn(states[idx[2]], pair[c])
        for k in range(chips):
            where = slice(2 * own + c * SEEN, 2 * own + (c + 1) * SEEN)
            att_out[k][where, :] = kv[pl.ds(begin, SEEN), :].astype(BF16)
    for k in range(chips):
        for cc in range(2):
            att_out[k][cc * own : (cc + 1) * own, :] = att[at(idx[0] ^ (2 * k + cc), own), :]


def pair_tiles(block, heads):
    return jnp.concatenate([head_only(block, h, heads) for h in range(heads)], 0)


def half_reduce(op, value, heads, fill):
    if heads == 1:
        return op(value, -1, keepdims=True)
    half = lax.broadcasted_iota(jnp.int32, value.shape, 1) // SEEN
    first = op(jnp.where(half == 0, value, fill), -1, keepdims=True)
    other = op(jnp.where(half == 1, value, fill), -1, keepdims=True)
    return jnp.where(half == 0, first, other)


def fetch_weights(chips, dps, idx, weights, wf, sem):
    width = wf.shape[1] // (2 * chips)
    cut = wf.shape[2] // dps
    span = (chips - 1) * width
    half = chips * width
    lists = []
    for m in range(3):
        copies = []
        for cc in range(2):
            source = weights[cc * (dps + 1)]
            where = wf.at[m, cc * half : cc * half + width, :]
            copies.append((source.at[m * width : (m + 1) * width, :], where))
            for q in range(dps):
                source = weights[cc * (dps + 1) + 1 + q]
                cols = at(idx[1] ^ q, cut)
                where = wf.at[m, cc * half + width : (cc + 1) * half, cols]
                copies.append((source.at[m * span : (m + 1) * span, :], where))
        lists.append(
            [pltpu.make_async_copy(s, d, sem.at[m, i]) for i, (s, d) in enumerate(copies)]
        )
    return lists


def own_rows(idx, source, rows, sem):
    copy = pltpu.make_async_copy(source.at[at(idx[0], rows.shape[0]), :], rows, sem)
    copy.start()
    return copy


def cross_kernel(chips, dps, idx, tokens, gain, shift, seen, *rest):
    take = iter(rest)
    pull = lambda n: [next(take) for _ in range(n)]
    weights = pull(2 * dps + 2)
    att_in = [pull(chips), pull(chips)]
    first_o, pack_o, q_o, cp_o, second_o, n3_o = pull(6)
    wf, sem, tok, tok_sem = pull(4)
    fetch = own_rows(idx, tokens, tok, tok_sem)
    own, dim = tok.shape
    width = wf.shape[1] // (2 * chips)
    heads = width // HDIM
    half = chips * width
    copies = fetch_weights(chips, dps, idx, weights, wf, sem)
    for each in copies:
        for copy in each:
            copy.start()
    for k in range(chips):
        pack_o[0, :, k * width : (k + 1) * width] = att_in[0][k][0:own, :]
        pack_o[0, :, half + k * width : half + (k + 1) * width] = att_in[1][k][own : 2 * own, :]
    fetch.wait()
    for copy in copies[0]:
        copy.wait()
    resid = tok[...].astype(F32) + dot_nn(pack_o[0], wf[0])
    first_o[...] = resid
    n2 = (normalize(resid)[0] * gain[1:2, :].astype(F32) + shift[1:2, :].astype(F32)).astype(BF16)
    pack_o[1, :, :] = n2
    for copy in copies[1]:
        copy.wait()
    q_o[...] = dot_nt(n2, wf[1]).astype(BF16)
    allowed = seen[...] > 0
    for cc in range(2):
        for k in range(chips):
            b = cc * chips + k
            lanes = slice(b * width, (b + 1) * width)
            keys = pair_tiles(att_in[cc][k][2 * own : 2 * own + SEEN, :], heads)
            values = pair_tiles(att_in[cc][k][2 * own + SEEN :, :], heads)
            scores = dot_nt(q_o[:, lanes], keys) * SCALE
            scores = jnp.where(allowed, scores, NEG_FILL)
            e = jnp.exp(scores - half_reduce(jnp.max, scores, heads, NEG_FILL))
            p = (e * (1.0 / half_reduce(jnp.sum, e, heads, 0.0))).astype(BF16)
            cp_o[b] = p
            pack_o[2, :, lanes] = dot_nn(p, values).astype(BF16)
    for copy in copies[2]:
        copy.wait()
    resid = resid + dot_nn(pack_o[2], wf[2])
    second_o[...] = resid
    n3 = normalize(resid)[0] * gain[2:3, :].astype(F32) + shift[2:3, :].astype(F32)
    n3_o[...] = n3.astype(BF16)


def active_kernel(chips, idx, cot, weight, *rest):
    outs, part = rest[:chips], rest[chips]
    rows = outs[0].shape[0]

    def chip(k, carry):
        part[k] = dot_nt(cot[at((idx[0] // 2) ^ k, rows), :], weight[...])
        return carry

    lax.fori_loop(0, chips, chip, 0)
    for k in range(chips):
        outs[k][...] = part[k]


def hidden_kernel(idx, same, other, weight, bias, grad_active, n3_o, act_o, ghi_o, bs_o, bo_o, back):
    own = same.shape[0]
    core = lax.rem(idx[0], 2)
    n3_o[at(core, own), :] = same[...]
    n3_o[at(1 - core, own), :] = other[...]
    v = dot_nn(n3_o[...], weight[...]) + bias[...].astype(F32)
    root = 0.7978845608028654
    square = v * v
    t = jnp.tanh(root * v * (1.0 + 0.044715 * square))
    act_o[...] = (0.5 * v * (1.0 + t)).astype(BF16)
    slope = 0.5 * (1.0 + t) + 0.5 * v * (1.0 - t * t) * (root * (1.0 + 0.134145 * square))
    ghi = (grad_active[...] * slope).astype(BF16)
    ghi_o[...] = ghi
    back[...] = dot_nt(ghi, weight[...])
    bs_o[...] = back[at(core, own), :].astype(BF16)
    dim = back.shape[1]
    bo_o[:, 0:dim] = back[at(1 - core, own), :].astype(BF16)
    bo_o[:, dim:] = act_o[at(1 - core, own), :]


def mlp_out_kernel(chips, idx, weight, weight2, *rest):
    acts, others, outs = rest[:chips], rest[chips : 2 * chips], rest[2 * chips : 3 * chips]
    near, part, sem = rest[3 * chips :]
    own, dim = outs[0].shape
    hid = weight.shape[0]
    mine = at(lax.rem(idx[0], 2), own)
    copies = []
    for k in range(chips):
        sources = acts[k].at[mine, :], others[k].at[:, dim : dim + hid]
        for c, source in enumerate(sources):
            copies.append(pltpu.make_async_copy(source, near.at[c, k], sem.at[c, k]))
    for copy in copies:
        copy.start()
    for copy in copies:
        copy.wait()

    def chip(k, carry):
        value = dot_nn(near[0, k], weight[...]) + dot_nn(near[1, k], weight2[...])
        part[k] = value.astype(BF16)
        return carry

    lax.fori_loop(0, chips, chip, 0)
    for k in range(chips):
        outs[k][...] = part[k]


def mlp_grad_kernel(chips, idx, cot, *rest):
    acts = rest[:chips]
    ghis = rest[chips : 2 * chips]
    n3s = rest[2 * chips : 3 * chips]
    out, act, ghi, n3 = rest[3 * chips :]
    step = acts[0].shape[0]
    hid = acts[0].shape[1]
    dps, _, cut = out.shape
    total = jnp.zeros((1, hid), F32)
    for k in range(chips):
        rows = at((idx[0] // 2) ^ k, step)
        act[rows, :] = acts[k][...]
        ghi[rows, :] = ghis[k][...]
        n3[rows, :] = n3s[k][...]
        total += jnp.sum(ghis[k][...].astype(F32), 0, keepdims=True)
    row = lax.broadcasted_iota(jnp.int32, (PAD, cut), 0)
    bias = jnp.zeros((PAD, cut), F32)
    for j in range(hid // cut):
        bias = jnp.where(row == j, total[:, j * cut : (j + 1) * cut], bias)
    def columns(q, carry):
        cols = at(q, cut)
        out[q, 0:hid, :] = dot_tn(act[...], cot[:, cols]).astype(BF16)
        out[q, hid : 2 * hid, :] = dot_tn(ghi[...], n3[:, cols]).astype(BF16)
        out[q, 2 * hid : 2 * hid + PAD, :] = bias.astype(BF16)
        return carry

    lax.fori_loop(0, dps, columns, 0)


def cross_back_kernel(chips, dps, count, idx, cotangent, gain, second, first, cp, q, *rest):
    take = iter(rest)
    pull = lambda n: [next(take) for _ in range(n)]
    weights = pull(2 * dps + 2)
    parts = pull(count)
    kv = [pull(chips), pull(chips)]
    pack_o, gf_o, stat_o, same_o, other_o = pull(5)
    gt_o = pull(chips)
    gc, wf, sem, cot, cot_sem = pull(5)
    fetch = own_rows(idx, cotangent, cot, cot_sem)
    copies = fetch_weights(chips, dps, idx, weights, wf, sem)
    for each in reversed(copies):
        for copy in each:
            copy.start()
    dkv_o = (same_o, other_o)
    own = cot.shape[0]
    width = kv[0][0].shape[1]
    heads = width // HDIM
    grad_normed = parts[0][...].astype(F32)
    for part in parts[1:]:
        grad_normed += part[...].astype(F32)
    fetch.wait()
    c = cot[...].astype(F32)
    standard, inverse = normalize(second[...])
    grad = c + norm_backward(standard, inverse, grad_normed, gain[2:3, :].astype(F32))
    stat_o[0:1, :] = jnp.sum(grad_normed * standard, 0, keepdims=True)
    stat_o[1:2, :] = jnp.sum(grad_normed, 0, keepdims=True)
    stat_o[4:5, :] = jnp.sum(c, 0, keepdims=True)
    g2 = grad.astype(BF16)
    pack_o[2, :, :] = g2
    for copy in copies[2]:
        copy.wait()
    gc[...] = dot_nt(g2, wf[2]).astype(BF16)
    for cc in range(2):
        for k in range(chips):
            b = cc * chips + k
            lanes = slice(b * width, (b + 1) * width)
            keys = pair_tiles(kv[cc][k][2 * own : 2 * own + SEEN, :], heads)
            values = pair_tiles(kv[cc][k][2 * own + SEEN :, :], heads)
            gcb = gc[:, lanes]
            dp = dot_nt(gcb, values)
            low = cp[b]
            p = low.astype(F32)
            inner = half_reduce(jnp.sum, dp * p, heads, 0.0)
            ds = (p * (dp - inner) * SCALE).astype(BF16)
            pack_o[1, :, lanes] = dot_nn(ds, keys).astype(BF16)
            dk = dot_tn(ds, q[:, lanes])
            dv = dot_tn(low, gcb)
            for i, d in enumerate((dk, dv)):
                fold = head_select([d[h * SEEN : (h + 1) * SEEN, :] for h in range(heads)], 1)
                dkv_o[cc][k, i, :, :] = fold.astype(BF16)
    for copy in copies[1]:
        copy.wait()
    grad_normed = dot_nn(pack_o[1], wf[1])
    standard, inverse = normalize(first[...])
    grad = grad + norm_backward(standard, inverse, grad_normed, gain[1:2, :].astype(F32))
    stat_o[2:3, :] = jnp.sum(grad_normed * standard, 0, keepdims=True)
    stat_o[3:4, :] = jnp.sum(grad_normed, 0, keepdims=True)
    gf_o[...] = grad
    g1 = grad.astype(BF16)
    pack_o[0, :, :] = g1
    for copy in copies[0]:
        copy.wait()
    gatt = dot_nt(g1, wf[0]).astype(BF16)
    for cc in range(2):
        for k in range(chips):
            b = cc * chips + k
            gt_o[k][cc, :, :] = gatt[:, b * width : (b + 1) * width]


def row_grad_kernel(chips, idx, fwd, fwd2, bwd, bwd2, out, left, right):
    dps, height, cut = out.shape
    width = height // (3 * chips)
    own = fwd.shape[1]
    half = chips * width
    for m, (l, r) in enumerate((((fwd, fwd2), (bwd, bwd2)), ((bwd, bwd2), (fwd, fwd2)), ((fwd, fwd2), (bwd, bwd2)))):
        left[0:own, :] = l[0][m, :, 0:half]
        left[own : 2 * own, :] = l[1][m, :, half : 2 * half]
        right[0:own, :] = r[0][m]
        right[own : 2 * own, :] = r[1][m]
        for q in range(dps):
            part = dot_tn(left[...], right[:, q * cut : (q + 1) * cut]).astype(BF16)
            for k in range(chips):
                row = (3 * k + m) * width
                out[q, row : row + width, :] = part[k * width : (k + 1) * width, :]


def pack_kernel(idx, *refs):
    parts, out = refs[:-1], refs[-1]
    width = parts[0].shape[0] // 3
    for m in range(3):
        for k, part in enumerate(parts):
            row = (m * len(parts) + k) * width
            out[row : row + width, :] = part[m * width : (m + 1) * width, :]


def self_back_kernel(chips, idx, triple, probs, weight, *rest):
    take = iter(rest)
    pull = lambda n: [next(take) for _ in range(n)]
    grads = [pull(chips), pull(chips)]
    (gt_o,) = pull(1)
    bs_o, bo_o = pull(chips), pull(chips)
    gout, key_t, wcat, dq, dk, dv, back = pull(7)
    rows, width = triple.shape[1], triple.shape[2]
    heads = width // HDIM
    own = bs_o[0].shape[0]
    for k in range(chips):
        gout[at(idx[0] ^ (2 * k), own), :] = grads[0][k][0]
        gout[at(idx[0] ^ (2 * k + 1), own), :] = grads[1][k][1]
    for c in range(3):
        wcat[:, c * width : (c + 1) * width] = weight[c]
    count = rows // QB
    for i in range(count):
        here = slice(i * QB, (i + 1) * QB)
        key_t[:, here] = triple[1, here, :].astype(F32).T.astype(BF16)
    dk[...] = jnp.zeros(dk.shape, F32)
    dv[...] = jnp.zeros(dv.shape, F32)

    def one_head(h, carry):
        for i in reversed(range(count)):
            here = slice(i * QB, (i + 1) * QB)
            seen = (i + 1) * QB
            go = head_only(gout[here, :], h, heads)
            query = head_only(triple[0, here, :], h, heads)
            dp = dot_nt(triple[2, 0:seen, :], go)
            low = probs[h, 0:seen, here]
            p = low.astype(F32)
            inner = jnp.sum(dp * p, 0, keepdims=True)
            ds = (p * (dp - inner) * SCALE).astype(BF16)
            dk[0:seen, :] += dot_nn(ds, query)
            dv[0:seen, :] += dot_nn(low, go)
            new_q = dot_nn(key_t[:, 0:seen], ds)
            head = lax.broadcasted_iota(jnp.int32, new_q.shape, 0) // HDIM
            dq[:, here] = jnp.where(head == h, new_q, dq[:, here])
        return carry

    lax.fori_loop(0, heads, one_head, 0)
    for i in range(count):
        here = slice(i * QB, (i + 1) * QB)
        gt_o[here, 0:width] = dq[:, here].T.astype(BF16)
        gt_o[here, width : 2 * width] = dk[here, :].astype(BF16)
        gt_o[here, 2 * width : 3 * width] = dv[here, :].astype(BF16)

    def project(i, carry):
        back[at(i, QB), :] = dot_nt(gt_o[at(i, QB), :], wcat[...]).astype(BF16)
        return carry

    lax.fori_loop(0, count, project, 0)
    for k in range(chips):
        bs_o[k][...] = back[at(idx[0] ^ (2 * k), own), :]
        bo_o[k][...] = back[at(idx[0] ^ (2 * k + 1), own), :]


def self_grad_kernel(chips, dps, idx, tok, normed, gt, states, gp, stat, *rest):
    parts, (out, held, sem) = rest[: 2 * chips], rest[2 * chips :]
    cut = out.shape[2]
    width = gp.shape[2]
    own = held.shape[1]
    copies = []
    for k in range(chips):
        for cc in range(2):
            j = 2 * k + cc
            copies.append(pltpu.make_async_copy(parts[cc * chips + k], held.at[j], sem.at[j]))
    for copy in copies:
        copy.start()

    def columns(q, carry):
        cols = at(q, cut)
        out[q, 0 : 3 * width, :] = dot_tn(gt[...], normed[:, cols]).astype(BF16)
        for c in range(2):
            out[q, (3 + c) * width : (4 + c) * width, :] = dot_tn(
                gp[c], states[:, cols]
            ).astype(BF16)
        return carry

    lax.fori_loop(0, dps, columns, 0)
    for copy in copies:
        copy.wait()

    def add_rows(j, carry):
        g = held[j].astype(F32)
        standard, _ = normalize(tok[at(idx[0] ^ j, own), :].astype(F32))
        gain = carry[0] + jnp.sum(g * standard, 0, keepdims=True)
        return gain, carry[1] + jnp.sum(g, 0, keepdims=True)

    none = jnp.zeros((1, tok.shape[1]), F32)
    gain, shift = lax.fori_loop(0, 2 * chips, add_rows, (none, none))
    row = lax.broadcasted_iota(jnp.int32, (PAD, tok.shape[1]), 0)
    both = jnp.where(row == 0, gain, jnp.where(row == 1, shift, 0.0))
    for i in range(5):
        both = jnp.where(row == i + 2, stat[i : i + 1, :], both)
    both = both.astype(BF16)
    for q in range(dps):
        for c in range(dps):
            here = slice(5 * width + c * PAD, 5 * width + (c + 1) * PAD)
            out[q, here, :] = both[:, c * cut : (c + 1) * cut]


def add_kernel(idx, *refs):
    count = len(refs) // 3
    for k in range(count):
        total = refs[k][...].astype(F32) + refs[count + k][...].astype(F32)
        refs[2 * count + k][...] = total.astype(BF16)


def sum_kernel(idx, pieces, out):
    step = math.gcd(out.shape[0], 64)

    def add_rows(i, carry):
        here = at(i, step)
        out[here, :] = jnp.sum(pieces[:, here, :].astype(F32), 0).astype(BF16)
        return carry

    lax.fori_loop(0, out.shape[0] // step, add_rows, 0)


def token_kernel(idx, tokens, gain, grad, *rest):
    parts, (out, tok, sem) = rest[:-3], rest[-3:]
    own_rows(idx, tokens, tok, sem).wait()
    grad_normed = parts[0][...].astype(F32)
    for part in parts[1:]:
        grad_normed += part[...].astype(F32)
    standard, inverse = normalize(tok[...].astype(F32))
    out[...] = grad[...] + norm_backward(standard, inverse, grad_normed, gain[0:1, :].astype(F32))


def place_kernel(plan, idx, *refs):
    parts, outs = refs[: -len(plan)], refs[-len(plan) :]
    if len(parts) == 1:
        source = parts[0]
        count, _, cut = source.shape
        take = lambda q, rows: source[q, rows, :]
        where_of = lambda q: slice(q * cut, (q + 1) * cut)
    else:
        count, cut = len(parts), parts[0].shape[1]
        take = lambda q, rows: parts[q][rows, :]
        where_of = lambda q: at(idx[1] ^ q, cut)
    row = 0
    for out, (height, lead, flip) in zip(outs, plan):
        for q in range(count):
            where = where_of(q)
            piece = take(q, slice(row, row + height)).astype(F32)
            if not flip:
                out[:, where] = piece
            elif lead is None:
                out[where, :] = piece.T
            else:
                step = height // lead
                for c in range(lead):
                    out[c, where, :] = piece[c * step : (c + 1) * step, :].T
        row += height


def flip_bits(axis, bits, size):
    return functools.partial(
        lax.ppermute, axis_name=axis, perm=[(i, i ^ bits) for i in range(size)]
    )


def total(*parts):
    out = parts[0].astype(F32)
    for part in parts[1:]:
        out = out + part.astype(F32)
    return out


def body(
    tokens,
    states,
    cotangent,
    self_weight,
    self_output,
    cross_query,
    cross_pair,
    cross_output,
    hidden_weight,
    hidden_bias,
    output_weight,
    output_bias,
    norm_gain,
    norm_shift,
    state_row,
    state_segment,
    caption,
):
    rows, dim = tokens.shape
    width = cross_query.shape[1]
    heads = width // HDIM
    hid = hidden_bias.shape[0]
    cores = lax.axis_size("mp")
    chips = cores // 2
    dps = lax.axis_size("dp")
    own = rows // cores
    cut = dim // dps
    me = lax.axis_index("mp")
    dpi = lax.axis_index("dp")
    idx = jnp.stack([me, dpi, state_row[0], caption[0]]).astype(jnp.int32)
    to_z = [flip_bits("mp", 2 * k, cores) for k in range(chips)]
    to_core = flip_bits("mp", 1, cores)
    to_dp = [flip_bits("dp", q, dps) for q in range(dps)]
    far = range(1, chips)
    peers = range(1, dps)

    def share_dp(piece):
        return lax.all_to_all(jnp.broadcast_to(piece[None], (dps,) + piece.shape), "dp", 0, 0)

    def add_all(left, right, name):
        return list(
            call(
            add_kernel,
            [((own, dim), BF16)] * chips,
            idx,
            *left,
            *right,
            stage=True,
            name=name,
        ))

    def swap_dp(pieces):
        return lax.all_to_all(pieces, "dp", 0, 0)

    def sum_dp(pieces):
        return jnp.sum(pieces.astype(F32), 0).astype(BF16)

    labels = lax.dynamic_index_in_dim(state_segment, state_row[0], 0, False)
    begin = jnp.minimum(jnp.sum((labels < caption[0]).astype(jnp.int32)), labels.shape[0] - SEEN)
    labels = lax.dynamic_slice_in_dim(labels, begin, SEEN, 0)
    seen = jnp.tile((labels == caption[0]).astype(jnp.int32)[None, :], (1, heads))
    near = lax.dynamic_slice(states, (state_row[0], begin, 0), (1, SEEN, dim))[0]

    mine = jnp.concatenate([self_output, cross_query.T, cross_output], 0)
    piece = lax.dynamic_slice_in_dim(mine, dpi * cut, cut, 1)
    got = [to_z[k](piece) for k in far]
    output_weight2 = to_core(output_weight)

    outs = call(
        functools.partial(self_kernel, chips),
        [
            ((rows, dim), BF16),
            ((3, rows, width), BF16),
            ((heads, rows, rows), BF16),
        ]
        + [((2 * own + 2 * SEEN, width), BF16)] * chips,
        idx,
        tokens,
        self_weight,
        norm_gain,
        norm_shift,
        states,
        cross_pair,
        state_segment,
        scratch=[
            pltpu.VMEM((width, rows), BF16),
            pltpu.VMEM((rows, width), BF16),
            pltpu.VMEM((states.shape[1], width), F32),
        ],
        after=(piece,),
        stage=True,
        name="self_fwd",
    )
    normed_one, triple, probs = outs[:3]
    att = outs[3:]
    *got, output_weight2, _ = lax.optimization_barrier((*got, output_weight2, att[0]))
    (cat,) = call(pack_kernel, [((3 * width * (chips - 1), cut), BF16)], idx, *got, tight=True, name="pack")
    att = [att[0]] + [to_z[k](att[k]) for k in far]
    att2 = [to_core(x) for x in att]

    grad_active = call(
        functools.partial(active_kernel, chips),
        [((2 * own, hid), F32)] * chips,
        idx,
        cotangent,
        output_weight,
        scratch=[pltpu.VMEM((chips, 2 * own, hid), F32)],
        after=att[:1],
        stage=True,
        name="grad_active",
    )

    cats = [cat] + [to_dp[q](cat) for q in peers]
    cats, grad_active, seen = lax.optimization_barrier((cats, grad_active, seen))
    weights = [mine, *cats, to_core(mine), *[to_core(x) for x in cats]]

    sq = cores * width
    first, fwd, q, cp, second, n3 = call(
        functools.partial(cross_kernel, chips, dps),
        [
            ((own, dim), F32),
            ((3, own, dim), BF16),
            ((own, sq), BF16),
            ((cores, own, heads * SEEN), BF16),
            ((own, dim), F32),
            ((own, dim), BF16),
        ],
        idx,
        tokens,
        norm_gain,
        norm_shift,
        seen,
        *weights,
        *att,
        *att2,
        scratch=[
            pltpu.VMEM((3, sq, dim), BF16),
            pltpu.SemaphoreType.DMA((3, 2 * dps + 2)),
            pltpu.VMEM((own, dim), BF16),
            pltpu.SemaphoreType.DMA,
        ],
        raw=(0, *range(4, 4 + len(weights))),
        stage=True,
        name="cross_fwd",
    )

    relay = chips == 4
    order = (0, 1, 3, 2) if relay else range(chips)
    n3s = [n3] + [None if relay and k == 2 else to_z[k](n3) for k in far]
    fwd2 = to_core(fwd)
    bias_row = hidden_bias[None, :]
    acts, ghis, chunks, sent, others = ([None] * chips for _ in range(5))
    done = ()
    for k in order:
        arrived = n3s[k]
        chunk, act, ghi, bs, bo = call(
            hidden_kernel,
            [
                ((2 * own, dim), BF16),
                ((2 * own, hid), BF16),
                ((2 * own, hid), BF16),
                ((own, dim), BF16),
                ((own, dim + hid), BF16),
            ],
            idx,
            arrived,
            to_core(arrived),
            hidden_weight,
            bias_row,
            grad_active[k],
            scratch=[pltpu.VMEM((2 * own, dim), F32)],
            after=done,
            tight=True,
            name="hidden",
        )
        done = (act,)
        acts[k], ghis[k], chunks[k] = act, ghi, chunk
        others[k] = to_core(bo)
        sent[k] = total(bs, others[k][:, :dim]).astype(BF16)
        if k == 0:
            *n3s, _ = lax.optimization_barrier((*n3s, act))
            if relay:
                n3s[2] = to_z[1](n3s[3])
    backs = sent[:1] + [to_z[k](sent[k]) for k in range(1, 2 if relay else chips)]
    if relay:
        sent[2] = total(sent[2], to_z[1](sent[3])).astype(BF16)
        backs.append(to_z[2](sent[2]))
    (mlp_grad,) = call(
        functools.partial(mlp_grad_kernel, chips),
        [((dps, 2 * hid + PAD, cut), BF16)],
        idx,
        cotangent,
        *acts,
        *ghis,
        *chunks,
        scratch=[
            pltpu.VMEM((rows, hid), BF16),
            pltpu.VMEM((rows, hid), BF16),
            pltpu.VMEM((rows, dim), BF16),
        ],
        after=sent,
        stage=True,
        name="mlp_grad",
    )
    mlp_grad, backs[1] = lax.optimization_barrier((mlp_grad, backs[1]))
    mlp_swap = swap_dp(mlp_grad)
    mlp_part = call(
        functools.partial(mlp_out_kernel, chips),
        [((own, dim), BF16)] * chips,
        idx,
        output_weight,
        output_weight2,
        *acts,
        *others,
        scratch=[
            pltpu.VMEM((2, chips, own, hid), BF16),
            pltpu.VMEM((chips, own, dim), BF16),
            pltpu.SemaphoreType.DMA((2, chips)),
        ],
        raw=tuple(range(2, 2 + 2 * chips)),
        after=(mlp_grad,),
        stage=True,
        name="mlp_out",
    )
    *backs, mlp_part = lax.optimization_barrier((*backs, list(mlp_part)))
    mlp_parts = mlp_part[:1] + [to_z[k](mlp_part[k]) for k in far[:2]]

    outs = call(
        functools.partial(cross_back_kernel, chips, dps, len(backs)),
        [
            ((3, own, dim), BF16),
            ((own, dim), F32),
            ((8, dim), F32),
            ((chips, 2, SEEN, width), BF16),
            ((chips, 2, SEEN, width), BF16),
        ]
        + [((2, own, width), BF16)] * chips,
        idx,
        cotangent,
        norm_gain,
        second,
        first,
        cp,
        q,
        *weights,
        *backs,
        *att,
        *att2,
        scratch=[
            pltpu.VMEM((own, sq), BF16),
            pltpu.VMEM((3, sq, dim), BF16),
            pltpu.SemaphoreType.DMA((3, 2 * dps + 2)),
            pltpu.VMEM((own, dim), BF16),
            pltpu.SemaphoreType.DMA,
        ],
        raw=(0, *range(6, 6 + len(weights))),
        cost=10**12,
        stage=True,
        name="cross_bwd",
    )
    outs, mlp_parts, mlp_swap = lax.optimization_barrier((outs, mlp_parts, mlp_swap))
    mlp_piece = call(
        sum_kernel, [((2 * hid, cut), BF16)], idx, mlp_swap, stage=True, name="sum_mlp"
    )[0]
    mlp_all = [mlp_piece] + [to_dp[q](mlp_piece) for q in (1, 2)]
    bwd, gf, stat_a, dkv, dkv_other = outs[:5]
    gatt = outs[5:]
    gatt = [gatt[0]] + [to_z[k](gatt[k]) for k in far]

    (row_grad,) = call(
        functools.partial(row_grad_kernel, chips),
        [((dps, chips * 3 * width, cut), BF16)],
        idx,
        fwd,
        fwd2,
        bwd,
        to_core(bwd),
        scratch=[pltpu.VMEM((2 * own, chips * width), BF16), pltpu.VMEM((2 * own, dim), BF16)],
        stage=True,
        name="row_grad",
    )
    gatt, row_grad, mlp_all, mlp_part = lax.optimization_barrier(
        (gatt, row_grad, mlp_all, mlp_part)
    )
    mlp_all += [to_dp[q](mlp_all[0]) for q in range(3, dps)]
    gatt2 = [to_core(x) for x in gatt]
    row_swap = swap_dp(row_grad)
    mlp_parts += [to_z[k](mlp_part[k]) for k in far[2:]]

    outs = call(
        functools.partial(self_back_kernel, chips),
        [((rows, 3 * width), BF16)] + [((own, dim), BF16)] * (2 * chips),
        idx,
        triple,
        probs,
        self_weight,
        *gatt,
        *gatt2,
        scratch=[
            pltpu.VMEM((rows, width), BF16),
            pltpu.VMEM((width, rows), BF16),
            pltpu.VMEM((dim, 3 * width), BF16),
            pltpu.VMEM((width, rows), F32),
            pltpu.VMEM((rows, width), F32),
            pltpu.VMEM((rows, width), F32),
            pltpu.VMEM((rows, dim), BF16),
        ],
        cost=10**12,
        stage=True,
        name="self_bwd",
    )
    outs, mlp_parts = lax.optimization_barrier((outs, mlp_parts))
    gt, bs, bo = outs[0], outs[1 : 1 + chips], outs[1 + chips :]
    bos = [to_core(x) for x in bo]

    dkv = total(dkv, to_core(dkv_other)).astype(BF16)
    gp = total(dkv[0], *[to_z[k](dkv[k]) for k in far]).astype(BF16)

    *bos, gp = lax.optimization_barrier((*bos, gp))
    sent = add_all(bs, bos, "self_add")
    parts = sent[:1] + [to_z[k](sent[k]) for k in far]

    (self_part,) = call(
        functools.partial(self_grad_kernel, chips, dps),
        [((dps, 5 * width + dps * PAD, cut), BF16)],
        idx,
        tokens,
        normed_one,
        gt,
        near,
        gp,
        stat_a,
        *bs,
        *bo,
        scratch=[
            pltpu.VMEM((cores, own, dim), BF16),
            pltpu.SemaphoreType.DMA((cores,)),
        ],
        raw=tuple(range(6, 6 + cores)),
        after=sent[:1],
        stage=True,
        name="self_grad",
    )
    self_part, row_swap, mlp_all, parts[1:3] = lax.optimization_barrier(
        (self_part, row_swap, mlp_all, parts[1:3])
    )
    self_swap = swap_dp(self_part)
    row_piece = sum_dp(row_swap).reshape(chips, 3 * width, cut)
    row_parts = [row_piece[0]] + [to_z[k](row_piece[k]) for k in far]
    row_parts, self_swap = lax.optimization_barrier((row_parts, self_swap))
    row_piece = total(*row_parts).astype(BF16)
    self_sum = sum_dp(self_swap)
    piece = jnp.concatenate([row_piece, self_sum[: 5 * width]], 0)
    swapped = share_dp(piece)
    (grad_tokens,) = call(
        token_kernel,
        [((own, dim), F32)],
        idx,
        tokens,
        norm_gain,
        gf,
        *parts,
        scratch=[pltpu.VMEM((own, dim), BF16), pltpu.SemaphoreType.DMA],
        raw=(0,),
        stage=True,
        name="tokens",
    )
    state_part = jnp.einsum("cse,cde->sd", gp, cross_pair, preferred_element_type=F32)
    held = self_sum[5 * width :].reshape(dps, PAD, cut)
    held = jnp.concatenate([held[c] for c in range(dps)], 1)
    state_part = jnp.concatenate([state_part.astype(BF16), held], 0)
    core = lax.rem(me, 2)
    half_of = lambda c: lax.dynamic_slice_in_dim(state_part, c * (dim // 2), dim // 2, 1)
    state_half = total(half_of(core), to_core(half_of(1 - core))).astype(BF16)
    state_half = total(state_half, *[to_z[k](state_half) for k in far])
    state_sum = jnp.zeros((state_part.shape[0], dim), F32)
    for c, part in ((core, state_half), (1 - core, to_core(state_half))):
        state_sum = lax.dynamic_update_slice(state_sum, part, (0, c * (dim // 2)))
    grad_states = lax.dynamic_update_slice(
        jnp.zeros(states.shape, F32), state_sum[None, :SEEN], (state_row[0], begin, 0)
    )
    stats = state_sum[SEEN:]

    def place(pieces, plan, shapes, name):
        return call(
            functools.partial(place_kernel, plan),
            [(s, F32) for s in shapes],
            idx,
            *pieces,
            stage=True,
            name=name,
        )

    block_output = (second + total(*mlp_parts) + output_bias.astype(F32)).astype(BF16)
    grad_output_weight, grad_hidden_weight = place(
        mlp_all, ((hid, None, False), (hid, None, True)), ((hid, dim), (dim, hid)), "place_mlp"
    )
    swapped, block_output, grad_output_weight, grad_tokens, state_sum = lax.optimization_barrier(
        (swapped, block_output, grad_output_weight, grad_tokens, state_sum)
    )
    (
        grad_self_output,
        grad_cross_query,
        grad_cross_output,
        grad_self_weight,
        grad_cross_pair,
    ) = place(
        [swapped],
        (
            (width, None, False),
            (width, None, True),
            (width, None, False),
            (3 * width, 3, True),
            (2 * width, 2, True),
        ),
        (
            (width, dim),
            (dim, width),
            (width, dim),
            (3, dim, width),
            (2, dim, width),
        ),
        "place",
    )
    grad_norm_gain = jnp.stack([stats[0], stats[4], stats[2]])
    grad_norm_shift = jnp.stack([stats[1], stats[5], stats[3]])
    grad_output_bias = stats[6]
    grad_hidden_bias = jnp.sum(mlp_swap[:, 2 * hid : 2 * hid + hid // cut].astype(F32), 0).reshape(hid)
    return (
        block_output,
        grad_tokens,
        grad_states,
        grad_self_weight,
        grad_self_output,
        grad_cross_query,
        grad_cross_pair,
        grad_cross_output,
        grad_hidden_weight,
        grad_hidden_bias,
        grad_output_weight,
        grad_output_bias,
        grad_norm_gain,
        grad_norm_shift,
    )


def solution(mesh):
    placed = (
        P("dp", None),
        P("dp", None, None),
        P("dp", None),
        P(None, None, "mp"),
        P("mp", None),
        P(None, "mp"),
        P(None, None, "mp"),
        P("mp", None),
        P(None, "mp"),
        P("mp"),
        P("mp", None),
        P(),
        P(),
        P(),
        P("dp"),
        P("dp", None),
        P("dp"),
    )
    return jax.shard_map(
        body,
        mesh=mesh,
        in_specs=placed,
        out_specs=(
            P(("dp", "mp"), None),
            P(("dp", "mp"), None),
            P("dp", None, None),
            P(None, None, "mp"),
            P("mp", None),
            P(None, "mp"),
            P(None, None, "mp"),
            P("mp", None),
            P(None, "mp"),
            P("mp"),
            P("mp", None),
            P(),
            P(),
            P(),
        ),
        check_vma=False,
    )
```

```python
import functools
import math

import jax
import jax.numpy as jnp
from jax import lax
from jax.experimental import pallas as pl
from jax.experimental.pallas import tpu as pltpu
from jax.sharding import PartitionSpec as P

HDIM = 64
SEEN = 64
QB = 256
PAD = 16
EPSILON = 1e-05
NEG_FILL = -1e30
SCALE = HDIM ** (-0.5)
F32 = jnp.float32
BF16 = jnp.bfloat16


def dot_nn(a, b):
    return lax.dot_general(a, b, (((1,), (0,)), ((), ())), preferred_element_type=F32)


def dot_nt(a, b):
    return lax.dot_general(a, b, (((1,), (1,)), ((), ())), preferred_element_type=F32)


def dot_tn(a, b):
    return lax.dot_general(a, b, (((0,), (0,)), ((), ())), preferred_element_type=F32)


def normalize(resid):
    center = resid - jnp.mean(resid, -1, keepdims=True)
    inverse = lax.rsqrt(jnp.mean(center * center, -1, keepdims=True) + EPSILON)
    return (center * inverse, inverse)


def norm_backward(standard, inverse, grad_normed, gain):
    scaled = grad_normed * gain
    return inverse * (
        scaled
        - jnp.mean(scaled, -1, keepdims=True)
        - standard * jnp.mean(scaled * standard, -1, keepdims=True)
    )


def at(index, size):
    return pl.ds(pl.multiple_of(index * size, size), size)


def staged(kernel, ins, outs, extra, *refs):
    count_in, count_out = len(ins), len(outs)
    idx, refs = refs[0], list(refs[1:])
    inner = refs[: count_in + count_out]
    own = refs[count_in + count_out : count_in + count_out + extra]
    rest = refs[count_in + count_out + extra :]
    sem_in, sem_out = rest[-2:]
    held = iter(rest[:-2])
    started, results = [], []
    for i, here in enumerate(ins):
        if here:
            local = next(held)
            started.append(pltpu.make_async_copy(inner[i], local, sem_in.at[len(started)]))
            inner[i] = local
    for i, here in enumerate(outs):
        if here:
            local = next(held)
            target = inner[count_in + i]
            results.append(pltpu.make_async_copy(local, target, sem_out.at[len(results)]))
            inner[count_in + i] = local
    for copy in started:
        copy.start()
    for copy in started:
        copy.wait()
    kernel(idx, *inner, *own)
    for copy in results:
        copy.start()
    for copy in results:
        copy.wait()


def call(
    kernel, outs, idx, *args, scratch=(), after=(), stage=False, tight=False, raw=(), near=(), sent=(), cost=1, name=None, spill=8
):
    if after:
        idx = lax.optimization_barrier((idx, *after))[0]
    out_shape = [jax.ShapeDtypeStruct(s, t) for s, t in outs]
    big = lambda a: bool(stage) and a.size >= 1 << 15
    ins_far = [big(a) and i not in raw and i not in near for i, a in enumerate(args)]
    outs_far = [big(a) for a in out_shape]
    vmem = pl.BlockSpec(memory_space=pltpu.VMEM)
    hbm = pl.BlockSpec(memory_space=pltpu.HBM)
    held = spill << 20
    for i, a in enumerate((*args, *out_shape)):
        if i not in raw:
            held += a.size * a.dtype.itemsize
    for a in scratch:
        if len(getattr(a, "shape", ())) > 1 and a.dtype in (F32, BF16):
            held += math.prod(a.shape) * jnp.dtype(a.dtype).itemsize
    out_shape = [pltpu.HBM(a.shape, a.dtype) if i in sent else a for i, a in enumerate(out_shape)]
    scratch = list(scratch)
    if any(ins_far) or any(outs_far):
        kernel = functools.partial(staged, kernel, ins_far, outs_far, len(scratch))
        for a, far in zip((*args, *out_shape), ins_far + outs_far):
            if far:
                scratch.append(pltpu.VMEM(a.shape, a.dtype))
        scratch.append(pltpu.SemaphoreType.DMA((max(1, sum(ins_far)),)))
        scratch.append(pltpu.SemaphoreType.DMA((max(1, sum(outs_far)),)))
    return pl.pallas_call(
        kernel,
        out_shape=out_shape,
        in_specs=[pl.BlockSpec(memory_space=pltpu.SMEM)]
        + [hbm if far or i in raw else vmem for i, far in enumerate(ins_far)],
        out_specs=[hbm if far or i in sent else vmem for i, far in enumerate(outs_far)],
        scratch_shapes=scratch,
        cost_estimate=pl.CostEstimate(flops=cost, bytes_accessed=1, transcendentals=0),
        compiler_params=pltpu.CompilerParams(
            vmem_limit_bytes=min(held, 60 << 20) if tight else 60 << 20
        ),
        name=name,
    )(idx, *args)


def head_select(parts, axis):
    if len(parts) == 1:
        return parts[0]
    head = lax.broadcasted_iota(jnp.int32, parts[0].shape, axis) // HDIM
    return jnp.where(head == 0, parts[0], parts[1])


def head_only(value, h, count):
    if count == 1:
        return value
    head = lax.broadcasted_iota(jnp.int32, value.shape, 1) // HDIM
    return jnp.where(head == h, value, jnp.zeros_like(value))


def self_kernel(
    chips, idx, tok, weight, gain, shift, states, pair, segment, normed, triple, probs, *rest
):
    att_out = rest[:chips]
    val_t, att, kv = rest[chips:]
    rows, width = tok.shape[0], weight.shape[2]
    heads = width // HDIM
    g = gain[0:1, :].astype(F32)
    s = shift[0:1, :].astype(F32)

    def project(i, carry):
        here = at(i, QB)
        standard, _ = normalize(tok[here, :].astype(F32))
        n = (standard * g + s).astype(BF16)
        normed[here, :] = n
        triple[0, here, :] = dot_nn(n, weight[0]).astype(BF16)
        triple[1, here, :] = dot_nn(n, weight[1]).astype(BF16)
        value = dot_nn(n, weight[2])
        triple[2, here, :] = value.astype(BF16)
        val_t[:, here] = value.T.astype(BF16)
        return carry

    lax.fori_loop(0, rows // QB, project, 0)
    for i in range(rows // QB):
        here = slice(i * QB, (i + 1) * QB)
        query = triple[0, here, :]
        seen = (i + 1) * QB
        outs = []
        for h in range(heads):
            scores = dot_nt(triple[1, 0:seen, :], head_only(query, h, heads)) * SCALE
            key_at = lax.broadcasted_iota(jnp.int32, scores.shape, 0)
            row_at = lax.broadcasted_iota(jnp.int32, scores.shape, 1) + i * QB
            scores = jnp.where(key_at <= row_at, scores, NEG_FILL)
            e = jnp.exp(scores - jnp.max(scores, 0, keepdims=True))
            p = (e * (1.0 / jnp.sum(e, 0, keepdims=True))).astype(BF16)
            probs[h, 0:seen, here] = p
            outs.append(dot_nn(val_t[:, 0:seen], p))
        att[here, :] = head_select(outs, 0).T.astype(BF16)
    own = (att_out[0].shape[0] - 2 * SEEN) // 2
    before = segment[pl.ds(idx[2], 1), :] < idx[3]
    begin = jnp.minimum(jnp.sum(before.astype(jnp.int32)), states.shape[1] - SEEN)
    for c in range(2):
        kv[...] = dot_nn(states[idx[2]], pair[c])
        for k in range(chips):
            where = slice(2 * own + c * SEEN, 2 * own + (c + 1) * SEEN)
            att_out[k][where, :] = kv[pl.ds(begin, SEEN), :].astype(BF16)
    for k in range(chips):
        for cc in range(2):
            att_out[k][cc * own : (cc + 1) * own, :] = att[at(idx[0] ^ (2 * k + cc), own), :]


def pair_tiles(block, heads):
    return jnp.concatenate([head_only(block, h, heads) for h in range(heads)], 0)


def half_reduce(op, value, heads, fill):
    if heads == 1:
        return op(value, -1, keepdims=True)
    half = lax.broadcasted_iota(jnp.int32, value.shape, 1) // SEEN
    first = op(jnp.where(half == 0, value, fill), -1, keepdims=True)
    other = op(jnp.where(half == 1, value, fill), -1, keepdims=True)
    return jnp.where(half == 0, first, other)


def fetch_weights(chips, dps, idx, weights, wf, sem):
    width = wf.shape[1] // (2 * chips)
    cut = wf.shape[2] // dps
    span = (chips - 1) * width
    half = chips * width
    lists = []
    for m in range(3):
        copies = []
        for cc in range(2):
            source = weights[cc * (dps + 1)]
            where = wf.at[m, cc * half : cc * half + width, :]
            copies.append((source.at[m * width : (m + 1) * width, :], where))
            for q in range(dps):
                source = weights[cc * (dps + 1) + 1 + q]
                cols = at(idx[1] ^ q, cut)
                where = wf.at[m, cc * half + width : (cc + 1) * half, cols]
                copies.append((source.at[m * span : (m + 1) * span, :], where))
        lists.append(
            [pltpu.make_async_copy(s, d, sem.at[m, i]) for i, (s, d) in enumerate(copies)]
        )
    return lists


def own_rows(idx, source, rows, sem):
    copy = pltpu.make_async_copy(source.at[at(idx[0], rows.shape[0]), :], rows, sem)
    copy.start()
    return copy


def cross_kernel(chips, dps, idx, tokens, gain, shift, seen, *rest):
    take = iter(rest)
    pull = lambda n: [next(take) for _ in range(n)]
    weights = pull(2 * dps + 2)
    att_in = [pull(chips), pull(chips)]
    first_o, pack_o, q_o, cp_o, second_o, n3_o = pull(6)
    wf, sem, tok, tok_sem = pull(4)
    fetch = own_rows(idx, tokens, tok, tok_sem)
    own, dim = tok.shape
    width = wf.shape[1] // (2 * chips)
    heads = width // HDIM
    half = chips * width
    copies = fetch_weights(chips, dps, idx, weights, wf, sem)
    for each in copies:
        for copy in each:
            copy.start()
    for k in range(chips):
        pack_o[0, :, k * width : (k + 1) * width] = att_in[0][k][0:own, :]
        pack_o[0, :, half + k * width : half + (k + 1) * width] = att_in[1][k][own : 2 * own, :]
    fetch.wait()
    for copy in copies[0]:
        copy.wait()
    resid = tok[...].astype(F32) + dot_nn(pack_o[0], wf[0])
    first_o[...] = resid
    n2 = (normalize(resid)[0] * gain[1:2, :].astype(F32) + shift[1:2, :].astype(F32)).astype(BF16)
    pack_o[1, :, :] = n2
    for copy in copies[1]:
        copy.wait()
    q_o[...] = dot_nt(n2, wf[1]).astype(BF16)
    allowed = seen[...] > 0
    for cc in range(2):
        for k in range(chips):
            b = cc * chips + k
            lanes = slice(b * width, (b + 1) * width)
            keys = pair_tiles(att_in[cc][k][2 * own : 2 * own + SEEN, :], heads)
            values = pair_tiles(att_in[cc][k][2 * own + SEEN :, :], heads)
            scores = dot_nt(q_o[:, lanes], keys) * SCALE
            scores = jnp.where(allowed, scores, NEG_FILL)
            e = jnp.exp(scores - half_reduce(jnp.max, scores, heads, NEG_FILL))
            p = (e * (1.0 / half_reduce(jnp.sum, e, heads, 0.0))).astype(BF16)
            cp_o[b] = p
            pack_o[2, :, lanes] = dot_nn(p, values).astype(BF16)
    for copy in copies[2]:
        copy.wait()
    resid = resid + dot_nn(pack_o[2], wf[2])
    second_o[...] = resid
    n3 = normalize(resid)[0] * gain[2:3, :].astype(F32) + shift[2:3, :].astype(F32)
    n3_o[...] = n3.astype(BF16)


def active_kernel(chips, idx, cot, weight, *rest):
    outs, part = rest[:chips], rest[chips]
    rows = outs[0].shape[0]

    def chip(k, carry):
        part[k] = dot_nt(cot[at((idx[0] // 2) ^ k, rows), :], weight[...])
        return carry

    lax.fori_loop(0, chips, chip, 0)
    for k in range(chips):
        outs[k][...] = part[k]


def hidden_kernel(idx, same, other, weight, bias, grad_active, *rest):
    n3_h, act_h, ghi_h, bs_o, bo_o, back, n3_o, act_o, ghi_o, sem = rest
    own = same.shape[0]
    core = lax.rem(idx[0], 2)
    pairs = ((n3_o, n3_h), (act_o, act_h), (ghi_o, ghi_h))
    keep = [pltpu.make_async_copy(a, b, sem.at[i]) for i, (a, b) in enumerate(pairs)]
    n3_o[at(core, own), :] = same[...]
    n3_o[at(1 - core, own), :] = other[...]
    keep[0].start()
    v = dot_nn(n3_o[...], weight[...]) + bias[...].astype(F32)
    root = 0.7978845608028654
    square = v * v
    t = jnp.tanh(root * v * (1.0 + 0.044715 * square))
    act_o[...] = (0.5 * v * (1.0 + t)).astype(BF16)
    slope = 0.5 * (1.0 + t) + 0.5 * v * (1.0 - t * t) * (root * (1.0 + 0.134145 * square))
    ghi = (grad_active[...] * slope).astype(BF16)
    ghi_o[...] = ghi
    keep[1].start()
    keep[2].start()
    back[...] = dot_nt(ghi, weight[...])
    bs_o[...] = back[at(core, own), :].astype(BF16)
    dim = back.shape[1]
    bo_o[:, 0:dim] = back[at(1 - core, own), :].astype(BF16)
    bo_o[:, dim:] = act_o[at(1 - core, own), :]
    for copy in keep:
        copy.wait()


def mlp_out_kernel(chips, idx, weight, weight2, *rest):
    acts, others, outs = rest[:chips], rest[chips : 2 * chips], rest[2 * chips : 3 * chips]
    near, part, sem = rest[3 * chips :]
    own, dim = outs[0].shape
    hid = weight.shape[0]
    mine = at(lax.rem(idx[0], 2), own)
    copies = []
    for k in range(chips):
        sources = acts[k].at[mine, :], others[k].at[:, dim : dim + hid]
        for c, source in enumerate(sources):
            copies.append(pltpu.make_async_copy(source, near.at[c, k], sem.at[c, k]))
    for copy in copies:
        copy.start()
    for copy in copies:
        copy.wait()

    def chip(k, carry):
        value = dot_nn(near[0, k], weight[...]) + dot_nn(near[1, k], weight2[...])
        part[k] = value.astype(BF16)
        return carry

    lax.fori_loop(0, chips, chip, 0)
    for k in range(chips):
        outs[k][...] = part[k]


def mlp_grad_kernel(chips, idx, cot, *rest):
    acts = rest[:chips]
    ghis = rest[chips : 2 * chips]
    n3s = rest[2 * chips : 3 * chips]
    out, act, ghi, n3 = rest[3 * chips :]
    step = acts[0].shape[0]
    hid = acts[0].shape[1]
    dps, _, cut = out.shape
    total = jnp.zeros((1, hid), F32)
    for k in range(chips):
        rows = at((idx[0] // 2) ^ k, step)
        act[rows, :] = acts[k][...]
        ghi[rows, :] = ghis[k][...]
        n3[rows, :] = n3s[k][...]
        total += jnp.sum(ghis[k][...].astype(F32), 0, keepdims=True)
    row = lax.broadcasted_iota(jnp.int32, (PAD, cut), 0)
    bias = jnp.zeros((PAD, cut), F32)
    for j in range(hid // cut):
        bias = jnp.where(row == j, total[:, j * cut : (j + 1) * cut], bias)
    def columns(q, carry):
        cols = at(q, cut)
        out[q, 0:hid, :] = dot_tn(act[...], cot[:, cols]).astype(BF16)
        out[q, hid : 2 * hid, :] = dot_tn(ghi[...], n3[:, cols]).astype(BF16)
        out[q, 2 * hid : 2 * hid + PAD, :] = bias.astype(BF16)
        return carry

    lax.fori_loop(0, dps, columns, 0)


def cross_back_kernel(chips, dps, count, idx, cotangent, gain, second, first, cp, q, *rest):
    take = iter(rest)
    pull = lambda n: [next(take) for _ in range(n)]
    weights = pull(2 * dps + 2)
    parts = pull(count)
    kv = [pull(chips), pull(chips)]
    pack_o, gf_o, stat_o, same_o, other_o = pull(5)
    gt_o = pull(chips)
    gc, wf, sem, cot, cot_sem = pull(5)
    fetch = own_rows(idx, cotangent, cot, cot_sem)
    copies = fetch_weights(chips, dps, idx, weights, wf, sem)
    for each in reversed(copies):
        for copy in each:
            copy.start()
    dkv_o = (same_o, other_o)
    own = cot.shape[0]
    width = kv[0][0].shape[1]
    heads = width // HDIM
    grad_normed = parts[0][...].astype(F32)
    for part in parts[1:]:
        grad_normed += part[...].astype(F32)
    fetch.wait()
    c = cot[...].astype(F32)
    standard, inverse = normalize(second[...])
    grad = c + norm_backward(standard, inverse, grad_normed, gain[2:3, :].astype(F32))
    stat_o[0:1, :] = jnp.sum(grad_normed * standard, 0, keepdims=True)
    stat_o[1:2, :] = jnp.sum(grad_normed, 0, keepdims=True)
    stat_o[4:5, :] = jnp.sum(c, 0, keepdims=True)
    g2 = grad.astype(BF16)
    pack_o[2, :, :] = g2
    for copy in copies[2]:
        copy.wait()
    gc[...] = dot_nt(g2, wf[2]).astype(BF16)
    for cc in range(2):
        for k in range(chips):
            b = cc * chips + k
            lanes = slice(b * width, (b + 1) * width)
            keys = pair_tiles(kv[cc][k][2 * own : 2 * own + SEEN, :], heads)
            values = pair_tiles(kv[cc][k][2 * own + SEEN :, :], heads)
            gcb = gc[:, lanes]
            dp = dot_nt(gcb, values)
            low = cp[b]
            p = low.astype(F32)
            inner = half_reduce(jnp.sum, dp * p, heads, 0.0)
            ds = (p * (dp - inner) * SCALE).astype(BF16)
            pack_o[1, :, lanes] = dot_nn(ds, keys).astype(BF16)
            dk = dot_tn(ds, q[:, lanes])
            dv = dot_tn(low, gcb)
            for i, d in enumerate((dk, dv)):
                fold = head_select([d[h * SEEN : (h + 1) * SEEN, :] for h in range(heads)], 1)
                dkv_o[cc][k, i, :, :] = fold.astype(BF16)
    for copy in copies[1]:
        copy.wait()
    grad_normed = dot_nn(pack_o[1], wf[1])
    standard, inverse = normalize(first[...])
    grad = grad + norm_backward(standard, inverse, grad_normed, gain[1:2, :].astype(F32))
    stat_o[2:3, :] = jnp.sum(grad_normed * standard, 0, keepdims=True)
    stat_o[3:4, :] = jnp.sum(grad_normed, 0, keepdims=True)
    gf_o[...] = grad
    g1 = grad.astype(BF16)
    pack_o[0, :, :] = g1
    for copy in copies[0]:
        copy.wait()
    gatt = dot_nt(g1, wf[0]).astype(BF16)
    for cc in range(2):
        for k in range(chips):
            b = cc * chips + k
            gt_o[k][cc, :, :] = gatt[:, b * width : (b + 1) * width]


def row_grad_kernel(chips, idx, fwd, fwd2, bwd, bwd2, out, left, right):
    dps, height, cut = out.shape
    width = height // (3 * chips)
    own = fwd.shape[1]
    half = chips * width
    for m, (l, r) in enumerate((((fwd, fwd2), (bwd, bwd2)), ((bwd, bwd2), (fwd, fwd2)), ((fwd, fwd2), (bwd, bwd2)))):
        left[0:own, :] = l[0][m, :, 0:half]
        left[own : 2 * own, :] = l[1][m, :, half : 2 * half]
        right[0:own, :] = r[0][m]
        right[own : 2 * own, :] = r[1][m]
        for q in range(dps):
            part = dot_tn(left[...], right[:, q * cut : (q + 1) * cut]).astype(BF16)
            for k in range(chips):
                row = (3 * k + m) * width
                out[q, row : row + width, :] = part[k * width : (k + 1) * width, :]


def pack_kernel(idx, *refs):
    parts, out = refs[:-1], refs[-1]
    width = parts[0].shape[0] // 3
    for m in range(3):
        for k, part in enumerate(parts):
            row = (m * len(parts) + k) * width
            out[row : row + width, :] = part[m * width : (m + 1) * width, :]


def self_back_kernel(chips, idx, triple, probs, weight, *rest):
    take = iter(rest)
    pull = lambda n: [next(take) for _ in range(n)]
    grads = [pull(chips), pull(chips)]
    (gt_o,) = pull(1)
    bs_o, bo_o = pull(chips), pull(chips)
    gout, key_t, wcat, dq, dk, dv, back = pull(7)
    rows, width = triple.shape[1], triple.shape[2]
    heads = width // HDIM
    own = bs_o[0].shape[0]
    for k in range(chips):
        gout[at(idx[0] ^ (2 * k), own), :] = grads[0][k][0]
        gout[at(idx[0] ^ (2 * k + 1), own), :] = grads[1][k][1]
    for c in range(3):
        wcat[:, c * width : (c + 1) * width] = weight[c]
    count = rows // QB
    for i in range(count):
        here = slice(i * QB, (i + 1) * QB)
        key_t[:, here] = triple[1, here, :].astype(F32).T.astype(BF16)
    dk[...] = jnp.zeros(dk.shape, F32)
    dv[...] = jnp.zeros(dv.shape, F32)

    def one_head(h, carry):
        for i in reversed(range(count)):
            here = slice(i * QB, (i + 1) * QB)
            seen = (i + 1) * QB
            go = head_only(gout[here, :], h, heads)
            query = head_only(triple[0, here, :], h, heads)
            dp = dot_nt(triple[2, 0:seen, :], go)
            low = probs[h, 0:seen, here]
            p = low.astype(F32)
            inner = jnp.sum(dp * p, 0, keepdims=True)
            ds = (p * (dp - inner) * SCALE).astype(BF16)
            dk[0:seen, :] += dot_nn(ds, query)
            dv[0:seen, :] += dot_nn(low, go)
            new_q = dot_nn(key_t[:, 0:seen], ds)
            head = lax.broadcasted_iota(jnp.int32, new_q.shape, 0) // HDIM
            dq[:, here] = jnp.where(head == h, new_q, dq[:, here])
        return carry

    lax.fori_loop(0, heads, one_head, 0)
    for i in range(count):
        here = slice(i * QB, (i + 1) * QB)
        gt_o[here, 0:width] = dq[:, here].T.astype(BF16)
        gt_o[here, width : 2 * width] = dk[here, :].astype(BF16)
        gt_o[here, 2 * width : 3 * width] = dv[here, :].astype(BF16)

    def project(i, carry):
        back[at(i, QB), :] = dot_nt(gt_o[at(i, QB), :], wcat[...]).astype(BF16)
        return carry

    lax.fori_loop(0, count, project, 0)
    for k in range(chips):
        bs_o[k][...] = back[at(idx[0] ^ (2 * k), own), :]
        bo_o[k][...] = back[at(idx[0] ^ (2 * k + 1), own), :]


def self_grad_kernel(chips, dps, idx, tok, normed, gt, states, gp, stat, *rest):
    parts, (out, held, sem) = rest[: 2 * chips], rest[2 * chips :]
    cut = out.shape[2]
    width = gp.shape[2]
    own = held.shape[1]
    copies = []
    for k in range(chips):
        for cc in range(2):
            j = 2 * k + cc
            copies.append(pltpu.make_async_copy(parts[cc * chips + k], held.at[j], sem.at[j]))
    for copy in copies:
        copy.start()

    def columns(q, carry):
        cols = at(q, cut)
        out[q, 0 : 3 * width, :] = dot_tn(gt[...], normed[:, cols]).astype(BF16)
        for c in range(2):
            out[q, (3 + c) * width : (4 + c) * width, :] = dot_tn(
                gp[c], states[:, cols]
            ).astype(BF16)
        return carry

    lax.fori_loop(0, dps, columns, 0)
    for copy in copies:
        copy.wait()

    def add_rows(j, carry):
        g = held[j].astype(F32)
        standard, _ = normalize(tok[at(idx[0] ^ j, own), :].astype(F32))
        gain = carry[0] + jnp.sum(g * standard, 0, keepdims=True)
        return gain, carry[1] + jnp.sum(g, 0, keepdims=True)

    none = jnp.zeros((1, tok.shape[1]), F32)
    gain, shift = lax.fori_loop(0, 2 * chips, add_rows, (none, none))
    row = lax.broadcasted_iota(jnp.int32, (PAD, tok.shape[1]), 0)
    both = jnp.where(row == 0, gain, jnp.where(row == 1, shift, 0.0))
    for i in range(5):
        both = jnp.where(row == i + 2, stat[i : i + 1, :], both)
    both = both.astype(BF16)
    for q in range(dps):
        for c in range(dps):
            here = slice(5 * width + c * PAD, 5 * width + (c + 1) * PAD)
            out[q, here, :] = both[:, c * cut : (c + 1) * cut]


def add_kernel(idx, *refs):
    count = len(refs) // 3
    step = math.gcd(refs[0].shape[0], 32)

    def add_rows(i, carry):
        here = at(i, step)
        for k in range(count):
            total = refs[k][here, :].astype(F32) + refs[count + k][here, :].astype(F32)
            refs[2 * count + k][here, :] = total.astype(BF16)
        return carry

    lax.fori_loop(0, refs[0].shape[0] // step, add_rows, 0)


def sum_kernel(idx, pieces, out):
    step = math.gcd(out.shape[0], 64)

    def add_rows(i, carry):
        here = at(i, step)
        out[here, :] = jnp.sum(pieces[:, here, :].astype(F32), 0).astype(BF16)
        return carry

    lax.fori_loop(0, out.shape[0] // step, add_rows, 0)


def token_kernel(idx, tokens, gain, grad, *rest):
    parts, (out, tok, sem) = rest[:-3], rest[-3:]
    own_rows(idx, tokens, tok, sem).wait()
    grad_normed = parts[0][...].astype(F32)
    for part in parts[1:]:
        grad_normed += part[...].astype(F32)
    standard, inverse = normalize(tok[...].astype(F32))
    out[...] = grad[...] + norm_backward(standard, inverse, grad_normed, gain[0:1, :].astype(F32))


def place_kernel(plan, idx, *refs):
    parts, outs = refs[: -len(plan)], refs[-len(plan) :]
    if len(parts) == 1:
        source = parts[0]
        count, _, cut = source.shape
        take = lambda q, rows: source[q, rows, :]
        where_of = lambda q: slice(q * cut, (q + 1) * cut)
    else:
        count, cut = len(parts), parts[0].shape[1]
        take = lambda q, rows: parts[q][rows, :]
        where_of = lambda q: at(idx[1] ^ q, cut)
    row = 0
    for out, (height, lead, flip) in zip(outs, plan):
        for q in range(count):
            where = where_of(q)
            piece = take(q, slice(row, row + height)).astype(F32)
            if not flip:
                out[:, where] = piece
            elif lead is None:
                out[where, :] = piece.T
            else:
                step = height // lead
                for c in range(lead):
                    out[c, where, :] = piece[c * step : (c + 1) * step, :].T
        row += height


def flip_bits(axis, bits, size):
    return functools.partial(
        lax.ppermute, axis_name=axis, perm=[(i, i ^ bits) for i in range(size)]
    )


def total(*parts):
    out = parts[0].astype(F32)
    for part in parts[1:]:
        out = out + part.astype(F32)
    return out


def body(
    tokens,
    states,
    cotangent,
    self_weight,
    self_output,
    cross_query,
    cross_pair,
    cross_output,
    hidden_weight,
    hidden_bias,
    output_weight,
    output_bias,
    norm_gain,
    norm_shift,
    state_row,
    state_segment,
    caption,
):
    rows, dim = tokens.shape
    width = cross_query.shape[1]
    heads = width // HDIM
    hid = hidden_bias.shape[0]
    cores = lax.axis_size("mp")
    chips = cores // 2
    dps = lax.axis_size("dp")
    own = rows // cores
    cut = dim // dps
    me = lax.axis_index("mp")
    dpi = lax.axis_index("dp")
    idx = jnp.stack([me, dpi, state_row[0], caption[0]]).astype(jnp.int32)
    to_z = [flip_bits("mp", 2 * k, cores) for k in range(chips)]
    to_core = flip_bits("mp", 1, cores)
    to_dp = [flip_bits("dp", q, dps) for q in range(dps)]
    far = range(1, chips)
    peers = range(1, dps)

    def share_dp(piece):
        return lax.all_to_all(jnp.broadcast_to(piece[None], (dps,) + piece.shape), "dp", 0, 0)

    def add_all(left, right, name):
        return list(
            call(
            add_kernel,
            [((own, dim), BF16)] * chips,
            idx,
            *left,
            *right,
            stage=True,
            name=name,
        ))

    def swap_dp(pieces):
        return lax.all_to_all(pieces, "dp", 0, 0)

    def sum_dp(pieces):
        return jnp.sum(pieces.astype(F32), 0).astype(BF16)

    labels = lax.dynamic_index_in_dim(state_segment, state_row[0], 0, False)
    begin = jnp.minimum(jnp.sum((labels < caption[0]).astype(jnp.int32)), labels.shape[0] - SEEN)
    labels = lax.dynamic_slice_in_dim(labels, begin, SEEN, 0)
    seen = jnp.tile((labels == caption[0]).astype(jnp.int32)[None, :], (1, heads))
    near = lax.dynamic_slice(states, (state_row[0], begin, 0), (1, SEEN, dim))[0]

    mine = jnp.concatenate([self_output, cross_query.T, cross_output], 0)
    piece = lax.dynamic_slice_in_dim(mine, dpi * cut, cut, 1)
    got = [to_z[k](piece) for k in far]
    output_weight2 = to_core(output_weight)

    outs = call(
        functools.partial(self_kernel, chips),
        [
            ((rows, dim), BF16),
            ((3, rows, width), BF16),
            ((heads, rows, rows), BF16),
        ]
        + [((2 * own + 2 * SEEN, width), BF16)] * chips,
        idx,
        tokens,
        self_weight,
        norm_gain,
        norm_shift,
        states,
        cross_pair,
        state_segment,
        scratch=[
            pltpu.VMEM((width, rows), BF16),
            pltpu.VMEM((rows, width), BF16),
            pltpu.VMEM((states.shape[1], width), F32),
        ],
        after=(piece,),
        stage=True,
        name="self_fwd",
    )
    normed_one, triple, probs = outs[:3]
    att = outs[3:]
    *got, output_weight2, _ = lax.optimization_barrier((*got, output_weight2, att[0]))
    (cat,) = call(pack_kernel, [((3 * width * (chips - 1), cut), BF16)], idx, *got, tight=True, name="pack")
    att = [att[0]] + [to_z[k](att[k]) for k in far]
    att2 = [to_core(x) for x in att]

    grad_active = call(
        functools.partial(active_kernel, chips),
        [((2 * own, hid), F32)] * chips,
        idx,
        cotangent,
        output_weight,
        scratch=[pltpu.VMEM((chips, 2 * own, hid), F32)],
        after=att[:1],
        stage=True,
        name="grad_active",
    )

    cats = [cat] + [to_dp[q](cat) for q in peers]
    cats, grad_active, seen = lax.optimization_barrier((cats, grad_active, seen))
    weights = [mine, *cats, to_core(mine), *[to_core(x) for x in cats]]

    sq = cores * width
    first, fwd, q, cp, second, n3 = call(
        functools.partial(cross_kernel, chips, dps),
        [
            ((own, dim), F32),
            ((3, own, dim), BF16),
            ((own, sq), BF16),
            ((cores, own, heads * SEEN), BF16),
            ((own, dim), F32),
            ((own, dim), BF16),
        ],
        idx,
        tokens,
        norm_gain,
        norm_shift,
        seen,
        *weights,
        *att,
        *att2,
        scratch=[
            pltpu.VMEM((3, sq, dim), BF16),
            pltpu.SemaphoreType.DMA((3, 2 * dps + 2)),
            pltpu.VMEM((own, dim), BF16),
            pltpu.SemaphoreType.DMA,
        ],
        raw=(0, *range(4, 4 + len(weights))),
        stage=True,
        name="cross_fwd",
    )

    relay = chips == 4
    order = (0, 1, 3, 2) if relay else range(chips)
    n3s = [n3] + [None if relay and k == 2 else to_z[k](n3) for k in far]
    fwd2 = to_core(fwd)
    bias_row = hidden_bias[None, :]
    acts, ghis, chunks, sent, others = ([None] * chips for _ in range(5))
    done = ()
    for k in order:
        arrived = n3s[k]
        chunk, act, ghi, bs, bo = call(
            hidden_kernel,
            [
                ((2 * own, dim), BF16),
                ((2 * own, hid), BF16),
                ((2 * own, hid), BF16),
                ((own, dim), BF16),
                ((own, dim + hid), BF16),
            ],
            idx,
            arrived,
            to_core(arrived),
            hidden_weight,
            bias_row,
            grad_active[k],
            scratch=[
                pltpu.VMEM((2 * own, dim), F32),
                pltpu.VMEM((2 * own, dim), BF16),
                pltpu.VMEM((2 * own, hid), BF16),
                pltpu.VMEM((2 * own, hid), BF16),
                pltpu.SemaphoreType.DMA((3,)),
            ],
            sent=(0, 1, 2),
            after=done,
            tight=True,
            name="hidden",
        )
        done = (act,)
        acts[k], ghis[k], chunks[k] = act, ghi, chunk
        others[k] = to_core(bo)
        sent[k] = total(bs, others[k][:, :dim]).astype(BF16)
        if k == 0:
            *n3s, _ = lax.optimization_barrier((*n3s, act))
            if relay:
                n3s[2] = to_z[1](n3s[3])
    backs = sent[:1] + [to_z[k](sent[k]) for k in range(1, 2 if relay else chips)]
    if relay:
        sent[2] = total(sent[2], to_z[1](sent[3])).astype(BF16)
        backs.append(to_z[2](sent[2]))
    (mlp_grad,) = call(
        functools.partial(mlp_grad_kernel, chips),
        [((dps, 2 * hid + PAD, cut), BF16)],
        idx,
        cotangent,
        *acts,
        *ghis,
        *chunks,
        scratch=[
            pltpu.VMEM((rows, hid), BF16),
            pltpu.VMEM((rows, hid), BF16),
            pltpu.VMEM((rows, dim), BF16),
        ],
        after=sent,
        stage=True,
        name="mlp_grad",
    )
    mlp_grad, backs[1] = lax.optimization_barrier((mlp_grad, backs[1]))
    mlp_swap = swap_dp(mlp_grad)
    mlp_part = call(
        functools.partial(mlp_out_kernel, chips),
        [((own, dim), BF16)] * chips,
        idx,
        output_weight,
        output_weight2,
        *acts,
        *others,
        scratch=[
            pltpu.VMEM((2, chips, own, hid), BF16),
            pltpu.VMEM((chips, own, dim), BF16),
            pltpu.SemaphoreType.DMA((2, chips)),
        ],
        raw=tuple(range(2, 2 + 2 * chips)),
        after=(mlp_grad,),
        stage=True,
        name="mlp_out",
    )
    *backs, mlp_part = lax.optimization_barrier((*backs, list(mlp_part)))
    mlp_parts = mlp_part[:1] + [to_z[k](mlp_part[k]) for k in far[:2]]

    outs = call(
        functools.partial(cross_back_kernel, chips, dps, len(backs)),
        [
            ((3, own, dim), BF16),
            ((own, dim), F32),
            ((8, dim), F32),
            ((chips, 2, SEEN, width), BF16),
            ((chips, 2, SEEN, width), BF16),
        ]
        + [((2, own, width), BF16)] * chips,
        idx,
        cotangent,
        norm_gain,
        second,
        first,
        cp,
        q,
        *weights,
        *backs,
        *att,
        *att2,
        scratch=[
            pltpu.VMEM((own, sq), BF16),
            pltpu.VMEM((3, sq, dim), BF16),
            pltpu.SemaphoreType.DMA((3, 2 * dps + 2)),
            pltpu.VMEM((own, dim), BF16),
            pltpu.SemaphoreType.DMA,
        ],
        raw=(0, *range(6, 6 + len(weights))),
        cost=10**12,
        stage=True,
        name="cross_bwd",
    )
    outs, mlp_parts, mlp_swap = lax.optimization_barrier((outs, mlp_parts, mlp_swap))
    mlp_piece = call(
        sum_kernel, [((2 * hid, cut), BF16)], idx, mlp_swap, stage=True, name="sum_mlp"
    )[0]
    mlp_all = [mlp_piece] + [to_dp[q](mlp_piece) for q in (1, 2)]
    bwd, gf, stat_a, dkv, dkv_other = outs[:5]
    gatt = outs[5:]
    gatt = [gatt[0]] + [to_z[k](gatt[k]) for k in far]

    (row_grad,) = call(
        functools.partial(row_grad_kernel, chips),
        [((dps, chips * 3 * width, cut), BF16)],
        idx,
        fwd,
        fwd2,
        bwd,
        to_core(bwd),
        scratch=[pltpu.VMEM((2 * own, chips * width), BF16), pltpu.VMEM((2 * own, dim), BF16)],
        stage=True,
        name="row_grad",
    )
    gatt, row_grad, mlp_all, mlp_part = lax.optimization_barrier(
        (gatt, row_grad, mlp_all, mlp_part)
    )
    mlp_all += [to_dp[q](mlp_all[0]) for q in range(3, dps)]
    gatt2 = [to_core(x) for x in gatt]
    row_swap = swap_dp(row_grad)
    mlp_parts += [to_z[k](mlp_part[k]) for k in far[2:]]

    outs = call(
        functools.partial(self_back_kernel, chips),
        [((rows, 3 * width), BF16)] + [((own, dim), BF16)] * (2 * chips),
        idx,
        triple,
        probs,
        self_weight,
        *gatt,
        *gatt2,
        scratch=[
            pltpu.VMEM((rows, width), BF16),
            pltpu.VMEM((width, rows), BF16),
            pltpu.VMEM((dim, 3 * width), BF16),
            pltpu.VMEM((width, rows), F32),
            pltpu.VMEM((rows, width), F32),
            pltpu.VMEM((rows, width), F32),
            pltpu.VMEM((rows, dim), BF16),
        ],
        cost=10**12,
        stage=True,
        name="self_bwd",
    )
    outs, mlp_parts = lax.optimization_barrier((outs, mlp_parts))
    gt, bs, bo = outs[0], outs[1 : 1 + chips], outs[1 + chips :]
    bos = [to_core(x) for x in bo]

    dkv = total(dkv, to_core(dkv_other)).astype(BF16)
    gp = total(dkv[0], *[to_z[k](dkv[k]) for k in far]).astype(BF16)

    *bos, gp = lax.optimization_barrier((*bos, gp))
    sent = add_all(bs, bos, "self_add")
    parts = sent[:1] + [to_z[k](sent[k]) for k in far[:2]]

    (self_part,) = call(
        functools.partial(self_grad_kernel, chips, dps),
        [((dps, 5 * width + dps * PAD, cut), BF16)],
        idx,
        tokens,
        normed_one,
        gt,
        near,
        gp,
        stat_a,
        *bs,
        *bo,
        scratch=[
            pltpu.VMEM((cores, own, dim), BF16),
            pltpu.SemaphoreType.DMA((cores,)),
        ],
        raw=tuple(range(6, 6 + cores)),
        after=sent[:1],
        stage=True,
        name="self_grad",
    )
    self_part, row_swap, mlp_all, parts[1:3] = lax.optimization_barrier(
        (self_part, row_swap, mlp_all, parts[1:3])
    )
    self_swap = swap_dp(self_part)
    row_piece = sum_dp(row_swap).reshape(chips, 3 * width, cut)
    row_parts = [row_piece[0]] + [to_z[k](row_piece[k]) for k in far]
    row_parts, self_swap, sent = lax.optimization_barrier((row_parts, self_swap, sent))
    parts += [to_z[k](sent[k]) for k in far[2:]]
    row_piece = total(*row_parts).astype(BF16)
    self_sum = sum_dp(self_swap)
    piece = jnp.concatenate([row_piece, self_sum[: 5 * width]], 0)
    swapped = share_dp(piece)
    (grad_tokens,) = call(
        token_kernel,
        [((own, dim), F32)],
        idx,
        tokens,
        norm_gain,
        gf,
        *parts,
        scratch=[pltpu.VMEM((own, dim), BF16), pltpu.SemaphoreType.DMA],
        raw=(0,),
        stage=True,
        name="tokens",
    )
    state_part = jnp.einsum("cse,cde->sd", gp, cross_pair, preferred_element_type=F32)
    held = self_sum[5 * width :].reshape(dps, PAD, cut)
    held = jnp.concatenate([held[c] for c in range(dps)], 1)
    state_part = jnp.concatenate([state_part.astype(BF16), held], 0)
    core = lax.rem(me, 2)
    half_of = lambda c: lax.dynamic_slice_in_dim(state_part, c * (dim // 2), dim // 2, 1)
    state_half = total(half_of(core), to_core(half_of(1 - core))).astype(BF16)
    state_got = [to_z[k](state_half) for k in far]
    def place(pieces, plan, shapes, name, **kept):
        return call(
            functools.partial(place_kernel, plan),
            [(s, F32) for s in shapes],
            idx,
            *pieces,
            stage=True,
            name=name,
            **kept,
        )

    block_output = (second + total(*mlp_parts) + output_bias.astype(F32)).astype(BF16)
    grad_output_weight, grad_hidden_weight = place(
        mlp_all, ((hid, None, False), (hid, None, True)), ((hid, dim), (dim, hid)), "place_mlp"
    )
    state_got, block_output, grad_output_weight, grad_tokens = lax.optimization_barrier(
        (state_got, block_output, grad_output_weight, grad_tokens)
    )
    state_half = total(state_half, *state_got)
    state_sum = jnp.zeros((state_part.shape[0], dim), F32)
    for c, part in ((core, state_half), (1 - core, to_core(state_half))):
        state_sum = lax.dynamic_update_slice(state_sum, part, (0, c * (dim // 2)))
    grad_states = lax.dynamic_update_slice(
        jnp.zeros(states.shape, F32), state_sum[None, :SEEN], (state_row[0], begin, 0)
    )
    stats = state_sum[SEEN:]
    swapped, state_sum = lax.optimization_barrier((swapped, state_sum))
    (
        grad_self_output,
        grad_cross_query,
        grad_cross_output,
        grad_self_weight,
        grad_cross_pair,
    ) = place(
        [swapped],
        (
            (width, None, False),
            (width, None, True),
            (width, None, False),
            (3 * width, 3, True),
            (2 * width, 2, True),
        ),
        (
            (width, dim),
            (dim, width),
            (width, dim),
            (3, dim, width),
            (2, dim, width),
        ),
        "place",
        near=(0,),
        tight=True,
    )
    grad_norm_gain = jnp.stack([stats[0], stats[4], stats[2]])
    grad_norm_shift = jnp.stack([stats[1], stats[5], stats[3]])
    grad_output_bias = stats[6]
    grad_hidden_bias = jnp.sum(mlp_swap[:, 2 * hid : 2 * hid + hid // cut].astype(F32), 0).reshape(hid)
    return (
        block_output,
        grad_tokens,
        grad_states,
        grad_self_weight,
        grad_self_output,
        grad_cross_query,
        grad_cross_pair,
        grad_cross_output,
        grad_hidden_weight,
        grad_hidden_bias,
        grad_output_weight,
        grad_output_bias,
        grad_norm_gain,
        grad_norm_shift,
    )


def solution(mesh):
    placed = (
        P("dp", None),
        P("dp", None, None),
        P("dp", None),
        P(None, None, "mp"),
        P("mp", None),
        P(None, "mp"),
        P(None, None, "mp"),
        P("mp", None),
        P(None, "mp"),
        P("mp"),
        P("mp", None),
        P(),
        P(),
        P(),
        P("dp"),
        P("dp", None),
        P("dp"),
    )
    return jax.shard_map(
        body,
        mesh=mesh,
        in_specs=placed,
        out_specs=(
            P(("dp", "mp"), None),
            P(("dp", "mp"), None),
            P("dp", None, None),
            P(None, None, "mp"),
            P("mp", None),
            P(None, "mp"),
            P(None, None, "mp"),
            P("mp", None),
            P(None, "mp"),
            P("mp"),
            P("mp", None),
            P(),
            P(),
            P(),
        ),
        check_vma=False,
    )
```

```python
import functools
import math

import jax
import jax.numpy as jnp
from jax import lax
from jax.experimental import pallas as pl
from jax.experimental.pallas import tpu as pltpu
from jax.sharding import PartitionSpec as P

HDIM = 64
SEEN = 64
QB = 256
PAD = 16
EPSILON = 1e-05
NEG_FILL = -1e30
SCALE = HDIM ** (-0.5)
F32 = jnp.float32
BF16 = jnp.bfloat16


def dot_nn(a, b):
    return lax.dot_general(a, b, (((1,), (0,)), ((), ())), preferred_element_type=F32)


def dot_nt(a, b):
    return lax.dot_general(a, b, (((1,), (1,)), ((), ())), preferred_element_type=F32)


def dot_tn(a, b):
    return lax.dot_general(a, b, (((0,), (0,)), ((), ())), preferred_element_type=F32)


def normalize(resid):
    center = resid - jnp.mean(resid, -1, keepdims=True)
    inverse = lax.rsqrt(jnp.mean(center * center, -1, keepdims=True) + EPSILON)
    return (center * inverse, inverse)


def norm_backward(standard, inverse, grad_normed, gain):
    scaled = grad_normed * gain
    return inverse * (
        scaled
        - jnp.mean(scaled, -1, keepdims=True)
        - standard * jnp.mean(scaled * standard, -1, keepdims=True)
    )


def at(index, size):
    return pl.ds(pl.multiple_of(index * size, size), size)


def staged(kernel, ins, outs, extra, *refs):
    count_in, count_out = len(ins), len(outs)
    idx, refs = refs[0], list(refs[1:])
    inner = refs[: count_in + count_out]
    own = refs[count_in + count_out : count_in + count_out + extra]
    rest = refs[count_in + count_out + extra :]
    sem_in, sem_out = rest[-2:]
    held = iter(rest[:-2])
    started, results = [], []
    for i, here in enumerate(ins):
        if here:
            local = next(held)
            started.append(pltpu.make_async_copy(inner[i], local, sem_in.at[len(started)]))
            inner[i] = local
    for i, here in enumerate(outs):
        if here:
            local = next(held)
            target = inner[count_in + i]
            results.append(pltpu.make_async_copy(local, target, sem_out.at[len(results)]))
            inner[count_in + i] = local
    for copy in started:
        copy.start()
    for copy in started:
        copy.wait()
    kernel(idx, *inner, *own)
    for copy in results:
        copy.start()
    for copy in results:
        copy.wait()


def call(
    kernel, outs, idx, *args, scratch=(), after=(), stage=False, tight=False, raw=(), near=(), sent=(), cost=1, name=None, spill=8
):
    if after:
        idx = lax.optimization_barrier((idx, *after))[0]
    out_shape = [jax.ShapeDtypeStruct(s, t) for s, t in outs]
    big = lambda a: bool(stage) and a.size >= 1 << 15
    ins_far = [big(a) and i not in raw and i not in near for i, a in enumerate(args)]
    outs_far = [big(a) for a in out_shape]
    vmem = pl.BlockSpec(memory_space=pltpu.VMEM)
    hbm = pl.BlockSpec(memory_space=pltpu.HBM)
    held = spill << 20
    for i, a in enumerate((*args, *out_shape)):
        if i not in raw:
            held += a.size * a.dtype.itemsize
    for a in scratch:
        if len(getattr(a, "shape", ())) > 1 and a.dtype in (F32, BF16):
            held += math.prod(a.shape) * jnp.dtype(a.dtype).itemsize
    out_shape = [pltpu.HBM(a.shape, a.dtype) if i in sent else a for i, a in enumerate(out_shape)]
    scratch = list(scratch)
    if any(ins_far) or any(outs_far):
        kernel = functools.partial(staged, kernel, ins_far, outs_far, len(scratch))
        for a, far in zip((*args, *out_shape), ins_far + outs_far):
            if far:
                scratch.append(pltpu.VMEM(a.shape, a.dtype))
        scratch.append(pltpu.SemaphoreType.DMA((max(1, sum(ins_far)),)))
        scratch.append(pltpu.SemaphoreType.DMA((max(1, sum(outs_far)),)))
    return pl.pallas_call(
        kernel,
        out_shape=out_shape,
        in_specs=[pl.BlockSpec(memory_space=pltpu.SMEM)]
        + [hbm if far or i in raw else vmem for i, far in enumerate(ins_far)],
        out_specs=[hbm if far or i in sent else vmem for i, far in enumerate(outs_far)],
        scratch_shapes=scratch,
        cost_estimate=pl.CostEstimate(flops=cost, bytes_accessed=1, transcendentals=0),
        compiler_params=pltpu.CompilerParams(
            vmem_limit_bytes=min(held, 60 << 20) if tight else 60 << 20
        ),
        name=name,
    )(idx, *args)


def head_select(parts, axis):
    if len(parts) == 1:
        return parts[0]
    head = lax.broadcasted_iota(jnp.int32, parts[0].shape, axis) // HDIM
    return jnp.where(head == 0, parts[0], parts[1])


def head_only(value, h, count):
    if count == 1:
        return value
    head = lax.broadcasted_iota(jnp.int32, value.shape, 1) // HDIM
    return jnp.where(head == h, value, jnp.zeros_like(value))


def self_kernel(
    chips, idx, tok, weight, gain, shift, states, pair, segment, normed, triple, probs, *rest
):
    att_out = rest[:chips]
    val_t, att, kv = rest[chips:]
    rows, width = tok.shape[0], weight.shape[2]
    heads = width // HDIM
    g = gain[0:1, :].astype(F32)
    s = shift[0:1, :].astype(F32)

    def project(i, carry):
        here = at(i, QB)
        standard, _ = normalize(tok[here, :].astype(F32))
        n = (standard * g + s).astype(BF16)
        normed[here, :] = n
        triple[0, here, :] = dot_nn(n, weight[0]).astype(BF16)
        triple[1, here, :] = dot_nn(n, weight[1]).astype(BF16)
        value = dot_nn(n, weight[2])
        triple[2, here, :] = value.astype(BF16)
        val_t[:, here] = value.T.astype(BF16)
        return carry

    lax.fori_loop(0, rows // QB, project, 0)
    for i in range(rows // QB):
        here = slice(i * QB, (i + 1) * QB)
        query = triple[0, here, :]
        seen = (i + 1) * QB
        outs = []
        for h in range(heads):
            scores = dot_nt(triple[1, 0:seen, :], head_only(query, h, heads)) * SCALE
            key_at = lax.broadcasted_iota(jnp.int32, scores.shape, 0)
            row_at = lax.broadcasted_iota(jnp.int32, scores.shape, 1) + i * QB
            scores = jnp.where(key_at <= row_at, scores, NEG_FILL)
            e = jnp.exp(scores - jnp.max(scores, 0, keepdims=True))
            p = (e * (1.0 / jnp.sum(e, 0, keepdims=True))).astype(BF16)
            probs[h, 0:seen, here] = p
            outs.append(dot_nn(val_t[:, 0:seen], p))
        att[here, :] = head_select(outs, 0).T.astype(BF16)
    own = (att_out[0].shape[0] - 2 * SEEN) // 2
    before = segment[pl.ds(idx[2], 1), :] < idx[3]
    begin = jnp.minimum(jnp.sum(before.astype(jnp.int32)), states.shape[1] - SEEN)
    for c in range(2):
        kv[...] = dot_nn(states[idx[2]], pair[c])
        for k in range(chips):
            where = slice(2 * own + c * SEEN, 2 * own + (c + 1) * SEEN)
            att_out[k][where, :] = kv[pl.ds(begin, SEEN), :].astype(BF16)
    for k in range(chips):
        for cc in range(2):
            att_out[k][cc * own : (cc + 1) * own, :] = att[at(idx[0] ^ (2 * k + cc), own), :]


def pair_tiles(block, heads):
    return jnp.concatenate([head_only(block, h, heads) for h in range(heads)], 0)


def half_reduce(op, value, heads, fill):
    if heads == 1:
        return op(value, -1, keepdims=True)
    half = lax.broadcasted_iota(jnp.int32, value.shape, 1) // SEEN
    first = op(jnp.where(half == 0, value, fill), -1, keepdims=True)
    other = op(jnp.where(half == 1, value, fill), -1, keepdims=True)
    return jnp.where(half == 0, first, other)


def fetch_weights(chips, dps, idx, weights, wf, sem):
    width = wf.shape[1] // (2 * chips)
    cut = wf.shape[2] // dps
    span = (chips - 1) * width
    half = chips * width
    lists = []
    for m in range(3):
        copies = []
        for cc in range(2):
            source = weights[cc * (dps + 1)]
            where = wf.at[m, cc * half : cc * half + width, :]
            copies.append((source.at[m * width : (m + 1) * width, :], where))
            for q in range(dps):
                source = weights[cc * (dps + 1) + 1 + q]
                cols = at(idx[1] ^ q, cut)
                where = wf.at[m, cc * half + width : (cc + 1) * half, cols]
                copies.append((source.at[m * span : (m + 1) * span, :], where))
        lists.append(
            [pltpu.make_async_copy(s, d, sem.at[m, i]) for i, (s, d) in enumerate(copies)]
        )
    return lists


def own_rows(idx, source, rows, sem):
    copy = pltpu.make_async_copy(source.at[at(idx[0], rows.shape[0]), :], rows, sem)
    copy.start()
    return copy


def cross_kernel(chips, dps, idx, tokens, gain, shift, seen, *rest):
    take = iter(rest)
    pull = lambda n: [next(take) for _ in range(n)]
    weights = pull(2 * dps + 2)
    att_in = [pull(chips), pull(chips)]
    first_o, pack_o, q_o, cp_o, second_o, n3_o = pull(6)
    wf, sem, tok, tok_sem = pull(4)
    fetch = own_rows(idx, tokens, tok, tok_sem)
    own, dim = tok.shape
    width = wf.shape[1] // (2 * chips)
    heads = width // HDIM
    half = chips * width
    copies = fetch_weights(chips, dps, idx, weights, wf, sem)
    for each in copies:
        for copy in each:
            copy.start()
    for k in range(chips):
        pack_o[0, :, k * width : (k + 1) * width] = att_in[0][k][0:own, :]
        pack_o[0, :, half + k * width : half + (k + 1) * width] = att_in[1][k][own : 2 * own, :]
    fetch.wait()
    for copy in copies[0]:
        copy.wait()
    resid = tok[...].astype(F32) + dot_nn(pack_o[0], wf[0])
    first_o[...] = resid
    n2 = (normalize(resid)[0] * gain[1:2, :].astype(F32) + shift[1:2, :].astype(F32)).astype(BF16)
    pack_o[1, :, :] = n2
    for copy in copies[1]:
        copy.wait()
    q_o[...] = dot_nt(n2, wf[1]).astype(BF16)
    allowed = seen[...] > 0
    for cc in range(2):
        for k in range(chips):
            b = cc * chips + k
            lanes = slice(b * width, (b + 1) * width)
            keys = pair_tiles(att_in[cc][k][2 * own : 2 * own + SEEN, :], heads)
            values = pair_tiles(att_in[cc][k][2 * own + SEEN :, :], heads)
            scores = dot_nt(q_o[:, lanes], keys) * SCALE
            scores = jnp.where(allowed, scores, NEG_FILL)
            e = jnp.exp(scores - half_reduce(jnp.max, scores, heads, NEG_FILL))
            p = (e * (1.0 / half_reduce(jnp.sum, e, heads, 0.0))).astype(BF16)
            cp_o[b] = p
            pack_o[2, :, lanes] = dot_nn(p, values).astype(BF16)
    for copy in copies[2]:
        copy.wait()
    resid = resid + dot_nn(pack_o[2], wf[2])
    second_o[...] = resid
    n3 = normalize(resid)[0] * gain[2:3, :].astype(F32) + shift[2:3, :].astype(F32)
    n3_o[...] = n3.astype(BF16)


def active_kernel(chips, idx, cot, weight, *rest):
    outs, part = rest[:chips], rest[chips]
    rows = outs[0].shape[0]

    def chip(k, carry):
        part[k] = dot_nt(cot[at((idx[0] // 2) ^ k, rows), :], weight[...])
        return carry

    lax.fori_loop(0, chips, chip, 0)
    for k in range(chips):
        outs[k][...] = part[k]


def hidden_kernel(idx, same, other, weight, bias, grad_active, *rest):
    n3_h, act_h, ghi_h, bs_o, bo_o, back, n3_o, act_o, ghi_o, sem = rest
    own = same.shape[0]
    core = lax.rem(idx[0], 2)
    pairs = ((n3_o, n3_h), (act_o, act_h), (ghi_o, ghi_h))
    keep = [pltpu.make_async_copy(a, b, sem.at[i]) for i, (a, b) in enumerate(pairs)]
    n3_o[at(core, own), :] = same[...]
    n3_o[at(1 - core, own), :] = other[...]
    keep[0].start()
    v = dot_nn(n3_o[...], weight[...]) + bias[...].astype(F32)
    root = 0.7978845608028654
    square = v * v
    t = jnp.tanh(root * v * (1.0 + 0.044715 * square))
    act_o[...] = (0.5 * v * (1.0 + t)).astype(BF16)
    slope = 0.5 * (1.0 + t) + 0.5 * v * (1.0 - t * t) * (root * (1.0 + 0.134145 * square))
    ghi = (grad_active[...] * slope).astype(BF16)
    ghi_o[...] = ghi
    keep[1].start()
    keep[2].start()
    back[...] = dot_nt(ghi, weight[...])
    bs_o[...] = back[at(core, own), :].astype(BF16)
    dim = back.shape[1]
    bo_o[:, 0:dim] = back[at(1 - core, own), :].astype(BF16)
    bo_o[:, dim:] = act_o[at(1 - core, own), :]
    for copy in keep:
        copy.wait()


def mlp_out_kernel(chips, idx, weight, weight2, *rest):
    acts, others, outs = rest[:chips], rest[chips : 2 * chips], rest[2 * chips : 3 * chips]
    near, part, sem = rest[3 * chips :]
    own, dim = outs[0].shape
    hid = weight.shape[0]
    mine = at(lax.rem(idx[0], 2), own)
    copies = []
    for k in range(chips):
        sources = acts[k].at[mine, :], others[k].at[:, dim : dim + hid]
        for c, source in enumerate(sources):
            copies.append(pltpu.make_async_copy(source, near.at[c, k], sem.at[c, k]))
    for copy in copies:
        copy.start()
    for copy in copies:
        copy.wait()

    def chip(k, carry):
        value = dot_nn(near[0, k], weight[...]) + dot_nn(near[1, k], weight2[...])
        part[k] = value.astype(BF16)
        return carry

    lax.fori_loop(0, chips, chip, 0)
    for k in range(chips):
        outs[k][...] = part[k]


def mlp_grad_kernel(chips, idx, cot, *rest):
    acts = rest[:chips]
    ghis = rest[chips : 2 * chips]
    n3s = rest[2 * chips : 3 * chips]
    out, act, ghi, n3 = rest[3 * chips :]
    step = acts[0].shape[0]
    hid = acts[0].shape[1]
    dps, _, cut = out.shape
    total = jnp.zeros((1, hid), F32)
    for k in range(chips):
        rows = at((idx[0] // 2) ^ k, step)
        act[rows, :] = acts[k][...]
        ghi[rows, :] = ghis[k][...]
        n3[rows, :] = n3s[k][...]
        total += jnp.sum(ghis[k][...].astype(F32), 0, keepdims=True)
    row = lax.broadcasted_iota(jnp.int32, (PAD, cut), 0)
    bias = jnp.zeros((PAD, cut), F32)
    for j in range(hid // cut):
        bias = jnp.where(row == j, total[:, j * cut : (j + 1) * cut], bias)
    def columns(q, carry):
        cols = at(q, cut)
        out[q, 0:hid, :] = dot_tn(act[...], cot[:, cols]).astype(BF16)
        out[q, hid : 2 * hid, :] = dot_tn(ghi[...], n3[:, cols]).astype(BF16)
        out[q, 2 * hid : 2 * hid + PAD, :] = bias.astype(BF16)
        return carry

    lax.fori_loop(0, dps, columns, 0)


def cross_back_kernel(chips, dps, count, idx, cotangent, gain, second, first, cp, q, *rest):
    take = iter(rest)
    pull = lambda n: [next(take) for _ in range(n)]
    weights = pull(2 * dps + 2)
    parts = pull(count)
    kv = [pull(chips), pull(chips)]
    pack_o, gf_o, stat_o, same_o, other_o = pull(5)
    gt_o = pull(chips)
    gc, wf, sem, cot, cot_sem = pull(5)
    fetch = own_rows(idx, cotangent, cot, cot_sem)
    copies = fetch_weights(chips, dps, idx, weights, wf, sem)
    for each in reversed(copies):
        for copy in each:
            copy.start()
    dkv_o = (same_o, other_o)
    own = cot.shape[0]
    width = kv[0][0].shape[1]
    heads = width // HDIM
    grad_normed = parts[0][...].astype(F32)
    for part in parts[1:]:
        grad_normed += part[...].astype(F32)
    fetch.wait()
    c = cot[...].astype(F32)
    standard, inverse = normalize(second[...])
    grad = c + norm_backward(standard, inverse, grad_normed, gain[2:3, :].astype(F32))
    stat_o[0:1, :] = jnp.sum(grad_normed * standard, 0, keepdims=True)
    stat_o[1:2, :] = jnp.sum(grad_normed, 0, keepdims=True)
    stat_o[4:5, :] = jnp.sum(c, 0, keepdims=True)
    g2 = grad.astype(BF16)
    pack_o[2, :, :] = g2
    for copy in copies[2]:
        copy.wait()
    gc[...] = dot_nt(g2, wf[2]).astype(BF16)
    for cc in range(2):
        for k in range(chips):
            b = cc * chips + k
            lanes = slice(b * width, (b + 1) * width)
            keys = pair_tiles(kv[cc][k][2 * own : 2 * own + SEEN, :], heads)
            values = pair_tiles(kv[cc][k][2 * own + SEEN :, :], heads)
            gcb = gc[:, lanes]
            dp = dot_nt(gcb, values)
            low = cp[b]
            p = low.astype(F32)
            inner = half_reduce(jnp.sum, dp * p, heads, 0.0)
            ds = (p * (dp - inner) * SCALE).astype(BF16)
            pack_o[1, :, lanes] = dot_nn(ds, keys).astype(BF16)
            dk = dot_tn(ds, q[:, lanes])
            dv = dot_tn(low, gcb)
            for i, d in enumerate((dk, dv)):
                fold = head_select([d[h * SEEN : (h + 1) * SEEN, :] for h in range(heads)], 1)
                dkv_o[cc][k, i, :, :] = fold.astype(BF16)
    for copy in copies[1]:
        copy.wait()
    grad_normed = dot_nn(pack_o[1], wf[1])
    standard, inverse = normalize(first[...])
    grad = grad + norm_backward(standard, inverse, grad_normed, gain[1:2, :].astype(F32))
    stat_o[2:3, :] = jnp.sum(grad_normed * standard, 0, keepdims=True)
    stat_o[3:4, :] = jnp.sum(grad_normed, 0, keepdims=True)
    gf_o[...] = grad
    g1 = grad.astype(BF16)
    pack_o[0, :, :] = g1
    for copy in copies[0]:
        copy.wait()
    gatt = dot_nt(g1, wf[0]).astype(BF16)
    for cc in range(2):
        for k in range(chips):
            b = cc * chips + k
            gt_o[k][cc, :, :] = gatt[:, b * width : (b + 1) * width]


def row_grad_kernel(chips, idx, fwd, fwd2, bwd, bwd2, out, left, right):
    dps, height, cut = out.shape
    width = height // (3 * chips)
    own = fwd.shape[1]
    half = chips * width
    for m, (l, r) in enumerate((((fwd, fwd2), (bwd, bwd2)), ((bwd, bwd2), (fwd, fwd2)), ((fwd, fwd2), (bwd, bwd2)))):
        left[0:own, :] = l[0][m, :, 0:half]
        left[own : 2 * own, :] = l[1][m, :, half : 2 * half]
        right[0:own, :] = r[0][m]
        right[own : 2 * own, :] = r[1][m]
        for q in range(dps):
            part = dot_tn(left[...], right[:, q * cut : (q + 1) * cut]).astype(BF16)
            for k in range(chips):
                row = (3 * k + m) * width
                out[q, row : row + width, :] = part[k * width : (k + 1) * width, :]


def pack_kernel(idx, *refs):
    parts, out = refs[:-1], refs[-1]
    width = parts[0].shape[0] // 3
    for m in range(3):
        for k, part in enumerate(parts):
            row = (m * len(parts) + k) * width
            out[row : row + width, :] = part[m * width : (m + 1) * width, :]


def self_back_kernel(chips, idx, triple, probs, weight, *rest):
    take = iter(rest)
    pull = lambda n: [next(take) for _ in range(n)]
    grads = [pull(chips), pull(chips)]
    (gt_o,) = pull(1)
    bs_o, bo_o = pull(chips), pull(chips)
    gout, key_t, wcat, dq, dk, dv, back = pull(7)
    rows, width = triple.shape[1], triple.shape[2]
    heads = width // HDIM
    own = bs_o[0].shape[0]
    for k in range(chips):
        gout[at(idx[0] ^ (2 * k), own), :] = grads[0][k][0]
        gout[at(idx[0] ^ (2 * k + 1), own), :] = grads[1][k][1]
    for c in range(3):
        wcat[:, c * width : (c + 1) * width] = weight[c]
    count = rows // QB
    for i in range(count):
        here = slice(i * QB, (i + 1) * QB)
        key_t[:, here] = triple[1, here, :].astype(F32).T.astype(BF16)
    dk[...] = jnp.zeros(dk.shape, F32)
    dv[...] = jnp.zeros(dv.shape, F32)

    def one_head(h, carry):
        for i in reversed(range(count)):
            here = slice(i * QB, (i + 1) * QB)
            seen = (i + 1) * QB
            go = head_only(gout[here, :], h, heads)
            query = head_only(triple[0, here, :], h, heads)
            dp = dot_nt(triple[2, 0:seen, :], go)
            low = probs[h, 0:seen, here]
            p = low.astype(F32)
            inner = jnp.sum(dp * p, 0, keepdims=True)
            ds = (p * (dp - inner) * SCALE).astype(BF16)
            dk[0:seen, :] += dot_nn(ds, query)
            dv[0:seen, :] += dot_nn(low, go)
            new_q = dot_nn(key_t[:, 0:seen], ds)
            head = lax.broadcasted_iota(jnp.int32, new_q.shape, 0) // HDIM
            dq[:, here] = jnp.where(head == h, new_q, dq[:, here])
        return carry

    lax.fori_loop(0, heads, one_head, 0)
    for i in range(count):
        here = slice(i * QB, (i + 1) * QB)
        gt_o[here, 0:width] = dq[:, here].T.astype(BF16)
        gt_o[here, width : 2 * width] = dk[here, :].astype(BF16)
        gt_o[here, 2 * width : 3 * width] = dv[here, :].astype(BF16)

    def project(i, carry):
        back[at(i, QB), :] = dot_nt(gt_o[at(i, QB), :], wcat[...]).astype(BF16)
        return carry

    lax.fori_loop(0, count, project, 0)
    for k in range(chips):
        bs_o[k][...] = back[at(idx[0] ^ (2 * k), own), :]
        bo_o[k][...] = back[at(idx[0] ^ (2 * k + 1), own), :]


def self_grad_kernel(chips, dps, idx, tok, normed, gt, states, gp, stat, *rest):
    parts, (out, held, sem) = rest[: 2 * chips], rest[2 * chips :]
    cut = out.shape[2]
    width = gp.shape[2]
    own = held.shape[1]
    copies = []
    for k in range(chips):
        for cc in range(2):
            j = 2 * k + cc
            copies.append(pltpu.make_async_copy(parts[cc * chips + k], held.at[j], sem.at[j]))
    for copy in copies:
        copy.start()

    def columns(q, carry):
        cols = at(q, cut)
        out[q, 0 : 3 * width, :] = dot_tn(gt[...], normed[:, cols]).astype(BF16)
        for c in range(2):
            out[q, (3 + c) * width : (4 + c) * width, :] = dot_tn(
                gp[c], states[:, cols]
            ).astype(BF16)
        return carry

    lax.fori_loop(0, dps, columns, 0)
    for copy in copies:
        copy.wait()

    def add_rows(j, carry):
        g = held[j].astype(F32)
        standard, _ = normalize(tok[at(idx[0] ^ j, own), :].astype(F32))
        gain = carry[0] + jnp.sum(g * standard, 0, keepdims=True)
        return gain, carry[1] + jnp.sum(g, 0, keepdims=True)

    none = jnp.zeros((1, tok.shape[1]), F32)
    gain, shift = lax.fori_loop(0, 2 * chips, add_rows, (none, none))
    row = lax.broadcasted_iota(jnp.int32, (PAD, tok.shape[1]), 0)
    both = jnp.where(row == 0, gain, jnp.where(row == 1, shift, 0.0))
    for i in range(5):
        both = jnp.where(row == i + 2, stat[i : i + 1, :], both)
    both = both.astype(BF16)
    for q in range(dps):
        for c in range(dps):
            here = slice(5 * width + c * PAD, 5 * width + (c + 1) * PAD)
            out[q, here, :] = both[:, c * cut : (c + 1) * cut]


def add_kernel(idx, *refs):
    count = len(refs) // 3
    step = math.gcd(refs[0].shape[0], 32)

    def add_rows(i, carry):
        here = at(i, step)
        for k in range(count):
            total = refs[k][here, :].astype(F32) + refs[count + k][here, :].astype(F32)
            refs[2 * count + k][here, :] = total.astype(BF16)
        return carry

    lax.fori_loop(0, refs[0].shape[0] // step, add_rows, 0)


def sum_kernel(idx, pieces, out):
    step = math.gcd(out.shape[0], 64)

    def add_rows(i, carry):
        here = at(i, step)
        out[here, :] = jnp.sum(pieces[:, here, :].astype(F32), 0).astype(BF16)
        return carry

    lax.fori_loop(0, out.shape[0] // step, add_rows, 0)


def token_kernel(idx, tokens, gain, grad, *rest):
    parts, (out, tok, sem) = rest[:-3], rest[-3:]
    own_rows(idx, tokens, tok, sem).wait()
    grad_normed = parts[0][...].astype(F32)
    for part in parts[1:]:
        grad_normed += part[...].astype(F32)
    standard, inverse = normalize(tok[...].astype(F32))
    out[...] = grad[...] + norm_backward(standard, inverse, grad_normed, gain[0:1, :].astype(F32))


def place_kernel(plan, idx, *refs):
    parts, outs = refs[: -len(plan)], refs[-len(plan) :]
    if len(parts) == 1:
        source = parts[0]
        count, _, cut = source.shape
        take = lambda q, rows: source[q, rows, :]
        where_of = lambda q: slice(q * cut, (q + 1) * cut)
    else:
        count, cut = len(parts), parts[0].shape[1]
        take = lambda q, rows: parts[q][rows, :]
        where_of = lambda q: at(idx[1] ^ q, cut)
    row = 0
    for out, (height, lead, flip) in zip(outs, plan):
        for q in range(count):
            where = where_of(q)
            piece = take(q, slice(row, row + height)).astype(F32)
            if not flip:
                out[:, where] = piece
            elif lead is None:
                out[where, :] = piece.T
            else:
                step = height // lead
                for c in range(lead):
                    out[c, where, :] = piece[c * step : (c + 1) * step, :].T
        row += height


def flip_bits(axis, bits, size):
    return functools.partial(
        lax.ppermute, axis_name=axis, perm=[(i, i ^ bits) for i in range(size)]
    )


def total(*parts):
    out = parts[0].astype(F32)
    for part in parts[1:]:
        out = out + part.astype(F32)
    return out


def body(
    tokens,
    states,
    cotangent,
    self_weight,
    self_output,
    cross_query,
    cross_pair,
    cross_output,
    hidden_weight,
    hidden_bias,
    output_weight,
    output_bias,
    norm_gain,
    norm_shift,
    state_row,
    state_segment,
    caption,
):
    rows, dim = tokens.shape
    width = cross_query.shape[1]
    heads = width // HDIM
    hid = hidden_bias.shape[0]
    cores = lax.axis_size("mp")
    chips = cores // 2
    dps = lax.axis_size("dp")
    own = rows // cores
    cut = dim // dps
    me = lax.axis_index("mp")
    dpi = lax.axis_index("dp")
    idx = jnp.stack([me, dpi, state_row[0], caption[0]]).astype(jnp.int32)
    to_z = [flip_bits("mp", 2 * k, cores) for k in range(chips)]
    to_core = flip_bits("mp", 1, cores)
    to_dp = [flip_bits("dp", q, dps) for q in range(dps)]
    far = range(1, chips)
    peers = range(1, dps)

    def share_dp(piece):
        return lax.all_to_all(jnp.broadcast_to(piece[None], (dps,) + piece.shape), "dp", 0, 0)

    def add_all(left, right, name):
        return list(
            call(
            add_kernel,
            [((own, dim), BF16)] * chips,
            idx,
            *left,
            *right,
            stage=True,
            name=name,
        ))

    def swap_dp(pieces):
        return lax.all_to_all(pieces, "dp", 0, 0)

    def sum_dp(pieces):
        return jnp.sum(pieces.astype(F32), 0).astype(BF16)

    labels = lax.dynamic_index_in_dim(state_segment, state_row[0], 0, False)
    begin = jnp.minimum(jnp.sum((labels < caption[0]).astype(jnp.int32)), labels.shape[0] - SEEN)
    labels = lax.dynamic_slice_in_dim(labels, begin, SEEN, 0)
    seen = jnp.tile((labels == caption[0]).astype(jnp.int32)[None, :], (1, heads))
    near = lax.dynamic_slice(states, (state_row[0], begin, 0), (1, SEEN, dim))[0]

    mine = jnp.concatenate([self_output, cross_query.T, cross_output], 0)
    piece = lax.dynamic_slice_in_dim(mine, dpi * cut, cut, 1)
    got = [to_z[k](piece) for k in far]
    output_weight2 = to_core(output_weight)

    outs = call(
        functools.partial(self_kernel, chips),
        [
            ((rows, dim), BF16),
            ((3, rows, width), BF16),
            ((heads, rows, rows), BF16),
        ]
        + [((2 * own + 2 * SEEN, width), BF16)] * chips,
        idx,
        tokens,
        self_weight,
        norm_gain,
        norm_shift,
        states,
        cross_pair,
        state_segment,
        scratch=[
            pltpu.VMEM((width, rows), BF16),
            pltpu.VMEM((rows, width), BF16),
            pltpu.VMEM((states.shape[1], width), F32),
        ],
        after=(piece,),
        stage=True,
        name="self_fwd",
    )
    normed_one, triple, probs = outs[:3]
    att = outs[3:]
    *got, output_weight2, _ = lax.optimization_barrier((*got, output_weight2, att[0]))
    (cat,) = call(pack_kernel, [((3 * width * (chips - 1), cut), BF16)], idx, *got, tight=True, name="pack")
    att = [att[0]] + [to_z[k](att[k]) for k in far]
    att2 = [to_core(x) for x in att]

    grad_active = call(
        functools.partial(active_kernel, chips),
        [((2 * own, hid), F32)] * chips,
        idx,
        cotangent,
        output_weight,
        scratch=[pltpu.VMEM((chips, 2 * own, hid), F32)],
        after=att[:1],
        stage=True,
        name="grad_active",
    )

    cats = [cat] + [to_dp[q](cat) for q in peers]
    cats, grad_active, seen = lax.optimization_barrier((cats, grad_active, seen))
    weights = [mine, *cats, to_core(mine), *[to_core(x) for x in cats]]

    sq = cores * width
    first, fwd, q, cp, second, n3 = call(
        functools.partial(cross_kernel, chips, dps),
        [
            ((own, dim), F32),
            ((3, own, dim), BF16),
            ((own, sq), BF16),
            ((cores, own, heads * SEEN), BF16),
            ((own, dim), F32),
            ((own, dim), BF16),
        ],
        idx,
        tokens,
        norm_gain,
        norm_shift,
        seen,
        *weights,
        *att,
        *att2,
        scratch=[
            pltpu.VMEM((3, sq, dim), BF16),
            pltpu.SemaphoreType.DMA((3, 2 * dps + 2)),
            pltpu.VMEM((own, dim), BF16),
            pltpu.SemaphoreType.DMA,
        ],
        raw=(0, *range(4, 4 + len(weights))),
        stage=True,
        name="cross_fwd",
    )

    relay = chips == 4
    order = (0, 1, 3, 2) if relay else range(chips)
    n3s = [n3] + [None if relay and k == 2 else to_z[k](n3) for k in far]
    fwd2 = to_core(fwd)
    bias_row = hidden_bias[None, :]
    acts, ghis, chunks, sent, others = ([None] * chips for _ in range(5))
    done = ()
    for k in order:
        arrived = n3s[k]
        chunk, act, ghi, bs, bo = call(
            hidden_kernel,
            [
                ((2 * own, dim), BF16),
                ((2 * own, hid), BF16),
                ((2 * own, hid), BF16),
                ((own, dim), BF16),
                ((own, dim + hid), BF16),
            ],
            idx,
            arrived,
            to_core(arrived),
            hidden_weight,
            bias_row,
            grad_active[k],
            scratch=[
                pltpu.VMEM((2 * own, dim), F32),
                pltpu.VMEM((2 * own, dim), BF16),
                pltpu.VMEM((2 * own, hid), BF16),
                pltpu.VMEM((2 * own, hid), BF16),
                pltpu.SemaphoreType.DMA((3,)),
            ],
            sent=(0, 1, 2),
            after=done,
            tight=True,
            name="hidden",
        )
        done = (act,)
        acts[k], ghis[k], chunks[k] = act, ghi, chunk
        others[k] = to_core(bo)
        sent[k] = total(bs, others[k][:, :dim]).astype(BF16)
        if k == 0:
            *n3s, _ = lax.optimization_barrier((*n3s, act))
            if relay:
                n3s[2] = to_z[1](n3s[3])
    backs = sent[:1] + [to_z[k](sent[k]) for k in range(1, 2 if relay else chips)]
    if relay:
        relayed = to_z[1](sent[3])
    (mlp_grad,) = call(
        functools.partial(mlp_grad_kernel, chips),
        [((dps, 2 * hid + PAD, cut), BF16)],
        idx,
        cotangent,
        *acts,
        *ghis,
        *chunks,
        scratch=[
            pltpu.VMEM((rows, hid), BF16),
            pltpu.VMEM((rows, hid), BF16),
            pltpu.VMEM((rows, dim), BF16),
        ],
        after=[x for k, x in enumerate(sent) if k != 2],
        cost=10**12,
        stage=True,
        name="mlp_grad",
    )
    if relay:
        mlp_grad, relayed = lax.optimization_barrier((mlp_grad, relayed))
        backs.append(to_z[2](total(sent[2], relayed).astype(BF16)))
    mlp_grad, backs[1] = lax.optimization_barrier((mlp_grad, backs[1]))
    mlp_swap = swap_dp(mlp_grad)
    mlp_part = call(
        functools.partial(mlp_out_kernel, chips),
        [((own, dim), BF16)] * chips,
        idx,
        output_weight,
        output_weight2,
        *acts,
        *others,
        scratch=[
            pltpu.VMEM((2, chips, own, hid), BF16),
            pltpu.VMEM((chips, own, dim), BF16),
            pltpu.SemaphoreType.DMA((2, chips)),
        ],
        raw=tuple(range(2, 2 + 2 * chips)),
        after=(mlp_grad,),
        stage=True,
        name="mlp_out",
    )
    *backs, mlp_part = lax.optimization_barrier((*backs, list(mlp_part)))
    mlp_parts = mlp_part[:1] + [to_z[k](mlp_part[k]) for k in far[:2]]

    outs = call(
        functools.partial(cross_back_kernel, chips, dps, len(backs)),
        [
            ((3, own, dim), BF16),
            ((own, dim), F32),
            ((8, dim), F32),
            ((chips, 2, SEEN, width), BF16),
            ((chips, 2, SEEN, width), BF16),
        ]
        + [((2, own, width), BF16)] * chips,
        idx,
        cotangent,
        norm_gain,
        second,
        first,
        cp,
        q,
        *weights,
        *backs,
        *att,
        *att2,
        scratch=[
            pltpu.VMEM((own, sq), BF16),
            pltpu.VMEM((3, sq, dim), BF16),
            pltpu.SemaphoreType.DMA((3, 2 * dps + 2)),
            pltpu.VMEM((own, dim), BF16),
            pltpu.SemaphoreType.DMA,
        ],
        raw=(0, *range(6, 6 + len(weights))),
        cost=10**12,
        stage=True,
        name="cross_bwd",
    )
    outs, mlp_parts, mlp_swap = lax.optimization_barrier((outs, mlp_parts, mlp_swap))
    mlp_piece = call(
        sum_kernel, [((2 * hid, cut), BF16)], idx, mlp_swap, stage=True, name="sum_mlp"
    )[0]
    mlp_all = [mlp_piece] + [to_dp[q](mlp_piece) for q in (1, 2)]
    bwd, gf, stat_a, dkv, dkv_other = outs[:5]
    gatt = outs[5:]
    gatt = [gatt[0]] + [to_z[k](gatt[k]) for k in far]

    (row_grad,) = call(
        functools.partial(row_grad_kernel, chips),
        [((dps, chips * 3 * width, cut), BF16)],
        idx,
        fwd,
        fwd2,
        bwd,
        to_core(bwd),
        scratch=[pltpu.VMEM((2 * own, chips * width), BF16), pltpu.VMEM((2 * own, dim), BF16)],
        stage=True,
        name="row_grad",
    )
    gatt, row_grad, mlp_all, mlp_part = lax.optimization_barrier(
        (gatt, row_grad, mlp_all, mlp_part)
    )
    mlp_all += [to_dp[q](mlp_all[0]) for q in range(3, dps)]
    gatt2 = [to_core(x) for x in gatt]
    row_swap = swap_dp(row_grad)
    mlp_parts += [to_z[k](mlp_part[k]) for k in far[2:]]

    outs = call(
        functools.partial(self_back_kernel, chips),
        [((rows, 3 * width), BF16)] + [((own, dim), BF16)] * (2 * chips),
        idx,
        triple,
        probs,
        self_weight,
        *gatt,
        *gatt2,
        scratch=[
            pltpu.VMEM((rows, width), BF16),
            pltpu.VMEM((width, rows), BF16),
            pltpu.VMEM((dim, 3 * width), BF16),
            pltpu.VMEM((width, rows), F32),
            pltpu.VMEM((rows, width), F32),
            pltpu.VMEM((rows, width), F32),
            pltpu.VMEM((rows, dim), BF16),
        ],
        cost=10**12,
        stage=True,
        name="self_bwd",
    )
    outs, mlp_parts = lax.optimization_barrier((outs, mlp_parts))
    gt, bs, bo = outs[0], outs[1 : 1 + chips], outs[1 + chips :]
    bos = [to_core(x) for x in bo]

    dkv = total(dkv, to_core(dkv_other)).astype(BF16)
    gp = total(dkv[0], *[to_z[k](dkv[k]) for k in far]).astype(BF16)

    *bos, gp = lax.optimization_barrier((*bos, gp))
    sent = add_all(bs, bos, "self_add")
    parts = sent[:1] + [to_z[k](sent[k]) for k in far[:2]]

    (self_part,) = call(
        functools.partial(self_grad_kernel, chips, dps),
        [((dps, 5 * width + dps * PAD, cut), BF16)],
        idx,
        tokens,
        normed_one,
        gt,
        near,
        gp,
        stat_a,
        *bs,
        *bo,
        scratch=[
            pltpu.VMEM((cores, own, dim), BF16),
            pltpu.SemaphoreType.DMA((cores,)),
        ],
        raw=tuple(range(6, 6 + cores)),
        after=sent[:1],
        stage=True,
        name="self_grad",
    )
    self_part, row_swap, mlp_all, parts[1:3] = lax.optimization_barrier(
        (self_part, row_swap, mlp_all, parts[1:3])
    )
    self_swap = swap_dp(self_part)
    row_piece = sum_dp(row_swap).reshape(chips, 3 * width, cut)
    row_parts = [row_piece[0]] + [to_z[k](row_piece[k]) for k in far]
    block_output = (second + total(*mlp_parts) + output_bias.astype(F32)).astype(BF16)
    row_parts, self_swap, sent, block_output = lax.optimization_barrier(
        (row_parts, self_swap, sent, block_output)
    )
    parts += [to_z[k](sent[k]) for k in far[2:]]
    row_piece = total(*row_parts).astype(BF16)
    self_sum = sum_dp(self_swap)
    piece = jnp.concatenate([row_piece, self_sum[: 5 * width]], 0)
    swapped = share_dp(piece)
    (grad_tokens,) = call(
        token_kernel,
        [((own, dim), F32)],
        idx,
        tokens,
        norm_gain,
        gf,
        *parts,
        scratch=[pltpu.VMEM((own, dim), BF16), pltpu.SemaphoreType.DMA],
        raw=(0,),
        stage=True,
        name="tokens",
    )
    state_part = jnp.einsum("cse,cde->sd", gp, cross_pair, preferred_element_type=F32)
    held = self_sum[5 * width :].reshape(dps, PAD, cut)
    held = jnp.concatenate([held[c] for c in range(dps)], 1)
    state_part = jnp.concatenate([state_part.astype(BF16), held], 0)
    core = lax.rem(me, 2)
    half_of = lambda c: lax.dynamic_slice_in_dim(state_part, c * (dim // 2), dim // 2, 1)
    state_half = total(half_of(core), to_core(half_of(1 - core))).astype(BF16)
    state_got = [to_z[k](state_half) for k in far]
    def place(pieces, plan, shapes, name, **kept):
        return call(
            functools.partial(place_kernel, plan),
            [(s, F32) for s in shapes],
            idx,
            *pieces,
            stage=True,
            name=name,
            **kept,
        )

    grad_output_weight, grad_hidden_weight = place(
        mlp_all, ((hid, None, False), (hid, None, True)), ((hid, dim), (dim, hid)), "place_mlp"
    )
    state_got, block_output, grad_output_weight, grad_tokens = lax.optimization_barrier(
        (state_got, block_output, grad_output_weight, grad_tokens)
    )
    state_half = total(state_half, *state_got)
    state_sum = jnp.zeros((state_part.shape[0], dim), F32)
    for c, part in ((core, state_half), (1 - core, to_core(state_half))):
        state_sum = lax.dynamic_update_slice(state_sum, part, (0, c * (dim // 2)))
    grad_states = lax.dynamic_update_slice(
        jnp.zeros(states.shape, F32), state_sum[None, :SEEN], (state_row[0], begin, 0)
    )
    stats = state_sum[SEEN:]
    swapped, state_sum = lax.optimization_barrier((swapped, state_sum))
    (
        grad_self_output,
        grad_cross_query,
        grad_cross_output,
        grad_self_weight,
        grad_cross_pair,
    ) = place(
        [swapped],
        (
            (width, None, False),
            (width, None, True),
            (width, None, False),
            (3 * width, 3, True),
            (2 * width, 2, True),
        ),
        (
            (width, dim),
            (dim, width),
            (width, dim),
            (3, dim, width),
            (2, dim, width),
        ),
        "place",
        near=(0,),
        tight=True,
    )
    grad_norm_gain = jnp.stack([stats[0], stats[4], stats[2]])
    grad_norm_shift = jnp.stack([stats[1], stats[5], stats[3]])
    grad_output_bias = stats[6]
    grad_hidden_bias = jnp.sum(mlp_swap[:, 2 * hid : 2 * hid + hid // cut].astype(F32), 0).reshape(hid)
    return (
        block_output,
        grad_tokens,
        grad_states,
        grad_self_weight,
        grad_self_output,
        grad_cross_query,
        grad_cross_pair,
        grad_cross_output,
        grad_hidden_weight,
        grad_hidden_bias,
        grad_output_weight,
        grad_output_bias,
        grad_norm_gain,
        grad_norm_shift,
    )


def solution(mesh):
    placed = (
        P("dp", None),
        P("dp", None, None),
        P("dp", None),
        P(None, None, "mp"),
        P("mp", None),
        P(None, "mp"),
        P(None, None, "mp"),
        P("mp", None),
        P(None, "mp"),
        P("mp"),
        P("mp", None),
        P(),
        P(),
        P(),
        P("dp"),
        P("dp", None),
        P("dp"),
    )
    return jax.shard_map(
        body,
        mesh=mesh,
        in_specs=placed,
        out_specs=(
            P(("dp", "mp"), None),
            P(("dp", "mp"), None),
            P("dp", None, None),
            P(None, None, "mp"),
            P("mp", None),
            P(None, "mp"),
            P(None, None, "mp"),
            P("mp", None),
            P(None, "mp"),
            P("mp"),
            P("mp", None),
            P(),
            P(),
            P(),
        ),
        check_vma=False,
    )
```

```python
import functools
import math

import jax
import jax.numpy as jnp
from jax import lax
from jax.experimental import pallas as pl
from jax.experimental.pallas import tpu as pltpu
from jax.sharding import PartitionSpec as P

HDIM = 64
SEEN = 64
QB = 256
PAD = 16
EPSILON = 1e-05
NEG_FILL = -1e30
SCALE = HDIM ** (-0.5)
F32 = jnp.float32
BF16 = jnp.bfloat16


def dot_nn(a, b):
    return lax.dot_general(a, b, (((1,), (0,)), ((), ())), preferred_element_type=F32)


def dot_nt(a, b):
    return lax.dot_general(a, b, (((1,), (1,)), ((), ())), preferred_element_type=F32)


def dot_tn(a, b):
    return lax.dot_general(a, b, (((0,), (0,)), ((), ())), preferred_element_type=F32)


def normalize(resid):
    center = resid - jnp.mean(resid, -1, keepdims=True)
    inverse = lax.rsqrt(jnp.mean(center * center, -1, keepdims=True) + EPSILON)
    return (center * inverse, inverse)


def norm_backward(standard, inverse, grad_normed, gain):
    scaled = grad_normed * gain
    return inverse * (
        scaled
        - jnp.mean(scaled, -1, keepdims=True)
        - standard * jnp.mean(scaled * standard, -1, keepdims=True)
    )


def at(index, size):
    return pl.ds(pl.multiple_of(index * size, size), size)


def staged(kernel, ins, outs, extra, *refs):
    count_in, count_out = len(ins), len(outs)
    idx, refs = refs[0], list(refs[1:])
    inner = refs[: count_in + count_out]
    own = refs[count_in + count_out : count_in + count_out + extra]
    rest = refs[count_in + count_out + extra :]
    sem_in, sem_out = rest[-2:]
    held = iter(rest[:-2])
    started, results = [], []
    for i, here in enumerate(ins):
        if here:
            local = next(held)
            started.append(pltpu.make_async_copy(inner[i], local, sem_in.at[len(started)]))
            inner[i] = local
    for i, here in enumerate(outs):
        if here:
            local = next(held)
            target = inner[count_in + i]
            results.append(pltpu.make_async_copy(local, target, sem_out.at[len(results)]))
            inner[count_in + i] = local
    for copy in started:
        copy.start()
    for copy in started:
        copy.wait()
    kernel(idx, *inner, *own)
    for copy in results:
        copy.start()
    for copy in results:
        copy.wait()


def call(
    kernel, outs, idx, *args, scratch=(), after=(), stage=False, tight=False, raw=(), near=(), sent=(), cost=1, name=None, spill=8
):
    if after:
        idx = lax.optimization_barrier((idx, *after))[0]
    out_shape = [jax.ShapeDtypeStruct(s, t) for s, t in outs]
    big = lambda a: bool(stage) and a.size >= 1 << 15
    ins_far = [big(a) and i not in raw and i not in near for i, a in enumerate(args)]
    outs_far = [big(a) for a in out_shape]
    vmem = pl.BlockSpec(memory_space=pltpu.VMEM)
    hbm = pl.BlockSpec(memory_space=pltpu.HBM)
    held = spill << 20
    for i, a in enumerate((*args, *out_shape)):
        if i not in raw:
            held += a.size * a.dtype.itemsize
    for a in scratch:
        if len(getattr(a, "shape", ())) > 1 and a.dtype in (F32, BF16):
            held += math.prod(a.shape) * jnp.dtype(a.dtype).itemsize
    out_shape = [pltpu.HBM(a.shape, a.dtype) if i in sent else a for i, a in enumerate(out_shape)]
    scratch = list(scratch)
    if any(ins_far) or any(outs_far):
        kernel = functools.partial(staged, kernel, ins_far, outs_far, len(scratch))
        for a, far in zip((*args, *out_shape), ins_far + outs_far):
            if far:
                scratch.append(pltpu.VMEM(a.shape, a.dtype))
        scratch.append(pltpu.SemaphoreType.DMA((max(1, sum(ins_far)),)))
        scratch.append(pltpu.SemaphoreType.DMA((max(1, sum(outs_far)),)))
    return pl.pallas_call(
        kernel,
        out_shape=out_shape,
        in_specs=[pl.BlockSpec(memory_space=pltpu.SMEM)]
        + [hbm if far or i in raw else vmem for i, far in enumerate(ins_far)],
        out_specs=[hbm if far or i in sent else vmem for i, far in enumerate(outs_far)],
        scratch_shapes=scratch,
        cost_estimate=pl.CostEstimate(flops=cost, bytes_accessed=1, transcendentals=0),
        compiler_params=pltpu.CompilerParams(
            vmem_limit_bytes=min(held, 60 << 20) if tight else 60 << 20
        ),
        name=name,
    )(idx, *args)


def head_select(parts, axis):
    if len(parts) == 1:
        return parts[0]
    head = lax.broadcasted_iota(jnp.int32, parts[0].shape, axis) // HDIM
    return jnp.where(head == 0, parts[0], parts[1])


def head_only(value, h, count):
    if count == 1:
        return value
    head = lax.broadcasted_iota(jnp.int32, value.shape, 1) // HDIM
    return jnp.where(head == h, value, jnp.zeros_like(value))


def self_kernel(
    chips, idx, tok, weight, gain, shift, states, pair, segment, normed, triple, probs, *rest
):
    att_out = rest[:chips]
    val_t, att, kv = rest[chips:]
    rows, width = tok.shape[0], weight.shape[2]
    heads = width // HDIM
    g = gain[0:1, :].astype(F32)
    s = shift[0:1, :].astype(F32)

    def project(i, carry):
        here = at(i, QB)
        standard, _ = normalize(tok[here, :].astype(F32))
        n = (standard * g + s).astype(BF16)
        normed[here, :] = n
        triple[0, here, :] = dot_nn(n, weight[0]).astype(BF16)
        triple[1, here, :] = dot_nn(n, weight[1]).astype(BF16)
        value = dot_nn(n, weight[2])
        triple[2, here, :] = value.astype(BF16)
        val_t[:, here] = value.T.astype(BF16)
        return carry

    lax.fori_loop(0, rows // QB, project, 0)
    for i in range(rows // QB):
        here = slice(i * QB, (i + 1) * QB)
        query = triple[0, here, :]
        seen = (i + 1) * QB
        outs = []
        for h in range(heads):
            scores = dot_nt(triple[1, 0:seen, :], head_only(query, h, heads)) * SCALE
            key_at = lax.broadcasted_iota(jnp.int32, scores.shape, 0)
            row_at = lax.broadcasted_iota(jnp.int32, scores.shape, 1) + i * QB
            scores = jnp.where(key_at <= row_at, scores, NEG_FILL)
            e = jnp.exp(scores - jnp.max(scores, 0, keepdims=True))
            p = (e * (1.0 / jnp.sum(e, 0, keepdims=True))).astype(BF16)
            probs[h, 0:seen, here] = p
            outs.append(dot_nn(val_t[:, 0:seen], p))
        att[here, :] = head_select(outs, 0).T.astype(BF16)
    own = (att_out[0].shape[0] - 2 * SEEN) // 2
    before = segment[pl.ds(idx[2], 1), :] < idx[3]
    begin = jnp.minimum(jnp.sum(before.astype(jnp.int32)), states.shape[1] - SEEN)
    for c in range(2):
        kv[...] = dot_nn(states[idx[2]], pair[c])
        for k in range(chips):
            where = slice(2 * own + c * SEEN, 2 * own + (c + 1) * SEEN)
            att_out[k][where, :] = kv[pl.ds(begin, SEEN), :].astype(BF16)
    for k in range(chips):
        for cc in range(2):
            att_out[k][cc * own : (cc + 1) * own, :] = att[at(idx[0] ^ (2 * k + cc), own), :]


def pair_tiles(block, heads):
    return jnp.concatenate([head_only(block, h, heads) for h in range(heads)], 0)


def half_reduce(op, value, heads, fill):
    if heads == 1:
        return op(value, -1, keepdims=True)
    half = lax.broadcasted_iota(jnp.int32, value.shape, 1) // SEEN
    first = op(jnp.where(half == 0, value, fill), -1, keepdims=True)
    other = op(jnp.where(half == 1, value, fill), -1, keepdims=True)
    return jnp.where(half == 0, first, other)


def fetch_weights(chips, dps, idx, weights, wf, sem):
    width = wf.shape[1] // (2 * chips)
    cut = wf.shape[2] // dps
    span = (chips - 1) * width
    half = chips * width
    lists = []
    for m in range(3):
        copies = []
        for cc in range(2):
            source = weights[cc * (dps + 1)]
            where = wf.at[m, cc * half : cc * half + width, :]
            copies.append((source.at[m * width : (m + 1) * width, :], where))
            for q in range(dps):
                source = weights[cc * (dps + 1) + 1 + q]
                cols = at(idx[1] ^ q, cut)
                where = wf.at[m, cc * half + width : (cc + 1) * half, cols]
                copies.append((source.at[m * span : (m + 1) * span, :], where))
        lists.append(
            [pltpu.make_async_copy(s, d, sem.at[m, i]) for i, (s, d) in enumerate(copies)]
        )
    return lists


def own_rows(idx, source, rows, sem):
    copy = pltpu.make_async_copy(source.at[at(idx[0], rows.shape[0]), :], rows, sem)
    copy.start()
    return copy


def cross_kernel(chips, dps, idx, tokens, gain, shift, seen, *rest):
    take = iter(rest)
    pull = lambda n: [next(take) for _ in range(n)]
    weights = pull(2 * dps + 2)
    att_in = [pull(chips), pull(chips)]
    first_o, pack_o, q_o, cp_o, second_o, n3_o = pull(6)
    wf, sem, tok, tok_sem = pull(4)
    fetch = own_rows(idx, tokens, tok, tok_sem)
    own, dim = tok.shape
    width = wf.shape[1] // (2 * chips)
    heads = width // HDIM
    half = chips * width
    copies = fetch_weights(chips, dps, idx, weights, wf, sem)
    for each in copies:
        for copy in each:
            copy.start()
    for k in range(chips):
        pack_o[0, :, k * width : (k + 1) * width] = att_in[0][k][0:own, :]
        pack_o[0, :, half + k * width : half + (k + 1) * width] = att_in[1][k][own : 2 * own, :]
    fetch.wait()
    for copy in copies[0]:
        copy.wait()
    resid = tok[...].astype(F32) + dot_nn(pack_o[0], wf[0])
    first_o[...] = resid
    n2 = (normalize(resid)[0] * gain[1:2, :].astype(F32) + shift[1:2, :].astype(F32)).astype(BF16)
    pack_o[1, :, :] = n2
    for copy in copies[1]:
        copy.wait()
    q_o[...] = dot_nt(n2, wf[1]).astype(BF16)
    allowed = seen[...] > 0
    for cc in range(2):
        for k in range(chips):
            b = cc * chips + k
            lanes = slice(b * width, (b + 1) * width)
            keys = pair_tiles(att_in[cc][k][2 * own : 2 * own + SEEN, :], heads)
            values = pair_tiles(att_in[cc][k][2 * own + SEEN :, :], heads)
            scores = dot_nt(q_o[:, lanes], keys) * SCALE
            scores = jnp.where(allowed, scores, NEG_FILL)
            e = jnp.exp(scores - half_reduce(jnp.max, scores, heads, NEG_FILL))
            p = (e * (1.0 / half_reduce(jnp.sum, e, heads, 0.0))).astype(BF16)
            cp_o[b] = p
            pack_o[2, :, lanes] = dot_nn(p, values).astype(BF16)
    for copy in copies[2]:
        copy.wait()
    resid = resid + dot_nn(pack_o[2], wf[2])
    second_o[...] = resid
    n3 = normalize(resid)[0] * gain[2:3, :].astype(F32) + shift[2:3, :].astype(F32)
    n3_o[...] = n3.astype(BF16)


def active_kernel(chips, idx, cot, weight, *rest):
    outs, part = rest[:chips], rest[chips]
    rows = outs[0].shape[0]

    def chip(k, carry):
        part[k] = dot_nt(cot[at((idx[0] // 2) ^ k, rows), :], weight[...])
        return carry

    lax.fori_loop(0, chips, chip, 0)
    for k in range(chips):
        outs[k][...] = part[k]


def hidden_kernel(idx, same, other, weight, bias, grad_active, *rest):
    n3_h, act_h, ghi_h, bs_o, bo_o, back, n3_o, act_o, ghi_o, sem = rest
    own = same.shape[0]
    core = lax.rem(idx[0], 2)
    pairs = ((n3_o, n3_h), (act_o, act_h), (ghi_o, ghi_h))
    keep = [pltpu.make_async_copy(a, b, sem.at[i]) for i, (a, b) in enumerate(pairs)]
    n3_o[at(core, own), :] = same[...]
    n3_o[at(1 - core, own), :] = other[...]
    keep[0].start()
    v = dot_nn(n3_o[...], weight[...]) + bias[...].astype(F32)
    root = 0.7978845608028654
    square = v * v
    t = jnp.tanh(root * v * (1.0 + 0.044715 * square))
    act_o[...] = (0.5 * v * (1.0 + t)).astype(BF16)
    slope = 0.5 * (1.0 + t) + 0.5 * v * (1.0 - t * t) * (root * (1.0 + 0.134145 * square))
    ghi = (grad_active[...] * slope).astype(BF16)
    ghi_o[...] = ghi
    keep[1].start()
    keep[2].start()
    back[...] = dot_nt(ghi, weight[...])
    bs_o[...] = back[at(core, own), :].astype(BF16)
    dim = back.shape[1]
    bo_o[:, 0:dim] = back[at(1 - core, own), :].astype(BF16)
    bo_o[:, dim:] = act_o[at(1 - core, own), :]
    for copy in keep:
        copy.wait()


def mlp_out_kernel(chips, idx, weight, weight2, *rest):
    acts, others, outs = rest[:chips], rest[chips : 2 * chips], rest[2 * chips : 3 * chips]
    near, part, sem = rest[3 * chips :]
    own, dim = outs[0].shape
    hid = weight.shape[0]
    mine = at(lax.rem(idx[0], 2), own)
    copies = []
    for k in range(chips):
        sources = acts[k].at[mine, :], others[k].at[:, dim : dim + hid]
        for c, source in enumerate(sources):
            copies.append(pltpu.make_async_copy(source, near.at[c, k], sem.at[c, k]))
    for copy in copies:
        copy.start()
    for copy in copies:
        copy.wait()

    def chip(k, carry):
        value = dot_nn(near[0, k], weight[...]) + dot_nn(near[1, k], weight2[...])
        part[k] = value.astype(BF16)
        return carry

    lax.fori_loop(0, chips, chip, 0)
    for k in range(chips):
        outs[k][...] = part[k]


def mlp_grad_kernel(chips, idx, cot, *rest):
    acts = rest[:chips]
    ghis = rest[chips : 2 * chips]
    n3s = rest[2 * chips : 3 * chips]
    out, act, ghi, n3 = rest[3 * chips :]
    step = acts[0].shape[0]
    hid = acts[0].shape[1]
    dps, _, cut = out.shape
    total = jnp.zeros((1, hid), F32)
    for k in range(chips):
        rows = at((idx[0] // 2) ^ k, step)
        act[rows, :] = acts[k][...]
        ghi[rows, :] = ghis[k][...]
        n3[rows, :] = n3s[k][...]
        total += jnp.sum(ghis[k][...].astype(F32), 0, keepdims=True)
    row = lax.broadcasted_iota(jnp.int32, (PAD, cut), 0)
    bias = jnp.zeros((PAD, cut), F32)
    for j in range(hid // cut):
        bias = jnp.where(row == j, total[:, j * cut : (j + 1) * cut], bias)
    def columns(q, carry):
        cols = at(q, cut)
        out[q, 0:hid, :] = dot_tn(act[...], cot[:, cols]).astype(BF16)
        out[q, hid : 2 * hid, :] = dot_tn(ghi[...], n3[:, cols]).astype(BF16)
        out[q, 2 * hid : 2 * hid + PAD, :] = bias.astype(BF16)
        return carry

    lax.fori_loop(0, dps, columns, 0)


def cross_back_kernel(chips, dps, count, idx, cotangent, gain, second, first, cp, q, *rest):
    take = iter(rest)
    pull = lambda n: [next(take) for _ in range(n)]
    weights = pull(2 * dps + 2)
    parts = pull(count)
    kv = [pull(chips), pull(chips)]
    pack_o, gf_o, stat_o, same_o, other_o = pull(5)
    gt_o = pull(chips)
    gc, wf, sem, cot, cot_sem = pull(5)
    fetch = own_rows(idx, cotangent, cot, cot_sem)
    copies = fetch_weights(chips, dps, idx, weights, wf, sem)
    for each in reversed(copies):
        for copy in each:
            copy.start()
    dkv_o = (same_o, other_o)
    own = cot.shape[0]
    width = kv[0][0].shape[1]
    heads = width // HDIM
    grad_normed = parts[0][...].astype(F32)
    for part in parts[1:]:
        grad_normed += part[...].astype(F32)
    fetch.wait()
    c = cot[...].astype(F32)
    standard, inverse = normalize(second[...])
    grad = c + norm_backward(standard, inverse, grad_normed, gain[2:3, :].astype(F32))
    stat_o[0:1, :] = jnp.sum(grad_normed * standard, 0, keepdims=True)
    stat_o[1:2, :] = jnp.sum(grad_normed, 0, keepdims=True)
    stat_o[4:5, :] = jnp.sum(c, 0, keepdims=True)
    g2 = grad.astype(BF16)
    pack_o[2, :, :] = g2
    for copy in copies[2]:
        copy.wait()
    gc[...] = dot_nt(g2, wf[2]).astype(BF16)
    for cc in range(2):
        for k in range(chips):
            b = cc * chips + k
            lanes = slice(b * width, (b + 1) * width)
            keys = pair_tiles(kv[cc][k][2 * own : 2 * own + SEEN, :], heads)
            values = pair_tiles(kv[cc][k][2 * own + SEEN :, :], heads)
            gcb = gc[:, lanes]
            dp = dot_nt(gcb, values)
            low = cp[b]
            p = low.astype(F32)
            inner = half_reduce(jnp.sum, dp * p, heads, 0.0)
            ds = (p * (dp - inner) * SCALE).astype(BF16)
            pack_o[1, :, lanes] = dot_nn(ds, keys).astype(BF16)
            dk = dot_tn(ds, q[:, lanes])
            dv = dot_tn(low, gcb)
            for i, d in enumerate((dk, dv)):
                fold = head_select([d[h * SEEN : (h + 1) * SEEN, :] for h in range(heads)], 1)
                dkv_o[cc][k, i, :, :] = fold.astype(BF16)
    for copy in copies[1]:
        copy.wait()
    grad_normed = dot_nn(pack_o[1], wf[1])
    standard, inverse = normalize(first[...])
    grad = grad + norm_backward(standard, inverse, grad_normed, gain[1:2, :].astype(F32))
    stat_o[2:3, :] = jnp.sum(grad_normed * standard, 0, keepdims=True)
    stat_o[3:4, :] = jnp.sum(grad_normed, 0, keepdims=True)
    gf_o[...] = grad
    g1 = grad.astype(BF16)
    pack_o[0, :, :] = g1
    for copy in copies[0]:
        copy.wait()
    gatt = dot_nt(g1, wf[0]).astype(BF16)
    for cc in range(2):
        for k in range(chips):
            b = cc * chips + k
            gt_o[k][cc, :, :] = gatt[:, b * width : (b + 1) * width]


def row_grad_kernel(chips, idx, fwd, fwd2, bwd, bwd2, out, left, right):
    dps, height, cut = out.shape
    width = height // (3 * chips)
    own = fwd.shape[1]
    half = chips * width
    for m, (l, r) in enumerate((((fwd, fwd2), (bwd, bwd2)), ((bwd, bwd2), (fwd, fwd2)), ((fwd, fwd2), (bwd, bwd2)))):
        left[0:own, :] = l[0][m, :, 0:half]
        left[own : 2 * own, :] = l[1][m, :, half : 2 * half]
        right[0:own, :] = r[0][m]
        right[own : 2 * own, :] = r[1][m]
        for q in range(dps):
            part = dot_tn(left[...], right[:, q * cut : (q + 1) * cut]).astype(BF16)
            for k in range(chips):
                row = (3 * k + m) * width
                out[q, row : row + width, :] = part[k * width : (k + 1) * width, :]


def pack_kernel(idx, *refs):
    parts, out = refs[:-1], refs[-1]
    width = parts[0].shape[0] // 3
    for m in range(3):
        for k, part in enumerate(parts):
            row = (m * len(parts) + k) * width
            out[row : row + width, :] = part[m * width : (m + 1) * width, :]


def self_back_kernel(chips, idx, triple, probs, weight, *rest):
    take = iter(rest)
    pull = lambda n: [next(take) for _ in range(n)]
    grads = [pull(chips), pull(chips)]
    (gt_o,) = pull(1)
    bs_o, bo_o = pull(chips), pull(chips)
    gout, key_t, wcat, dq, dk, dv, back = pull(7)
    rows, width = triple.shape[1], triple.shape[2]
    heads = width // HDIM
    own = bs_o[0].shape[0]
    for k in range(chips):
        gout[at(idx[0] ^ (2 * k), own), :] = grads[0][k][0]
        gout[at(idx[0] ^ (2 * k + 1), own), :] = grads[1][k][1]
    for c in range(3):
        wcat[:, c * width : (c + 1) * width] = weight[c]
    count = rows // QB
    for i in range(count):
        here = slice(i * QB, (i + 1) * QB)
        key_t[:, here] = triple[1, here, :].astype(F32).T.astype(BF16)
    dk[...] = jnp.zeros(dk.shape, F32)
    dv[...] = jnp.zeros(dv.shape, F32)

    def one_head(h, carry):
        for i in reversed(range(count)):
            here = slice(i * QB, (i + 1) * QB)
            seen = (i + 1) * QB
            go = head_only(gout[here, :], h, heads)
            query = head_only(triple[0, here, :], h, heads)
            dp = dot_nt(triple[2, 0:seen, :], go)
            low = probs[h, 0:seen, here]
            p = low.astype(F32)
            inner = jnp.sum(dp * p, 0, keepdims=True)
            ds = (p * (dp - inner) * SCALE).astype(BF16)
            dk[0:seen, :] += dot_nn(ds, query)
            dv[0:seen, :] += dot_nn(low, go)
            new_q = dot_nn(key_t[:, 0:seen], ds)
            head = lax.broadcasted_iota(jnp.int32, new_q.shape, 0) // HDIM
            dq[:, here] = jnp.where(head == h, new_q, dq[:, here])
        return carry

    lax.fori_loop(0, heads, one_head, 0)
    for i in range(count):
        here = slice(i * QB, (i + 1) * QB)
        gt_o[here, 0:width] = dq[:, here].T.astype(BF16)
        gt_o[here, width : 2 * width] = dk[here, :].astype(BF16)
        gt_o[here, 2 * width : 3 * width] = dv[here, :].astype(BF16)

    def project(i, carry):
        back[at(i, QB), :] = dot_nt(gt_o[at(i, QB), :], wcat[...]).astype(BF16)
        return carry

    lax.fori_loop(0, count, project, 0)
    for k in range(chips):
        bs_o[k][...] = back[at(idx[0] ^ (2 * k), own), :]
        bo_o[k][...] = back[at(idx[0] ^ (2 * k + 1), own), :]


def self_grad_kernel(chips, dps, idx, tok, normed, gt, states, gp, stat, *rest):
    parts, (out, held, sem) = rest[: 2 * chips], rest[2 * chips :]
    cut = out.shape[2]
    width = gp.shape[2]
    own = held.shape[1]
    copies = []
    for k in range(chips):
        for cc in range(2):
            j = 2 * k + cc
            copies.append(pltpu.make_async_copy(parts[cc * chips + k], held.at[j], sem.at[j]))
    for copy in copies:
        copy.start()

    def columns(q, carry):
        cols = at(q, cut)
        out[q, 0 : 3 * width, :] = dot_tn(gt[...], normed[:, cols]).astype(BF16)
        for c in range(2):
            out[q, (3 + c) * width : (4 + c) * width, :] = dot_tn(
                gp[c], states[:, cols]
            ).astype(BF16)
        return carry

    lax.fori_loop(0, dps, columns, 0)
    for copy in copies:
        copy.wait()

    def add_rows(j, carry):
        g = held[j].astype(F32)
        standard, _ = normalize(tok[at(idx[0] ^ j, own), :].astype(F32))
        gain = carry[0] + jnp.sum(g * standard, 0, keepdims=True)
        return gain, carry[1] + jnp.sum(g, 0, keepdims=True)

    none = jnp.zeros((1, tok.shape[1]), F32)
    gain, shift = lax.fori_loop(0, 2 * chips, add_rows, (none, none))
    row = lax.broadcasted_iota(jnp.int32, (PAD, tok.shape[1]), 0)
    both = jnp.where(row == 0, gain, jnp.where(row == 1, shift, 0.0))
    for i in range(5):
        both = jnp.where(row == i + 2, stat[i : i + 1, :], both)
    both = both.astype(BF16)
    for q in range(dps):
        for c in range(dps):
            here = slice(5 * width + c * PAD, 5 * width + (c + 1) * PAD)
            out[q, here, :] = both[:, c * cut : (c + 1) * cut]


def add_kernel(idx, *refs):
    count = len(refs) // 3
    step = math.gcd(refs[0].shape[0], 32)

    def add_rows(i, carry):
        here = at(i, step)
        for k in range(count):
            total = refs[k][here, :].astype(F32) + refs[count + k][here, :].astype(F32)
            refs[2 * count + k][here, :] = total.astype(BF16)
        return carry

    lax.fori_loop(0, refs[0].shape[0] // step, add_rows, 0)


def sum_kernel(idx, pieces, out):
    step = math.gcd(out.shape[0], 64)

    def add_rows(i, carry):
        here = at(i, step)
        out[here, :] = jnp.sum(pieces[:, here, :].astype(F32), 0).astype(BF16)
        return carry

    lax.fori_loop(0, out.shape[0] // step, add_rows, 0)


def token_kernel(idx, tokens, gain, grad, *rest):
    parts, (out, tok, sem) = rest[:-3], rest[-3:]
    own_rows(idx, tokens, tok, sem).wait()
    grad_normed = parts[0][...].astype(F32)
    for part in parts[1:]:
        grad_normed += part[...].astype(F32)
    standard, inverse = normalize(tok[...].astype(F32))
    out[...] = grad[...] + norm_backward(standard, inverse, grad_normed, gain[0:1, :].astype(F32))


def place_kernel(plan, idx, *refs):
    parts, outs = refs[: -len(plan)], refs[-len(plan) :]
    if len(parts) == 1:
        source = parts[0]
        count, _, cut = source.shape
        take = lambda q, rows: source[q, rows, :]
        where_of = lambda q: slice(q * cut, (q + 1) * cut)
    else:
        count, cut = len(parts), parts[0].shape[1]
        take = lambda q, rows: parts[q][rows, :]
        where_of = lambda q: at(idx[1] ^ q, cut)
    row = 0
    for out, (height, lead, flip) in zip(outs, plan):
        for q in range(count):
            where = where_of(q)
            piece = take(q, slice(row, row + height)).astype(F32)
            if not flip:
                out[:, where] = piece
            elif lead is None:
                out[where, :] = piece.T
            else:
                step = height // lead
                for c in range(lead):
                    out[c, where, :] = piece[c * step : (c + 1) * step, :].T
        row += height


def flip_bits(axis, bits, size):
    return functools.partial(
        lax.ppermute, axis_name=axis, perm=[(i, i ^ bits) for i in range(size)]
    )


def total(*parts):
    out = parts[0].astype(F32)
    for part in parts[1:]:
        out = out + part.astype(F32)
    return out


def body(
    tokens,
    states,
    cotangent,
    self_weight,
    self_output,
    cross_query,
    cross_pair,
    cross_output,
    hidden_weight,
    hidden_bias,
    output_weight,
    output_bias,
    norm_gain,
    norm_shift,
    state_row,
    state_segment,
    caption,
):
    rows, dim = tokens.shape
    width = cross_query.shape[1]
    heads = width // HDIM
    hid = hidden_bias.shape[0]
    cores = lax.axis_size("mp")
    chips = cores // 2
    dps = lax.axis_size("dp")
    own = rows // cores
    cut = dim // dps
    me = lax.axis_index("mp")
    dpi = lax.axis_index("dp")
    idx = jnp.stack([me, dpi, state_row[0], caption[0]]).astype(jnp.int32)
    to_z = [flip_bits("mp", 2 * k, cores) for k in range(chips)]
    to_core = flip_bits("mp", 1, cores)
    to_dp = [flip_bits("dp", q, dps) for q in range(dps)]
    far = range(1, chips)
    peers = range(1, dps)

    def share_dp(piece):
        return lax.all_to_all(jnp.broadcast_to(piece[None], (dps,) + piece.shape), "dp", 0, 0)

    def add_all(left, right, name):
        return list(
            call(
            add_kernel,
            [((own, dim), BF16)] * chips,
            idx,
            *left,
            *right,
            stage=True,
            name=name,
        ))

    def swap_dp(pieces):
        return lax.all_to_all(pieces, "dp", 0, 0)

    def sum_dp(pieces):
        return jnp.sum(pieces.astype(F32), 0).astype(BF16)

    labels = lax.dynamic_index_in_dim(state_segment, state_row[0], 0, False)
    begin = jnp.minimum(jnp.sum((labels < caption[0]).astype(jnp.int32)), labels.shape[0] - SEEN)
    labels = lax.dynamic_slice_in_dim(labels, begin, SEEN, 0)
    seen = jnp.tile((labels == caption[0]).astype(jnp.int32)[None, :], (1, heads))
    near = lax.dynamic_slice(states, (state_row[0], begin, 0), (1, SEEN, dim))[0]

    mine = jnp.concatenate([self_output, cross_query.T, cross_output], 0)
    piece = lax.dynamic_slice_in_dim(mine, dpi * cut, cut, 1)
    got = [to_z[k](piece) for k in far]
    output_weight2 = to_core(output_weight)

    outs = call(
        functools.partial(self_kernel, chips),
        [
            ((rows, dim), BF16),
            ((3, rows, width), BF16),
            ((heads, rows, rows), BF16),
        ]
        + [((2 * own + 2 * SEEN, width), BF16)] * chips,
        idx,
        tokens,
        self_weight,
        norm_gain,
        norm_shift,
        states,
        cross_pair,
        state_segment,
        scratch=[
            pltpu.VMEM((width, rows), BF16),
            pltpu.VMEM((rows, width), BF16),
            pltpu.VMEM((states.shape[1], width), F32),
        ],
        after=(piece,),
        stage=True,
        name="self_fwd",
    )
    normed_one, triple, probs = outs[:3]
    att = outs[3:]
    *got, output_weight2, _ = lax.optimization_barrier((*got, output_weight2, att[0]))
    (cat,) = call(pack_kernel, [((3 * width * (chips - 1), cut), BF16)], idx, *got, tight=True, name="pack")
    att = [att[0]] + [to_z[k](att[k]) for k in far]
    att2 = [to_core(x) for x in att]

    grad_active = call(
        functools.partial(active_kernel, chips),
        [((2 * own, hid), F32)] * chips,
        idx,
        cotangent,
        output_weight,
        scratch=[pltpu.VMEM((chips, 2 * own, hid), F32)],
        after=att[:1],
        stage=True,
        name="grad_active",
    )

    cats = [cat] + [to_dp[q](cat) for q in peers]
    cats, grad_active, seen = lax.optimization_barrier((cats, grad_active, seen))
    weights = [mine, *cats, to_core(mine), *[to_core(x) for x in cats]]

    sq = cores * width
    first, fwd, q, cp, second, n3 = call(
        functools.partial(cross_kernel, chips, dps),
        [
            ((own, dim), F32),
            ((3, own, dim), BF16),
            ((own, sq), BF16),
            ((cores, own, heads * SEEN), BF16),
            ((own, dim), F32),
            ((own, dim), BF16),
        ],
        idx,
        tokens,
        norm_gain,
        norm_shift,
        seen,
        *weights,
        *att,
        *att2,
        scratch=[
            pltpu.VMEM((3, sq, dim), BF16),
            pltpu.SemaphoreType.DMA((3, 2 * dps + 2)),
            pltpu.VMEM((own, dim), BF16),
            pltpu.SemaphoreType.DMA,
        ],
        raw=(0, *range(4, 4 + len(weights))),
        stage=True,
        name="cross_fwd",
    )

    relay = chips == 4
    order = (0, 1, 3, 2) if relay else range(chips)
    n3s = [n3] + [None if relay and k == 2 else to_z[k](n3) for k in far]
    fwd2 = to_core(fwd)
    bias_row = hidden_bias[None, :]
    acts, ghis, chunks, sent, others = ([None] * chips for _ in range(5))
    done = ()
    for k in order:
        arrived = n3s[k]
        chunk, act, ghi, bs, bo = call(
            hidden_kernel,
            [
                ((2 * own, dim), BF16),
                ((2 * own, hid), BF16),
                ((2 * own, hid), BF16),
                ((own, dim), BF16),
                ((own, dim + hid), BF16),
            ],
            idx,
            arrived,
            to_core(arrived),
            hidden_weight,
            bias_row,
            grad_active[k],
            scratch=[
                pltpu.VMEM((2 * own, dim), F32),
                pltpu.VMEM((2 * own, dim), BF16),
                pltpu.VMEM((2 * own, hid), BF16),
                pltpu.VMEM((2 * own, hid), BF16),
                pltpu.SemaphoreType.DMA((3,)),
            ],
            sent=(0, 1, 2),
            after=done,
            tight=True,
            name="hidden",
        )
        done = (act,)
        acts[k], ghis[k], chunks[k] = act, ghi, chunk
        others[k] = to_core(bo)
        sent[k] = total(bs, others[k][:, :dim]).astype(BF16)
        if k == 0:
            *n3s, _ = lax.optimization_barrier((*n3s, act))
            if relay:
                n3s[2] = to_z[1](n3s[3])
    backs = sent[:1] + [to_z[k](sent[k]) for k in range(1, 2 if relay else chips)]
    if relay:
        relayed = to_z[1](sent[3])
    (mlp_grad,) = call(
        functools.partial(mlp_grad_kernel, chips),
        [((dps, 2 * hid + PAD, cut), BF16)],
        idx,
        cotangent,
        *acts,
        *ghis,
        *chunks,
        scratch=[
            pltpu.VMEM((rows, hid), BF16),
            pltpu.VMEM((rows, hid), BF16),
            pltpu.VMEM((rows, dim), BF16),
        ],
        after=[x for k, x in enumerate(sent) if k != 2],
        cost=10**12,
        stage=True,
        name="mlp_grad",
    )
    if relay:
        mlp_grad, relayed = lax.optimization_barrier((mlp_grad, relayed))
        backs.append(to_z[2](total(sent[2], relayed).astype(BF16)))
    mlp_grad, backs[1] = lax.optimization_barrier((mlp_grad, backs[1]))
    mlp_swap = swap_dp(mlp_grad)
    mlp_part = call(
        functools.partial(mlp_out_kernel, chips),
        [((own, dim), BF16)] * chips,
        idx,
        output_weight,
        output_weight2,
        *acts,
        *others,
        scratch=[
            pltpu.VMEM((2, chips, own, hid), BF16),
            pltpu.VMEM((chips, own, dim), BF16),
            pltpu.SemaphoreType.DMA((2, chips)),
        ],
        raw=tuple(range(2, 2 + 2 * chips)),
        after=(mlp_grad,),
        stage=True,
        name="mlp_out",
    )
    *backs, mlp_part = lax.optimization_barrier((*backs, list(mlp_part)))
    mlp_parts = mlp_part[:1] + [to_z[k](mlp_part[k]) for k in far[:2]]

    outs = call(
        functools.partial(cross_back_kernel, chips, dps, len(backs)),
        [
            ((3, own, dim), BF16),
            ((own, dim), F32),
            ((8, dim), F32),
            ((chips, 2, SEEN, width), BF16),
            ((chips, 2, SEEN, width), BF16),
        ]
        + [((2, own, width), BF16)] * chips,
        idx,
        cotangent,
        norm_gain,
        second,
        first,
        cp,
        q,
        *weights,
        *backs,
        *att,
        *att2,
        scratch=[
            pltpu.VMEM((own, sq), BF16),
            pltpu.VMEM((3, sq, dim), BF16),
            pltpu.SemaphoreType.DMA((3, 2 * dps + 2)),
            pltpu.VMEM((own, dim), BF16),
            pltpu.SemaphoreType.DMA,
        ],
        raw=(0, *range(6, 6 + len(weights))),
        cost=10**12,
        stage=True,
        name="cross_bwd",
    )
    outs, mlp_parts, mlp_swap = lax.optimization_barrier((outs, mlp_parts, mlp_swap))
    mlp_piece = call(
        sum_kernel, [((2 * hid, cut), BF16)], idx, mlp_swap, stage=True, name="sum_mlp"
    )[0]
    mlp_all = [mlp_piece] + [to_dp[q](mlp_piece) for q in (1, 2)]
    bwd, gf, stat_a, dkv, dkv_other = outs[:5]
    gatt = outs[5:]
    gatt = [gatt[0]] + [to_z[k](gatt[k]) for k in far]

    (row_grad,) = call(
        functools.partial(row_grad_kernel, chips),
        [((dps, chips * 3 * width, cut), BF16)],
        idx,
        fwd,
        fwd2,
        bwd,
        to_core(bwd),
        scratch=[pltpu.VMEM((2 * own, chips * width), BF16), pltpu.VMEM((2 * own, dim), BF16)],
        stage=True,
        name="row_grad",
    )
    gatt, row_grad, mlp_all, mlp_part = lax.optimization_barrier(
        (gatt, row_grad, mlp_all, mlp_part)
    )
    mlp_all += [to_dp[q](mlp_all[0]) for q in range(3, dps)]
    gatt2 = [to_core(x) for x in gatt]
    row_swap = swap_dp(row_grad)
    mlp_parts += [to_z[k](mlp_part[k]) for k in far[2:]]

    outs = call(
        functools.partial(self_back_kernel, chips),
        [((rows, 3 * width), BF16)] + [((own, dim), BF16)] * (2 * chips),
        idx,
        triple,
        probs,
        self_weight,
        *gatt,
        *gatt2,
        scratch=[
            pltpu.VMEM((rows, width), BF16),
            pltpu.VMEM((width, rows), BF16),
            pltpu.VMEM((dim, 3 * width), BF16),
            pltpu.VMEM((width, rows), F32),
            pltpu.VMEM((rows, width), F32),
            pltpu.VMEM((rows, width), F32),
            pltpu.VMEM((rows, dim), BF16),
        ],
        cost=10**12,
        stage=True,
        name="self_bwd",
    )
    outs, mlp_parts = lax.optimization_barrier((outs, mlp_parts))
    gt, bs, bo = outs[0], outs[1 : 1 + chips], outs[1 + chips :]
    bos = [to_core(x) for x in bo]

    dkv = total(dkv, to_core(dkv_other)).astype(BF16)
    gp = total(dkv[0], *[to_z[k](dkv[k]) for k in far]).astype(BF16)

    *bos, gp = lax.optimization_barrier((*bos, gp))
    sent = add_all(bs, bos, "self_add")
    parts = sent[:1] + [to_z[k](sent[k]) for k in far[:2]]

    (self_part,) = call(
        functools.partial(self_grad_kernel, chips, dps),
        [((dps, 5 * width + dps * PAD, cut), BF16)],
        idx,
        tokens,
        normed_one,
        gt,
        near,
        gp,
        stat_a,
        *bs,
        *bo,
        scratch=[
            pltpu.VMEM((cores, own, dim), BF16),
            pltpu.SemaphoreType.DMA((cores,)),
        ],
        raw=tuple(range(6, 6 + cores)),
        after=sent[:1],
        stage=True,
        name="self_grad",
    )
    self_part, row_swap, mlp_all, parts[1:3] = lax.optimization_barrier(
        (self_part, row_swap, mlp_all, parts[1:3])
    )
    self_swap = swap_dp(self_part)
    row_piece = sum_dp(row_swap).reshape(chips, 3 * width, cut)
    row_parts = [row_piece[0]] + [to_z[k](row_piece[k]) for k in far]
    block_output = (second + total(*mlp_parts) + output_bias.astype(F32)).astype(BF16)
    def place(pieces, plan, shapes, name, **kept):
        return call(
            functools.partial(place_kernel, plan),
            [(s, F32) for s in shapes],
            idx,
            *pieces,
            stage=True,
            name=name,
            **kept,
        )

    grad_output_weight, grad_hidden_weight = place(
        mlp_all, ((hid, None, False), (hid, None, True)), ((hid, dim), (dim, hid)), "place_mlp"
    )
    row_parts, self_swap, sent, block_output, grad_output_weight = lax.optimization_barrier(
        (row_parts, self_swap, sent, block_output, grad_output_weight)
    )
    parts += [to_z[k](sent[k]) for k in far[2:]]
    row_piece = total(*row_parts).astype(BF16)
    self_sum = sum_dp(self_swap)
    piece = jnp.concatenate([row_piece, self_sum[: 5 * width]], 0)
    swapped = share_dp(piece)
    (grad_tokens,) = call(
        token_kernel,
        [((own, dim), F32)],
        idx,
        tokens,
        norm_gain,
        gf,
        *parts,
        scratch=[pltpu.VMEM((own, dim), BF16), pltpu.SemaphoreType.DMA],
        raw=(0,),
        stage=True,
        name="tokens",
    )
    state_part = jnp.einsum("cse,cde->sd", gp, cross_pair, preferred_element_type=F32)
    held = self_sum[5 * width :].reshape(dps, PAD, cut)
    held = jnp.concatenate([held[c] for c in range(dps)], 1)
    state_part = jnp.concatenate([state_part.astype(BF16), held], 0)
    core = lax.rem(me, 2)
    half_of = lambda c: lax.dynamic_slice_in_dim(state_part, c * (dim // 2), dim // 2, 1)
    state_half = total(half_of(core), to_core(half_of(1 - core))).astype(BF16)
    state_got = [to_z[k](state_half) for k in far]
    state_got, block_output, grad_output_weight, grad_tokens = lax.optimization_barrier(
        (state_got, block_output, grad_output_weight, grad_tokens)
    )
    state_half = total(state_half, *state_got)
    state_sum = jnp.zeros((state_part.shape[0], dim), F32)
    for c, part in ((core, state_half), (1 - core, to_core(state_half))):
        state_sum = lax.dynamic_update_slice(state_sum, part, (0, c * (dim // 2)))
    grad_states = lax.dynamic_update_slice(
        jnp.zeros(states.shape, F32), state_sum[None, :SEEN], (state_row[0], begin, 0)
    )
    stats = state_sum[SEEN:]
    swapped, state_sum = lax.optimization_barrier((swapped, state_sum))
    (
        grad_self_output,
        grad_cross_query,
        grad_cross_output,
        grad_self_weight,
        grad_cross_pair,
    ) = place(
        [swapped],
        (
            (width, None, False),
            (width, None, True),
            (width, None, False),
            (3 * width, 3, True),
            (2 * width, 2, True),
        ),
        (
            (width, dim),
            (dim, width),
            (width, dim),
            (3, dim, width),
            (2, dim, width),
        ),
        "place",
        near=(0,),
        tight=True,
    )
    grad_norm_gain = jnp.stack([stats[0], stats[4], stats[2]])
    grad_norm_shift = jnp.stack([stats[1], stats[5], stats[3]])
    grad_output_bias = stats[6]
    grad_hidden_bias = jnp.sum(mlp_swap[:, 2 * hid : 2 * hid + hid // cut].astype(F32), 0).reshape(hid)
    return (
        block_output,
        grad_tokens,
        grad_states,
        grad_self_weight,
        grad_self_output,
        grad_cross_query,
        grad_cross_pair,
        grad_cross_output,
        grad_hidden_weight,
        grad_hidden_bias,
        grad_output_weight,
        grad_output_bias,
        grad_norm_gain,
        grad_norm_shift,
    )


def solution(mesh):
    placed = (
        P("dp", None),
        P("dp", None, None),
        P("dp", None),
        P(None, None, "mp"),
        P("mp", None),
        P(None, "mp"),
        P(None, None, "mp"),
        P("mp", None),
        P(None, "mp"),
        P("mp"),
        P("mp", None),
        P(),
        P(),
        P(),
        P("dp"),
        P("dp", None),
        P("dp"),
    )
    return jax.shard_map(
        body,
        mesh=mesh,
        in_specs=placed,
        out_specs=(
            P(("dp", "mp"), None),
            P(("dp", "mp"), None),
            P("dp", None, None),
            P(None, None, "mp"),
            P("mp", None),
            P(None, "mp"),
            P(None, None, "mp"),
            P("mp", None),
            P(None, "mp"),
            P("mp"),
            P("mp", None),
            P(),
            P(),
            P(),
        ),
        check_vma=False,
    )
```
